256 devices in a mesh: exp: 32 (over y, z_hi, core), hid: 8 (over z_lo, x).
Axes of the slice: x: 4, y: 4, z: 8 (z_hi: 4, z_lo: 2; z = z_hi * 2 + z_lo), core: 2. Of those that a mesh axis runs over, the one named last changes fastest.
Arguments:
- tokens: bfloat16 [1024, 2048], P(('exp', 'hid')), may hold values from -6 to 6
- grad_out: bfloat16 [1024, 2048], P(('exp', 'hid')), may hold values from -3 to 3
- router_logits: float32 [1024, 128], P(('exp', 'hid')), may hold values from -12 to 330
- selected: int32 [1024, 8], P(('exp', 'hid')), may hold values from 0 to 127, as said below
- router_w: bfloat16 [2048, 128], replicated, may hold values from -0.59765625 to 0.59765625
- w_gate: bfloat16 [256, 2048, 384], P(('exp', 'hid')), may hold values from -0.125 to 0.125
- w_up: bfloat16 [256, 2048, 384], P(('exp', 'hid')), may hold values from -0.125 to 0.125
- w_down: bfloat16 [256, 384, 2048], P(('exp', 'hid')), may hold values from -0.21875 to 0.21875
Outputs:
- x_grad: bfloat16 [1024, 2048], P(('exp', 'hid'))
- router_grad: float32 [2048, 128], P(('exp', 'hid'))
The draws below stay inside these ranges and needn't reach their ends.
Inputs may be any that keep to these rules, and one draw needn't show every extreme that they name: `selected`: each row names 8 different experts; within each aligned block of 32 rows (the tokens of one index of exp) no expert is named by more than 4 rows, and in every block some expert is named by exactly 4 rows.
All inputs are finite; a program needn't handle non-finite values.
Results may differ from the reference program's by a relative error of at most 0.0075.
Values may be sent and summed in bfloat16 or wider, within the bound.
A program may use at most 64 MiB of HBM per device.

```python
import jax
import jax.numpy as jnp
from jax import lax

D = 2048
F = 768
TOPK = 8
TOK_DEV = 4
FH = 384
UNITS = 256
EXPERTS = 128
TOKENS = 1024
CAP_G = 4
N_HID = 8


def choose_block(key):
    block_rows = N_HID * TOK_DEV
    windows = EXPERTS // TOPK
    slot_count = windows * CAP_G
    keys = jax.random.split(key, 4)
    order = jax.random.permutation(keys[0], EXPERTS).astype(jnp.int32)
    first_window = jax.random.randint(keys[1], (), 0, windows).astype(jnp.int32)
    slot_window = (jnp.arange(slot_count, dtype=jnp.int32) // CAP_G).astype(jnp.int32)
    priority = jax.random.randint(keys[2], (slot_count,), 0, 1 << 20) * slot_count + jnp.arange(slot_count, dtype=jnp.int32)
    priority = jnp.where(slot_window == first_window, priority + (1 << 20) * slot_count, priority)
    taken = lax.top_k(priority, block_rows)[1].astype(jnp.int32)
    row_window = jax.random.permutation(keys[3], slot_window[taken]).astype(jnp.int32)
    positions = row_window[:, None] * TOPK + jnp.arange(TOPK, dtype=jnp.int32)[None, :]
    return order[positions].astype(jnp.int32)


def choose_experts(key):
    block_rows = N_HID * TOK_DEV
    block_count = TOKENS // block_rows
    block_keys = jax.random.split(jax.random.fold_in(key, 17), block_count)
    chosen = jax.vmap(choose_block)(block_keys)
    return chosen.reshape(TOKENS, TOPK).astype(jnp.int32)


def draw_selected(key, part):
    return choose_experts(key)


def draw_router_logits(key, part):
    chosen = choose_experts(key)
    expert_ids = jnp.arange(EXPERTS, dtype=jnp.int32)
    hit_table = jnp.sum((chosen[:, :, None] == expert_ids[None, None, :]).astype(jnp.float32), axis=1)
    subkeys = jax.random.split(jax.random.fold_in(key, 29), 3)
    col_offset = jax.random.uniform(subkeys[0], (1, EXPERTS), minval=-0.6, maxval=0.6)
    chosen_level = 2.0 + jax.random.uniform(subkeys[1], (TOKENS, EXPERTS), minval=-1.15, maxval=1.15)
    noise_draw = jnp.clip(0.6 * jax.random.normal(subkeys[2], (TOKENS, EXPERTS)), -0.9, 0.9)
    other_level = col_offset + noise_draw
    logits = jnp.where(hit_table > 0.5, chosen_level, other_level)
    return logits.astype(jnp.float32)


def block_scale(rng, dims, shards, low, largest):
    def one(dim, blocks):
        heights = jax.random.uniform(jax.random.fold_in(jax.random.fold_in(rng, 6), dim), (blocks,), jnp.float32, low / len(shards), largest / len(shards))
        return jnp.repeat(jnp.exp(heights), dims[dim] // blocks).reshape((-1,) + (1,) * (len(dims) - dim - 1))

    loudness = one(*shards[0])
    for cut in shards[1:]:
        loudness = loudness * one(*cut)
    return loudness


def centred(stream_key, shape, width, reach, shards=(), kind=jnp.bfloat16):
    drawn = jax.random.normal(stream_key, shape, jnp.float32) * width
    if len(shards) > 0:
        drawn = block_scale(stream_key, shape, shards, -0.22, 0.18) * drawn
    return jnp.clip(drawn, min=-reach, max=reach).astype(kind)


def setup_inputs(seed: int = 0) -> dict:
    arg_keys = jax.random.split(jax.random.key(seed), 9)
    tokens = centred(arg_keys[0], (TOKENS, D), 1.0, 6.0, ((0, 256),))
    grad_out = centred(arg_keys[1], (TOKENS, D), 0.5, 3.0, ((0, 256),))
    router_logits = draw_router_logits(jax.random.fold_in(arg_keys[8], 71), 0)
    selected = draw_selected(jax.random.fold_in(arg_keys[8], 71), 0)
    router_w = centred(arg_keys[4], (D, EXPERTS), 0.1, 0.59765625)
    w_gate = centred(arg_keys[5], (UNITS, D, FH), D ** -0.5, 0.125, ((0, 256),))
    w_up = centred(arg_keys[6], (UNITS, D, FH), D ** -0.5, 0.125, ((0, 256),))
    w_down = centred(arg_keys[7], (UNITS, FH, D), F ** -0.5, 0.21875, ((0, 256),))
    return {"tokens": tokens, "grad_out": grad_out, "router_logits": router_logits, "selected": selected, "router_w": router_w, "w_gate": w_gate, "w_up": w_up, "w_down": w_down}


def softmax_rows(values):
    top_val = jnp.max(values, axis=-1, keepdims=True)
    raised = jnp.exp(values - top_val)
    return raised / jnp.sum(raised, axis=-1, keepdims=True)


def combine_table(logits, chosen, expert_count):
    picked = jnp.take_along_axis(logits, chosen, axis=1)
    weights = softmax_rows(picked)
    expert_ids = jnp.arange(expert_count, dtype=jnp.int32)
    matched = (chosen[:, :, None] == expert_ids[None, None, :]).astype(jnp.float32)
    return jnp.sum(weights[:, :, None] * matched, axis=1).astype(jnp.bfloat16)


def reference(tokens, grad_out, router_logits, selected, router_w, w_gate, w_up, w_down):
    probs_all = softmax_rows(router_logits)
    combine = combine_table(router_logits, selected, EXPERTS)

    def one_unit(totals, packed):
        gate_w, up_w, down_w, unit_id = packed
        column = lax.dynamic_slice_in_dim(combine, unit_id // 2, 1, 1).astype(jnp.float32)
        gate_pre = jnp.dot(tokens, gate_w, preferred_element_type=jnp.float32)
        up_pre = jnp.dot(tokens, up_w, preferred_element_type=jnp.float32)
        back_grad = jnp.dot(grad_out, down_w.T, preferred_element_type=jnp.float32)
        sig_gate = jax.nn.sigmoid(gate_pre)
        act_gate = gate_pre * sig_gate
        score_part = jnp.sum(act_gate * up_pre * back_grad, axis=1)
        weighted = column * back_grad
        grad_gate = (weighted * up_pre * sig_gate * (1.0 + gate_pre * (1.0 - sig_gate))).astype(jnp.bfloat16)
        grad_up = (weighted * act_gate).astype(jnp.bfloat16)
        totals = totals + jnp.dot(grad_gate, gate_w.T, preferred_element_type=jnp.float32)
        totals = totals + jnp.dot(grad_up, up_w.T, preferred_element_type=jnp.float32)
        return totals, score_part

    unit_ids = jnp.arange(UNITS, dtype=jnp.int32)
    start_totals = jnp.zeros((TOKENS, D), jnp.float32)
    expert_grad, unit_scores = lax.scan(one_unit, start_totals, (w_gate, w_up, w_down, unit_ids))
    expert_scores = jnp.sum(unit_scores.reshape(EXPERTS, 2, TOKENS), axis=1).T
    mean_score = jnp.sum(probs_all * expert_scores, axis=1, keepdims=True)
    logit_grad = (probs_all * (expert_scores - mean_score)).astype(jnp.bfloat16)
    router_grad = jnp.dot(tokens.T, logit_grad, preferred_element_type=jnp.float32)
    router_part = jnp.dot(logit_grad, router_w.T, preferred_element_type=jnp.float32)
    x_grad = (expert_grad + router_part).astype(jnp.bfloat16)
    return x_grad, router_grad
```

```python
import jax
import jax.numpy as jnp
from jax import lax
from jax.sharding import PartitionSpec as P


def softmax_rows(values):
    top_val = jnp.max(values, axis=-1, keepdims=True)
    raised = jnp.exp(values - top_val)
    return raised / jnp.sum(raised, axis=-1, keepdims=True)


def combine_table(logits, chosen, expert_count):
    picked = jnp.take_along_axis(logits, chosen, axis=1)
    weights = softmax_rows(picked)
    expert_ids = jnp.arange(expert_count, dtype=jnp.int32)
    matched = (chosen[:, :, None] == expert_ids[None, None, :]).astype(jnp.float32)
    return jnp.sum(weights[:, :, None] * matched, axis=1).astype(jnp.bfloat16)


def unit_terms(x_rows, g_rows, c_rows, w_gate, w_up, w_down, unit_pick):
    gate_pre = jnp.einsum("td,udf->utf", x_rows, w_gate, preferred_element_type=jnp.float32)
    up_pre = jnp.einsum("td,udf->utf", x_rows, w_up, preferred_element_type=jnp.float32)
    back_grad = jnp.einsum("td,ufd->utf", g_rows, w_down, preferred_element_type=jnp.float32)
    sig_gate = jax.nn.sigmoid(gate_pre)
    act_gate = gate_pre * sig_gate
    score_part = jnp.sum(act_gate * up_pre * back_grad, axis=2).T
    column_rows = jnp.dot(c_rows, unit_pick, preferred_element_type=jnp.float32)
    weighted = column_rows.T[:, :, None] * back_grad
    grad_gate = (weighted * up_pre * sig_gate * (1.0 + gate_pre * (1.0 - sig_gate))).astype(
        jnp.bfloat16
    )
    grad_up = (weighted * act_gate).astype(jnp.bfloat16)
    input_part = jnp.einsum("utf,udf->td", grad_gate, w_gate, preferred_element_type=jnp.float32)
    input_part = input_part + jnp.einsum(
        "utf,udf->td", grad_up, w_up, preferred_element_type=jnp.float32
    )
    return (score_part, input_part, column_rows)


def on_device(tokens, grad_out, router_logits, selected, router_w, w_gate, w_up, w_down):
    tok_local, model_width = tokens.shape
    unit_count = w_gate.shape[0]
    expert_count = router_logits.shape[1]
    spread_exp = lax.axis_size("exp")
    spread_hid = lax.axis_size("hid")
    own_block = lax.axis_index(("exp", "hid"))
    unit_expert = (own_block * unit_count + jnp.arange(unit_count, dtype=jnp.int32)) // 2
    expert_ids = jnp.arange(expert_count, dtype=jnp.int32)
    unit_pick = (expert_ids[:, None] == unit_expert[None, :]).astype(jnp.bfloat16)
    combine = combine_table(router_logits, selected, expert_count)
    packed = jnp.concatenate([tokens, grad_out, combine], axis=1)
    gathered = lax.all_gather(lax.all_gather(packed, "hid", axis=0, tiled=True), "exp", axis=0, tiled=True)
    score_part, input_part, column_rows = unit_terms(
        gathered[:, :model_width],
        gathered[:, model_width : 2 * model_width],
        gathered[:, 2 * model_width :],
        w_gate,
        w_up,
        w_down,
        unit_pick,
    )
    input_sum = lax.psum_scatter(
        lax.psum_scatter(input_part, "exp", scatter_dimension=0, tiled=True),
        "hid",
        scatter_dimension=0,
        tiled=True,
    )
    shaped = score_part.reshape(spread_exp, spread_hid, tok_local, 1, unit_count)
    arrived = lax.all_to_all(
        lax.all_to_all(shaped, "exp", split_axis=0, concat_axis=3, tiled=True),
        "hid",
        split_axis=1,
        concat_axis=4,
        tiled=True,
    )
    expert_scores = jnp.sum(arrived.reshape(tok_local, expert_count, 2), axis=2)
    probs_all = softmax_rows(router_logits)
    mean_score = jnp.sum(probs_all * expert_scores, axis=1, keepdims=True)
    logit_grad = (probs_all * (expert_scores - mean_score)).astype(jnp.bfloat16)
    router_grad = lax.psum_scatter(
        jnp.einsum("tc,te->ce", tokens, logit_grad, preferred_element_type=jnp.float32),
        ("exp", "hid"),
        scatter_dimension=0,
        tiled=True,
    )
    router_part = jnp.einsum("te,de->td", logit_grad, router_w, preferred_element_type=jnp.float32)
    x_grad = (input_sum + router_part).astype(jnp.bfloat16)
    return (x_grad, router_grad)


def solution(mesh):
    placed = (
        P(("exp", "hid"), None),
        P(("exp", "hid"), None),
        P(("exp", "hid"), None),
        P(("exp", "hid"), None),
        P(),
        P(("exp", "hid"), None, None),
        P(("exp", "hid"), None, None),
        P(("exp", "hid"), None, None),
    )
    return jax.shard_map(
        on_device,
        mesh=mesh,
        in_specs=placed,
        out_specs=(P(("exp", "hid"), None), P(("exp", "hid"), None)),
        check_vma=False,
    )
```

```python
import jax
import jax.numpy as jnp
from jax import lax
from jax.sharding import PartitionSpec as P


def softmax_rows(values):
    top_val = jnp.max(values, axis=-1, keepdims=True)
    raised = jnp.exp(values - top_val)
    return raised / jnp.sum(raised, axis=-1, keepdims=True)


def combine_table(logits, chosen, expert_count):
    picked = jnp.take_along_axis(logits, chosen, axis=1)
    weights = softmax_rows(picked)
    expert_ids = jnp.arange(expert_count, dtype=jnp.int32)
    matched = (chosen[:, :, None] == expert_ids[None, None, :]).astype(jnp.float32)
    return jnp.sum(weights[:, :, None] * matched, axis=1).astype(jnp.bfloat16)


def unit_terms(x_rows, g_rows, c_rows, w_gate, w_up, w_down, unit_pick):
    gate_pre = jnp.einsum("td,udf->utf", x_rows, w_gate, preferred_element_type=jnp.float32)
    up_pre = jnp.einsum("td,udf->utf", x_rows, w_up, preferred_element_type=jnp.float32)
    back_grad = jnp.einsum("td,ufd->utf", g_rows, w_down, preferred_element_type=jnp.float32)
    sig_gate = jax.nn.sigmoid(gate_pre)
    act_gate = gate_pre * sig_gate
    score_part = jnp.sum(act_gate * up_pre * back_grad, axis=2).T
    column_rows = jnp.dot(c_rows, unit_pick, preferred_element_type=jnp.float32)
    weighted = column_rows.T[:, :, None] * back_grad
    grad_gate = (weighted * up_pre * sig_gate * (1.0 + gate_pre * (1.0 - sig_gate))).astype(
        jnp.bfloat16
    )
    grad_up = (weighted * act_gate).astype(jnp.bfloat16)
    input_part = jnp.einsum("utf,udf->td", grad_gate, w_gate, preferred_element_type=jnp.float32)
    input_part = input_part + jnp.einsum(
        "utf,udf->td", grad_up, w_up, preferred_element_type=jnp.float32
    )
    return (score_part, input_part, column_rows)


def on_device(tokens, grad_out, router_logits, selected, router_w, w_gate, w_up, w_down):
    tok_local, model_width = tokens.shape
    unit_count = w_gate.shape[0]
    expert_count = router_logits.shape[1]
    spread_exp = lax.axis_size("exp")
    spread_hid = lax.axis_size("hid")
    own_block = lax.axis_index(("exp", "hid"))
    unit_expert = (own_block * unit_count + jnp.arange(unit_count, dtype=jnp.int32)) // 2
    expert_ids = jnp.arange(expert_count, dtype=jnp.int32)
    unit_pick = (expert_ids[:, None] == unit_expert[None, :]).astype(jnp.bfloat16)
    combine = combine_table(router_logits, selected, expert_count)
    packed = jnp.concatenate([tokens, grad_out, combine], axis=1)
    gathered = lax.all_gather(lax.all_gather(packed, "hid", axis=0, tiled=True), "exp", axis=0, tiled=True)
    score_part, input_part, column_rows = unit_terms(
        gathered[:, :model_width],
        gathered[:, model_width : 2 * model_width],
        gathered[:, 2 * model_width :],
        w_gate,
        w_up,
        w_down,
        unit_pick,
    )
    input_sum = lax.psum_scatter(
        lax.psum_scatter(input_part, "exp", scatter_dimension=0, tiled=True),
        "hid",
        scatter_dimension=0,
        tiled=True,
    )
    shaped = score_part.reshape(spread_exp, spread_hid, tok_local, 1, unit_count)
    arrived = lax.all_to_all(
        lax.all_to_all(shaped, "exp", split_axis=0, concat_axis=3, tiled=True),
        "hid",
        split_axis=1,
        concat_axis=4,
        tiled=True,
    )
    expert_scores = jnp.sum(arrived.reshape(tok_local, expert_count, 2), axis=2)
    probs_all = softmax_rows(router_logits)
    mean_score = jnp.sum(probs_all * expert_scores, axis=1, keepdims=True)
    logit_grad = (probs_all * (expert_scores - mean_score)).astype(jnp.bfloat16)
    logit_all = lax.all_gather(
        lax.all_gather(logit_grad, "hid", axis=0, tiled=True), "exp", axis=0, tiled=True
    )
    grad_rows = model_width // (spread_exp * spread_hid)
    token_cols = lax.dynamic_slice_in_dim(gathered, own_block * grad_rows, grad_rows, 1)
    router_grad = jnp.einsum("tc,te->ce", token_cols, logit_all, preferred_element_type=jnp.float32)
    router_part = jnp.einsum("te,de->td", logit_grad, router_w, preferred_element_type=jnp.float32)
    x_grad = (input_sum + router_part).astype(jnp.bfloat16)
    return (x_grad, router_grad)


def solution(mesh):
    placed = (
        P(("exp", "hid"), None),
        P(("exp", "hid"), None),
        P(("exp", "hid"), None),
        P(("exp", "hid"), None),
        P(),
        P(("exp", "hid"), None, None),
        P(("exp", "hid"), None, None),
        P(("exp", "hid"), None, None),
    )
    return jax.shard_map(
        on_device,
        mesh=mesh,
        in_specs=placed,
        out_specs=(P(("exp", "hid"), None), P(("exp", "hid"), None)),
        check_vma=False,
    )
```

```python
import jax
import jax.numpy as jnp
from jax import lax
from jax.sharding import PartitionSpec as P


def softmax_rows(values):
    top_val = jnp.max(values, axis=-1, keepdims=True)
    raised = jnp.exp(values - top_val)
    return raised / jnp.sum(raised, axis=-1, keepdims=True)


def combine_table(logits, chosen, expert_count):
    picked = jnp.take_along_axis(logits, chosen, axis=1)
    weights = softmax_rows(picked)
    expert_ids = jnp.arange(expert_count, dtype=jnp.int32)
    matched = (chosen[:, :, None] == expert_ids[None, None, :]).astype(jnp.float32)
    return jnp.sum(weights[:, :, None] * matched, axis=1).astype(jnp.bfloat16)


CAP = 4


def slot_rows(column, group_rows):
    shaped = column.reshape(column.shape[:-1] + (-1, group_rows))
    place = jnp.arange(group_rows, dtype=jnp.int32)
    key = jnp.where(shaped != 0, 2 * group_rows - place, -place)
    return lax.top_k(key, CAP)[1]


def dense_terms(x_rows, g_rows, w_gate, w_up, w_down):
    gate_pre = jnp.einsum("td,udf->utf", x_rows, w_gate, preferred_element_type=jnp.float32)
    up_pre = jnp.einsum("td,udf->utf", x_rows, w_up, preferred_element_type=jnp.float32)
    back_grad = jnp.einsum("td,ufd->utf", g_rows, w_down, preferred_element_type=jnp.float32)
    sig_gate = jax.nn.sigmoid(gate_pre)
    act_gate = gate_pre * sig_gate
    score_part = jnp.sum(act_gate * up_pre * back_grad, axis=2).T
    return score_part, gate_pre, up_pre, back_grad


def sparse_terms(gate_pre, up_pre, back_grad, column, w_gate, w_up, group_rows):
    picked = slot_rows(column, group_rows)
    groups = picked.shape[1]
    starts = (jnp.arange(groups, dtype=jnp.int32) * group_rows)[None, :, None]
    rows = (picked + starts).reshape(picked.shape[0], -1)
    take = lambda a: jnp.take_along_axis(a, rows[:, :, None], axis=1)
    gate_s, up_s, back_s = take(gate_pre), take(up_pre), take(back_grad)
    col_s = jnp.take_along_axis(column, rows, axis=1)
    sig_gate = jax.nn.sigmoid(gate_s)
    act_gate = gate_s * sig_gate
    weighted = col_s[:, :, None] * back_s
    grad_gate = (weighted * up_s * sig_gate * (1.0 + gate_s * (1.0 - sig_gate))).astype(jnp.bfloat16)
    grad_up = (weighted * act_gate).astype(jnp.bfloat16)
    part = jnp.einsum("usf,udf->usd", grad_gate, w_gate, preferred_element_type=jnp.float32)
    part = part + jnp.einsum("usf,udf->usd", grad_up, w_up, preferred_element_type=jnp.float32)
    return part.reshape(part.shape[0], groups, CAP, part.shape[-1])


def on_device(tokens, grad_out, router_logits, selected, router_w, w_gate, w_up, w_down):
    tok_local, model_width = tokens.shape
    unit_count = w_gate.shape[0]
    expert_count = router_logits.shape[1]
    spread_exp = lax.axis_size("exp")
    spread_hid = lax.axis_size("hid")
    group_rows = spread_hid * tok_local
    own_exp = lax.axis_index("exp")
    own_hid = lax.axis_index("hid")
    own_block = lax.axis_index(("exp", "hid"))
    unit_expert = (own_block * unit_count + jnp.arange(unit_count, dtype=jnp.int32)) // 2
    expert_ids = jnp.arange(expert_count, dtype=jnp.int32)
    unit_pick = (expert_ids[:, None] == unit_expert[None, :]).astype(jnp.bfloat16)
    combine = combine_table(router_logits, selected, expert_count)
    packed = jnp.concatenate([tokens, grad_out, combine], axis=1)
    gathered = lax.all_gather(lax.all_gather(packed, "hid", axis=0, tiled=True), "exp", axis=0, tiled=True)
    combine_all = gathered[:, 2 * model_width :]
    score_part, gate_pre, up_pre, back_grad = dense_terms(
        gathered[:, :model_width], gathered[:, model_width : 2 * model_width], w_gate, w_up, w_down
    )
    column = jnp.dot(combine_all, unit_pick, preferred_element_type=jnp.float32).T
    part = sparse_terms(gate_pre, up_pre, back_grad, column, w_gate, w_up, group_rows)
    arrived_part = lax.all_to_all(jnp.swapaxes(part, 0, 1), "exp", split_axis=0, concat_axis=0, tiled=True)
    sender_block = (jnp.arange(spread_exp, dtype=jnp.int32) * spread_hid + own_hid)[:, None]
    sender_expert = (sender_block * unit_count + jnp.arange(unit_count, dtype=jnp.int32)[None, :]) // 2
    own_combine = lax.dynamic_slice_in_dim(combine_all, own_exp * group_rows, group_rows, 0)
    sender_pick = (expert_ids[:, None] == sender_expert.reshape(1, -1)).astype(jnp.bfloat16)
    sender_column = jnp.dot(own_combine, sender_pick, preferred_element_type=jnp.float32).T
    sender_rows = slot_rows(sender_column, group_rows).reshape(-1)
    place = (sender_rows[:, None] == jnp.arange(group_rows, dtype=jnp.int32)[None, :]).astype(jnp.float32)
    group_sum = jnp.einsum(
        "sj,sd->jd", place, arrived_part.reshape(-1, model_width), precision=lax.Precision.HIGHEST,
        preferred_element_type=jnp.float32,
    )
    spread_rows = lax.all_to_all(
        group_sum.reshape(spread_hid, tok_local, model_width), "hid", split_axis=0, concat_axis=0, tiled=True
    )
    input_sum = jnp.sum(spread_rows, axis=0)
    shaped = score_part.reshape(spread_exp, spread_hid, tok_local, 1, unit_count)
    arrived = lax.all_to_all(
        lax.all_to_all(shaped, "exp", split_axis=0, concat_axis=3, tiled=True),
        "hid",
        split_axis=1,
        concat_axis=4,
        tiled=True,
    )
    expert_scores = jnp.sum(arrived.reshape(tok_local, expert_count, 2), axis=2)
    probs_all = softmax_rows(router_logits)
    mean_score = jnp.sum(probs_all * expert_scores, axis=1, keepdims=True)
    logit_grad = (probs_all * (expert_scores - mean_score)).astype(jnp.bfloat16)
    logit_all = lax.all_gather(
        lax.all_gather(logit_grad, "hid", axis=0, tiled=True), "exp", axis=0, tiled=True
    )
    grad_rows = model_width // (spread_exp * spread_hid)
    token_cols = lax.dynamic_slice_in_dim(gathered, own_block * grad_rows, grad_rows, 1)
    router_grad = jnp.einsum("tc,te->ce", token_cols, logit_all, preferred_element_type=jnp.float32)
    router_part = jnp.einsum("te,de->td", logit_grad, router_w, preferred_element_type=jnp.float32)
    x_grad = (input_sum + router_part).astype(jnp.bfloat16)
    return (x_grad, router_grad)


def solution(mesh):
    placed = (
        P(("exp", "hid"), None),
        P(("exp", "hid"), None),
        P(("exp", "hid"), None),
        P(("exp", "hid"), None),
        P(),
        P(("exp", "hid"), None, None),
        P(("exp", "hid"), None, None),
        P(("exp", "hid"), None, None),
    )
    return jax.shard_map(
        on_device,
        mesh=mesh,
        in_specs=placed,
        out_specs=(P(("exp", "hid"), None), P(("exp", "hid"), None)),
        check_vma=False,
    )
```

```python
import jax
import jax.numpy as jnp
from jax import lax
from jax.sharding import PartitionSpec as P


def softmax_rows(values):
    top_val = jnp.max(values, axis=-1, keepdims=True)
    raised = jnp.exp(values - top_val)
    return raised / jnp.sum(raised, axis=-1, keepdims=True)


def combine_table(logits, chosen, expert_count):
    picked = jnp.take_along_axis(logits, chosen, axis=1)
    weights = softmax_rows(picked)
    expert_ids = jnp.arange(expert_count, dtype=jnp.int32)
    matched = (chosen[:, :, None] == expert_ids[None, None, :]).astype(jnp.float32)
    return jnp.sum(weights[:, :, None] * matched, axis=1).astype(jnp.bfloat16)


CAP = 4


def slot_rows(column, group_rows):
    shaped = column.reshape(column.shape[:-1] + (-1, group_rows))
    place = jnp.arange(group_rows, dtype=jnp.int32)
    key = jnp.where(shaped != 0, 2 * group_rows - place, -place)
    return lax.top_k(key, CAP)[1]


def dense_terms(x_rows, g_rows, w_gate, w_up, w_down):
    gate_pre = jnp.einsum("td,udf->utf", x_rows, w_gate, preferred_element_type=jnp.float32)
    up_pre = jnp.einsum("td,udf->utf", x_rows, w_up, preferred_element_type=jnp.float32)
    back_grad = jnp.einsum("td,ufd->utf", g_rows, w_down, preferred_element_type=jnp.float32)
    sig_gate = jax.nn.sigmoid(gate_pre)
    act_gate = gate_pre * sig_gate
    score_part = jnp.sum(act_gate * up_pre * back_grad, axis=2).T
    return score_part, gate_pre, up_pre, back_grad


def sparse_terms(gate_pre, up_pre, back_grad, column, w_gate, w_up, group_rows):
    picked = slot_rows(column, group_rows)
    groups = picked.shape[1]
    starts = (jnp.arange(groups, dtype=jnp.int32) * group_rows)[None, :, None]
    rows = (picked + starts).reshape(picked.shape[0], -1)
    take = lambda a: jnp.take_along_axis(a, rows[:, :, None], axis=1)
    gate_s, up_s, back_s = take(gate_pre), take(up_pre), take(back_grad)
    col_s = jnp.take_along_axis(column, rows, axis=1)
    sig_gate = jax.nn.sigmoid(gate_s)
    act_gate = gate_s * sig_gate
    weighted = col_s[:, :, None] * back_s
    grad_gate = (weighted * up_s * sig_gate * (1.0 + gate_s * (1.0 - sig_gate))).astype(jnp.bfloat16)
    grad_up = (weighted * act_gate).astype(jnp.bfloat16)
    part = jnp.einsum("usf,udf->usd", grad_gate, w_gate, preferred_element_type=jnp.float32)
    part = part + jnp.einsum("usf,udf->usd", grad_up, w_up, preferred_element_type=jnp.float32)
    return part.reshape(part.shape[0], groups, CAP, part.shape[-1])


def on_device(tokens, grad_out, router_logits, selected, router_w, w_gate, w_up, w_down):
    tok_local, model_width = tokens.shape
    unit_count = w_gate.shape[0]
    expert_count = router_logits.shape[1]
    spread_exp = lax.axis_size("exp")
    spread_hid = lax.axis_size("hid")
    group_rows = spread_hid * tok_local
    own_exp = lax.axis_index("exp")
    own_hid = lax.axis_index("hid")
    own_block = lax.axis_index(("exp", "hid"))
    unit_expert = (own_block * unit_count + jnp.arange(unit_count, dtype=jnp.int32)) // 2
    expert_ids = jnp.arange(expert_count, dtype=jnp.int32)
    unit_pick = (expert_ids[:, None] == unit_expert[None, :]).astype(jnp.bfloat16)
    combine = combine_table(router_logits, selected, expert_count)
    packed = jnp.concatenate([tokens, grad_out, combine], axis=1)
    gathered = lax.all_gather(lax.all_gather(packed, "hid", axis=0, tiled=True), "exp", axis=0, tiled=True)
    combine_all = gathered[:, 2 * model_width :]
    score_part, gate_pre, up_pre, back_grad = dense_terms(
        gathered[:, :model_width], gathered[:, model_width : 2 * model_width], w_gate, w_up, w_down
    )
    column = jnp.dot(combine_all, unit_pick, preferred_element_type=jnp.float32).T
    part = sparse_terms(gate_pre, up_pre, back_grad, column, w_gate, w_up, group_rows)
    lane = 128
    score_grp = jnp.swapaxes(score_part.T.reshape(unit_count, spread_exp, CAP, group_rows // CAP), 0, 1)
    score_grp = jnp.pad(score_grp, ((0, 0), (0, 0), (0, 0), (0, lane - group_rows // CAP)))
    sent = jnp.concatenate([jnp.swapaxes(part, 0, 1), score_grp], axis=3)
    arrived_part = lax.all_to_all(sent, "exp", split_axis=0, concat_axis=0, tiled=True)
    sender_block = (jnp.arange(spread_exp, dtype=jnp.int32) * spread_hid + own_hid)[:, None]
    sender_expert = (sender_block * unit_count + jnp.arange(unit_count, dtype=jnp.int32)[None, :]) // 2
    own_combine = lax.dynamic_slice_in_dim(combine_all, own_exp * group_rows, group_rows, 0)
    sender_pick = (expert_ids[:, None] == sender_expert.reshape(1, -1)).astype(jnp.bfloat16)
    sender_column = jnp.dot(own_combine, sender_pick, preferred_element_type=jnp.float32).T
    sender_rows = slot_rows(sender_column, group_rows).reshape(-1)
    place = (sender_rows[:, None] == jnp.arange(group_rows, dtype=jnp.int32)[None, :]).astype(jnp.float32)
    group_sum = jnp.einsum(
        "sj,sd->jd", place, arrived_part[..., :model_width].reshape(-1, model_width),
        precision=lax.Precision.HIGHEST, preferred_element_type=jnp.float32,
    )
    got_scores = arrived_part[..., model_width : model_width + group_rows // CAP]
    got_scores = got_scores.reshape(spread_exp, unit_count, spread_hid, tok_local)
    score_cols = spread_exp * unit_count
    score_width = -(-score_cols // lane) * lane
    hid_scores = jnp.transpose(got_scores, (2, 3, 0, 1)).reshape(spread_hid, tok_local, score_cols)
    hid_scores = jnp.pad(hid_scores, ((0, 0), (0, 0), (0, score_width - score_cols)))
    hid_sent = jnp.concatenate([group_sum.reshape(spread_hid, tok_local, model_width), hid_scores], axis=2)
    spread_rows = lax.all_to_all(hid_sent, "hid", split_axis=0, concat_axis=0, tiled=True)
    input_sum = jnp.sum(spread_rows[..., :model_width], axis=0)
    own_scores = spread_rows[..., model_width : model_width + score_cols]
    own_scores = own_scores.reshape(spread_hid, tok_local, spread_exp, unit_count)
    unit_scores = jnp.transpose(own_scores, (1, 2, 0, 3)).reshape(tok_local, -1)
    expert_scores = jnp.sum(unit_scores.reshape(tok_local, expert_count, 2), axis=2)
    probs_all = softmax_rows(router_logits)
    mean_score = jnp.sum(probs_all * expert_scores, axis=1, keepdims=True)
    logit_grad = (probs_all * (expert_scores - mean_score)).astype(jnp.bfloat16)
    devices = spread_exp * spread_hid
    logit_all = lax.all_to_all(
        jnp.broadcast_to(logit_grad[None], (devices,) + logit_grad.shape), ("exp", "hid"), 0, 0, tiled=True
    ).reshape(-1, expert_count)
    grad_rows = model_width // devices
    token_cols = lax.dynamic_slice_in_dim(gathered, own_block * grad_rows, grad_rows, 1)
    router_grad = jnp.einsum("tc,te->ce", token_cols, logit_all, preferred_element_type=jnp.float32)
    router_part = jnp.einsum("te,de->td", logit_grad, router_w, preferred_element_type=jnp.float32)
    x_grad = (input_sum + router_part).astype(jnp.bfloat16)
    return (x_grad, router_grad)


def solution(mesh):
    placed = (
        P(("exp", "hid"), None),
        P(("exp", "hid"), None),
        P(("exp", "hid"), None),
        P(("exp", "hid"), None),
        P(),
        P(("exp", "hid"), None, None),
        P(("exp", "hid"), None, None),
        P(("exp", "hid"), None, None),
    )
    return jax.shard_map(
        on_device,
        mesh=mesh,
        in_specs=placed,
        out_specs=(P(("exp", "hid"), None), P(("exp", "hid"), None)),
        check_vma=False,
    )
```

```python
import functools
import jax
import jax.numpy as jnp
from jax import lax
from jax.sharding import PartitionSpec as P
from jax.experimental import pallas as pl
from jax.experimental.pallas import tpu as pltpu


def hid_gather_kernel(n, x_ref, out_ref, local_sem, send_sem, recv_sem):
    me = lax.axis_index("hid")
    row = lax.axis_index("exp")
    mesh_ids = pl.DeviceIdType.MESH
    barrier = pltpu.get_barrier_semaphore()
    for k in range(1, n):
        peer = lax.rem(me + k, n)
        pl.semaphore_signal(barrier, inc=1, device_id=(row, peer), device_id_type=mesh_ids)
    pl.semaphore_wait(barrier, n - 1)
    local = pltpu.make_async_copy(x_ref, out_ref.at[me], local_sem)
    local.start()
    copies = []
    for k in range(1, n):
        peer = lax.rem(me + k, n)
        copy = pltpu.make_async_remote_copy(
            src_ref=x_ref,
            dst_ref=out_ref.at[me],
            send_sem=send_sem.at[k],
            recv_sem=recv_sem.at[k],
            device_id=(row, peer),
            device_id_type=mesh_ids,
        )
        copy.start()
        copies.append(copy)
    local.wait()
    for copy in copies:
        copy.wait()


def hid_gather(block):
    n = lax.axis_size("hid")
    return pl.pallas_call(
        functools.partial(hid_gather_kernel, n),
        out_shape=jax.ShapeDtypeStruct((n,) + block.shape, block.dtype),
        in_specs=[pl.BlockSpec(memory_space=pltpu.VMEM)],
        out_specs=pl.BlockSpec(memory_space=pltpu.VMEM),
        scratch_shapes=[
            pltpu.SemaphoreType.DMA,
            pltpu.SemaphoreType.DMA((n,)),
            pltpu.SemaphoreType.DMA((n,)),
        ],
        compiler_params=pltpu.CompilerParams(collective_id=0, has_side_effects=True),
    )(block).reshape((n * block.shape[0],) + block.shape[1:])


def softmax_rows(values):
    top_val = jnp.max(values, axis=-1, keepdims=True)
    raised = jnp.exp(values - top_val)
    return raised / jnp.sum(raised, axis=-1, keepdims=True)


def combine_table(logits, chosen, expert_count):
    picked = jnp.take_along_axis(logits, chosen, axis=1)
    weights = softmax_rows(picked)
    expert_ids = jnp.arange(expert_count, dtype=jnp.int32)
    matched = (chosen[:, :, None] == expert_ids[None, None, :]).astype(jnp.float32)
    return jnp.sum(weights[:, :, None] * matched, axis=1).astype(jnp.bfloat16)


CAP = 4


def slot_rows(column, group_rows):
    shaped = column.reshape(column.shape[:-1] + (-1, group_rows))
    place = jnp.arange(group_rows, dtype=jnp.int32)
    key = jnp.where(shaped != 0, 2 * group_rows - place, -place)
    return lax.top_k(key, CAP)[1]


def dense_terms(x_rows, g_rows, w_gate, w_up, w_down):
    gate_pre = jnp.einsum("td,udf->utf", x_rows, w_gate, preferred_element_type=jnp.float32)
    up_pre = jnp.einsum("td,udf->utf", x_rows, w_up, preferred_element_type=jnp.float32)
    back_grad = jnp.einsum("td,ufd->utf", g_rows, w_down, preferred_element_type=jnp.float32)
    sig_gate = jax.nn.sigmoid(gate_pre)
    act_gate = gate_pre * sig_gate
    score_part = jnp.sum(act_gate * up_pre * back_grad, axis=2).T
    return score_part, gate_pre, up_pre, back_grad


def sparse_terms(gate_pre, up_pre, back_grad, column, w_gate, w_up, group_rows):
    picked = slot_rows(column, group_rows)
    groups = picked.shape[1]
    starts = (jnp.arange(groups, dtype=jnp.int32) * group_rows)[None, :, None]
    rows = (picked + starts).reshape(picked.shape[0], -1)
    take = lambda a: jnp.take_along_axis(a, rows[:, :, None], axis=1)
    gate_s, up_s, back_s = take(gate_pre), take(up_pre), take(back_grad)
    col_s = jnp.take_along_axis(column, rows, axis=1)
    sig_gate = jax.nn.sigmoid(gate_s)
    act_gate = gate_s * sig_gate
    weighted = col_s[:, :, None] * back_s
    grad_gate = (weighted * up_s * sig_gate * (1.0 + gate_s * (1.0 - sig_gate))).astype(jnp.bfloat16)
    grad_up = (weighted * act_gate).astype(jnp.bfloat16)
    part = jnp.einsum("usf,udf->usd", grad_gate, w_gate, preferred_element_type=jnp.float32)
    part = part + jnp.einsum("usf,udf->usd", grad_up, w_up, preferred_element_type=jnp.float32)
    return part.reshape(part.shape[0], groups, CAP, part.shape[-1])


def on_device(tokens, grad_out, router_logits, selected, router_w, w_gate, w_up, w_down):
    tok_local, model_width = tokens.shape
    unit_count = w_gate.shape[0]
    expert_count = router_logits.shape[1]
    spread_exp = lax.axis_size("exp")
    spread_hid = lax.axis_size("hid")
    group_rows = spread_hid * tok_local
    own_exp = lax.axis_index("exp")
    own_hid = lax.axis_index("hid")
    own_block = lax.axis_index(("exp", "hid"))
    unit_expert = (own_block * unit_count + jnp.arange(unit_count, dtype=jnp.int32)) // 2
    expert_ids = jnp.arange(expert_count, dtype=jnp.int32)
    unit_pick = (expert_ids[:, None] == unit_expert[None, :]).astype(jnp.bfloat16)
    combine = combine_table(router_logits, selected, expert_count)
    packed = jnp.concatenate([tokens, grad_out, combine], axis=1)
    gathered = lax.all_gather(hid_gather(packed), "exp", axis=0, tiled=True)
    combine_all = gathered[:, 2 * model_width :]
    score_part, gate_pre, up_pre, back_grad = dense_terms(
        gathered[:, :model_width], gathered[:, model_width : 2 * model_width], w_gate, w_up, w_down
    )
    column = jnp.dot(combine_all, unit_pick, preferred_element_type=jnp.float32).T
    part = sparse_terms(gate_pre, up_pre, back_grad, column, w_gate, w_up, group_rows)
    lane = 128
    score_grp = jnp.swapaxes(score_part.T.reshape(unit_count, spread_exp, CAP, group_rows // CAP), 0, 1)
    score_grp = jnp.pad(score_grp, ((0, 0), (0, 0), (0, 0), (0, lane - group_rows // CAP)))
    sent = jnp.concatenate([jnp.swapaxes(part, 0, 1), score_grp], axis=3)
    arrived_part = lax.all_to_all(sent, "exp", split_axis=0, concat_axis=0, tiled=True)
    sender_block = (jnp.arange(spread_exp, dtype=jnp.int32) * spread_hid + own_hid)[:, None]
    sender_expert = (sender_block * unit_count + jnp.arange(unit_count, dtype=jnp.int32)[None, :]) // 2
    own_combine = lax.dynamic_slice_in_dim(combine_all, own_exp * group_rows, group_rows, 0)
    sender_pick = (expert_ids[:, None] == sender_expert.reshape(1, -1)).astype(jnp.bfloat16)
    sender_column = jnp.dot(own_combine, sender_pick, preferred_element_type=jnp.float32).T
    sender_rows = slot_rows(sender_column, group_rows).reshape(-1)
    place = (sender_rows[:, None] == jnp.arange(group_rows, dtype=jnp.int32)[None, :]).astype(jnp.float32)
    group_sum = jnp.einsum(
        "sj,sd->jd", place, arrived_part[..., :model_width].reshape(-1, model_width),
        precision=lax.Precision.HIGHEST, preferred_element_type=jnp.float32,
    )
    got_scores = arrived_part[..., model_width : model_width + group_rows // CAP]
    got_scores = got_scores.reshape(spread_exp, unit_count, spread_hid, tok_local)
    score_cols = spread_exp * unit_count
    score_width = -(-score_cols // lane) * lane
    hid_scores = jnp.transpose(got_scores, (2, 3, 0, 1)).reshape(spread_hid, tok_local, score_cols)
    hid_scores = jnp.pad(hid_scores, ((0, 0), (0, 0), (0, score_width - score_cols)))
    hid_sent = jnp.concatenate([group_sum.reshape(spread_hid, tok_local, model_width), hid_scores], axis=2)
    spread_rows = lax.all_to_all(hid_sent, "hid", split_axis=0, concat_axis=0, tiled=True)
    input_sum = jnp.sum(spread_rows[..., :model_width], axis=0)
    own_scores = spread_rows[..., model_width : model_width + score_cols]
    own_scores = own_scores.reshape(spread_hid, tok_local, spread_exp, unit_count)
    unit_scores = jnp.transpose(own_scores, (1, 2, 0, 3)).reshape(tok_local, -1)
    expert_scores = jnp.sum(unit_scores.reshape(tok_local, expert_count, 2), axis=2)
    probs_all = softmax_rows(router_logits)
    mean_score = jnp.sum(probs_all * expert_scores, axis=1, keepdims=True)
    logit_grad = (probs_all * (expert_scores - mean_score)).astype(jnp.bfloat16)
    devices = spread_exp * spread_hid
    logit_all = lax.all_to_all(
        jnp.broadcast_to(logit_grad[None], (devices,) + logit_grad.shape), ("exp", "hid"), 0, 0, tiled=True
    ).reshape(-1, expert_count)
    grad_rows = model_width // devices
    token_cols = lax.dynamic_slice_in_dim(gathered, own_block * grad_rows, grad_rows, 1)
    router_grad = jnp.einsum("tc,te->ce", token_cols, logit_all, preferred_element_type=jnp.float32)
    router_part = jnp.einsum("te,de->td", logit_grad, router_w, preferred_element_type=jnp.float32)
    x_grad = (input_sum + router_part).astype(jnp.bfloat16)
    return (x_grad, router_grad)


def solution(mesh):
    placed = (
        P(("exp", "hid"), None),
        P(("exp", "hid"), None),
        P(("exp", "hid"), None),
        P(("exp", "hid"), None),
        P(),
        P(("exp", "hid"), None, None),
        P(("exp", "hid"), None, None),
        P(("exp", "hid"), None, None),
    )
    return jax.shard_map(
        on_device,
        mesh=mesh,
        in_specs=placed,
        out_specs=(P(("exp", "hid"), None), P(("exp", "hid"), None)),
        check_vma=False,
    )
```

```python
import functools
import jax
import jax.numpy as jnp
from jax import lax
from jax.sharding import PartitionSpec as P
from jax.experimental import pallas as pl
from jax.experimental.pallas import tpu as pltpu


def hid_gather_kernel(n, x_ref, out_ref, local_sem, send_sem, recv_sem):
    me = lax.axis_index("hid")
    row = lax.axis_index("exp")
    mesh_ids = pl.DeviceIdType.MESH
    barrier = pltpu.get_barrier_semaphore()
    for k in range(1, n):
        peer = lax.rem(me + k, n)
        pl.semaphore_signal(barrier, inc=1, device_id=(row, peer), device_id_type=mesh_ids)
    pl.semaphore_wait(barrier, n - 1)
    local = pltpu.make_async_copy(x_ref, out_ref.at[me], local_sem)
    local.start()
    copies = []
    for k in range(1, n):
        peer = lax.rem(me + k, n)
        copy = pltpu.make_async_remote_copy(
            src_ref=x_ref,
            dst_ref=out_ref.at[me],
            send_sem=send_sem.at[k],
            recv_sem=recv_sem.at[k],
            device_id=(row, peer),
            device_id_type=mesh_ids,
        )
        copy.start()
        copies.append(copy)
    local.wait()
    for copy in copies:
        copy.wait()


def hid_gather(block):
    n = lax.axis_size("hid")
    return pl.pallas_call(
        functools.partial(hid_gather_kernel, n),
        out_shape=jax.ShapeDtypeStruct((n,) + block.shape, block.dtype),
        in_specs=[pl.BlockSpec(memory_space=pltpu.VMEM)],
        out_specs=pl.BlockSpec(memory_space=pltpu.VMEM),
        scratch_shapes=[
            pltpu.SemaphoreType.DMA,
            pltpu.SemaphoreType.DMA((n,)),
            pltpu.SemaphoreType.DMA((n,)),
        ],
        compiler_params=pltpu.CompilerParams(collective_id=0, has_side_effects=True),
    )(block).reshape((n * block.shape[0],) + block.shape[1:])


def softmax_rows(values):
    top_val = jnp.max(values, axis=-1, keepdims=True)
    raised = jnp.exp(values - top_val)
    return raised / jnp.sum(raised, axis=-1, keepdims=True)


def combine_table(logits, chosen, expert_count):
    picked = jnp.take_along_axis(logits, chosen, axis=1)
    weights = softmax_rows(picked)
    expert_ids = jnp.arange(expert_count, dtype=jnp.int32)
    matched = (chosen[:, :, None] == expert_ids[None, None, :]).astype(jnp.float32)
    return jnp.sum(weights[:, :, None] * matched, axis=1).astype(jnp.bfloat16)


CAP = 4


def slot_rows(column, group_rows):
    shaped = column.reshape(column.shape[:-1] + (-1, group_rows))
    place = jnp.arange(group_rows, dtype=jnp.int32)
    key = jnp.where(shaped != 0, 2 * group_rows - place, -place)
    return lax.top_k(key, CAP)[1]


def split3(value):
    hi = value.astype(jnp.bfloat16)
    rest = value - hi.astype(jnp.float32)
    mid = rest.astype(jnp.bfloat16)
    lo = (rest - mid.astype(jnp.float32)).astype(jnp.bfloat16)
    return jnp.concatenate([hi, mid, lo], axis=-1)


def join3(pieces, width):
    part = lambda i: pieces[..., i * width : (i + 1) * width].astype(jnp.float32)
    return (part(0) + part(1)) + part(2)


def dense_terms(x_rows, g_rows, w_gate, w_up, w_down):
    gate_pre = jnp.einsum("td,udf->utf", x_rows, w_gate, preferred_element_type=jnp.float32)
    up_pre = jnp.einsum("td,udf->utf", x_rows, w_up, preferred_element_type=jnp.float32)
    back_grad = jnp.einsum("td,ufd->utf", g_rows, w_down, preferred_element_type=jnp.float32)
    sig_gate = jax.nn.sigmoid(gate_pre)
    act_gate = gate_pre * sig_gate
    score_part = jnp.sum(act_gate * up_pre * back_grad, axis=2).T
    return score_part, gate_pre, up_pre, back_grad


def sparse_terms(gate_pre, up_pre, back_grad, column, w_gate, w_up, group_rows):
    picked = slot_rows(column, group_rows)
    groups = picked.shape[1]
    starts = (jnp.arange(groups, dtype=jnp.int32) * group_rows)[None, :, None]
    rows = (picked + starts).reshape(picked.shape[0], -1)
    take = lambda a: jnp.take_along_axis(a, rows[:, :, None], axis=1)
    gate_s, up_s, back_s = take(gate_pre), take(up_pre), take(back_grad)
    col_s = jnp.take_along_axis(column, rows, axis=1)
    sig_gate = jax.nn.sigmoid(gate_s)
    act_gate = gate_s * sig_gate
    weighted = col_s[:, :, None] * back_s
    grad_gate = (weighted * up_s * sig_gate * (1.0 + gate_s * (1.0 - sig_gate))).astype(jnp.bfloat16)
    grad_up = (weighted * act_gate).astype(jnp.bfloat16)
    part = jnp.einsum("usf,udf->usd", grad_gate, w_gate, preferred_element_type=jnp.float32)
    part = part + jnp.einsum("usf,udf->usd", grad_up, w_up, preferred_element_type=jnp.float32)
    return part.reshape(part.shape[0], groups, CAP, part.shape[-1])


def on_device(tokens, grad_out, router_logits, selected, router_w, w_gate, w_up, w_down):
    tok_local, model_width = tokens.shape
    unit_count = w_gate.shape[0]
    expert_count = router_logits.shape[1]
    spread_exp = lax.axis_size("exp")
    spread_hid = lax.axis_size("hid")
    group_rows = spread_hid * tok_local
    own_exp = lax.axis_index("exp")
    own_hid = lax.axis_index("hid")
    own_block = lax.axis_index(("exp", "hid"))
    unit_expert = (own_block * unit_count + jnp.arange(unit_count, dtype=jnp.int32)) // 2
    expert_ids = jnp.arange(expert_count, dtype=jnp.int32)
    unit_pick = (expert_ids[:, None] == unit_expert[None, :]).astype(jnp.bfloat16)
    combine = combine_table(router_logits, selected, expert_count)
    packed = jnp.concatenate([tokens, grad_out, combine], axis=1)
    gathered = lax.all_gather(hid_gather(packed), "exp", axis=0, tiled=True)
    combine_all = gathered[:, 2 * model_width :]
    score_part, gate_pre, up_pre, back_grad = dense_terms(
        gathered[:, :model_width], gathered[:, model_width : 2 * model_width], w_gate, w_up, w_down
    )
    column = jnp.dot(combine_all, unit_pick, preferred_element_type=jnp.float32).T
    part = sparse_terms(gate_pre, up_pre, back_grad, column, w_gate, w_up, group_rows)
    lane = 128
    score_grp = jnp.swapaxes(score_part.T.reshape(unit_count, spread_exp, CAP, group_rows // CAP), 0, 1)
    score_grp = split3(score_grp)
    score_grp = jnp.pad(score_grp, ((0, 0), (0, 0), (0, 0), (0, lane - score_grp.shape[3])))
    sent = jnp.concatenate([jnp.swapaxes(part, 0, 1).astype(jnp.bfloat16), score_grp], axis=3)
    arrived_part = lax.all_to_all(sent, "exp", split_axis=0, concat_axis=0, tiled=True)
    sender_block = (jnp.arange(spread_exp, dtype=jnp.int32) * spread_hid + own_hid)[:, None]
    sender_expert = (sender_block * unit_count + jnp.arange(unit_count, dtype=jnp.int32)[None, :]) // 2
    own_combine = lax.dynamic_slice_in_dim(combine_all, own_exp * group_rows, group_rows, 0)
    sender_pick = (expert_ids[:, None] == sender_expert.reshape(1, -1)).astype(jnp.bfloat16)
    sender_column = jnp.dot(own_combine, sender_pick, preferred_element_type=jnp.float32).T
    sender_rows = slot_rows(sender_column, group_rows).reshape(-1)
    place = (sender_rows[:, None] == jnp.arange(group_rows, dtype=jnp.int32)[None, :]).astype(jnp.bfloat16)
    group_sum = jnp.einsum(
        "sj,sd->jd", place, arrived_part[..., :model_width].reshape(-1, model_width),
        preferred_element_type=jnp.float32,
    )
    got_scores = join3(arrived_part[..., model_width:], group_rows // CAP)
    got_scores = got_scores.reshape(spread_exp, unit_count, spread_hid, tok_local)
    score_cols = spread_exp * unit_count
    hid_scores = jnp.transpose(got_scores, (2, 3, 0, 1)).reshape(spread_hid, tok_local, score_cols)
    hid_scores = split3(hid_scores)
    score_width = -(-hid_scores.shape[2] // lane) * lane
    hid_scores = jnp.pad(hid_scores, ((0, 0), (0, 0), (0, score_width - hid_scores.shape[2])))
    hid_sent = jnp.concatenate(
        [group_sum.reshape(spread_hid, tok_local, model_width).astype(jnp.bfloat16), hid_scores], axis=2
    )
    spread_rows = lax.all_to_all(hid_sent, "hid", split_axis=0, concat_axis=0, tiled=True)
    input_sum = jnp.sum(spread_rows[..., :model_width].astype(jnp.float32), axis=0)
    own_scores = join3(spread_rows[..., model_width:], score_cols)
    own_scores = own_scores.reshape(spread_hid, tok_local, spread_exp, unit_count)
    unit_scores = jnp.transpose(own_scores, (1, 2, 0, 3)).reshape(tok_local, -1)
    expert_scores = jnp.sum(unit_scores.reshape(tok_local, expert_count, 2), axis=2)
    probs_all = softmax_rows(router_logits)
    mean_score = jnp.sum(probs_all * expert_scores, axis=1, keepdims=True)
    logit_grad = (probs_all * (expert_scores - mean_score)).astype(jnp.bfloat16)
    devices = spread_exp * spread_hid
    logit_all = lax.all_to_all(
        jnp.broadcast_to(logit_grad[None], (devices,) + logit_grad.shape), ("exp", "hid"), 0, 0, tiled=True
    ).reshape(-1, expert_count)
    grad_rows = model_width // devices
    token_cols = lax.dynamic_slice_in_dim(gathered, own_block * grad_rows, grad_rows, 1)
    router_grad = jnp.einsum("tc,te->ce", token_cols, logit_all, preferred_element_type=jnp.float32)
    router_part = jnp.einsum("te,de->td", logit_grad, router_w, preferred_element_type=jnp.float32)
    x_grad = (input_sum + router_part).astype(jnp.bfloat16)
    return (x_grad, router_grad)


def solution(mesh):
    placed = (
        P(("exp", "hid"), None),
        P(("exp", "hid"), None),
        P(("exp", "hid"), None),
        P(("exp", "hid"), None),
        P(),
        P(("exp", "hid"), None, None),
        P(("exp", "hid"), None, None),
        P(("exp", "hid"), None, None),
    )
    return jax.shard_map(
        on_device,
        mesh=mesh,
        in_specs=placed,
        out_specs=(P(("exp", "hid"), None), P(("exp", "hid"), None)),
        check_vma=False,
    )
```

```python
import functools
import jax
import jax.numpy as jnp
from jax import lax
from jax.sharding import PartitionSpec as P
from jax.experimental import pallas as pl
from jax.experimental.pallas import tpu as pltpu


def hid_gather_kernel(n, x_ref, out_ref, local_sem, send_sem, recv_sem):
    me = lax.axis_index("hid")
    row = lax.axis_index("exp")
    mesh_ids = pl.DeviceIdType.MESH
    barrier = pltpu.get_barrier_semaphore()
    for k in range(1, n):
        peer = lax.rem(me + k, n)
        pl.semaphore_signal(barrier, inc=1, device_id=(row, peer), device_id_type=mesh_ids)
    pl.semaphore_wait(barrier, n - 1)
    local = pltpu.make_async_copy(x_ref, out_ref.at[me], local_sem)
    local.start()
    copies = []
    for k in range(1, n):
        peer = lax.rem(me + k, n)
        copy = pltpu.make_async_remote_copy(
            src_ref=x_ref,
            dst_ref=out_ref.at[me],
            send_sem=send_sem.at[k],
            recv_sem=recv_sem.at[k],
            device_id=(row, peer),
            device_id_type=mesh_ids,
        )
        copy.start()
        copies.append(copy)
    local.wait()
    for copy in copies:
        copy.wait()


def hid_gather(block):
    n = lax.axis_size("hid")
    return pl.pallas_call(
        functools.partial(hid_gather_kernel, n),
        out_shape=jax.ShapeDtypeStruct((n,) + block.shape, block.dtype),
        in_specs=[pl.BlockSpec(memory_space=pltpu.VMEM)],
        out_specs=pl.BlockSpec(memory_space=pltpu.VMEM),
        scratch_shapes=[
            pltpu.SemaphoreType.DMA,
            pltpu.SemaphoreType.DMA((n,)),
            pltpu.SemaphoreType.DMA((n,)),
        ],
        compiler_params=pltpu.CompilerParams(collective_id=0, has_side_effects=True),
    )(block).reshape((n * block.shape[0],) + block.shape[1:])


def softmax_rows(values):
    top_val = jnp.max(values, axis=-1, keepdims=True)
    raised = jnp.exp(values - top_val)
    return raised / jnp.sum(raised, axis=-1, keepdims=True)


def combine_table(logits, chosen, expert_count):
    picked = jnp.take_along_axis(logits, chosen, axis=1)
    weights = softmax_rows(picked)
    expert_ids = jnp.arange(expert_count, dtype=jnp.int32)
    matched = (chosen[:, :, None] == expert_ids[None, None, :]).astype(jnp.float32)
    return jnp.sum(weights[:, :, None] * matched, axis=1).astype(jnp.bfloat16)


CAP = 4


def slot_rows(column, group_rows):
    shaped = column.reshape(column.shape[:-1] + (-1, group_rows))
    place = jnp.arange(group_rows, dtype=jnp.int32)
    key = jnp.where(shaped != 0, 2 * group_rows - place, -place)
    return lax.top_k(key, CAP)[1]


def split3(value):
    hi = value.astype(jnp.bfloat16)
    rest = value - hi.astype(jnp.float32)
    mid = rest.astype(jnp.bfloat16)
    lo = (rest - mid.astype(jnp.float32)).astype(jnp.bfloat16)
    return jnp.concatenate([hi, mid, lo], axis=-1)


def join3(pieces, width):
    part = lambda i: pieces[..., i * width : (i + 1) * width].astype(jnp.float32)
    return (part(0) + part(1)) + part(2)


def dense_terms(x_rows, g_rows, w_gate, w_up, w_down):
    gate_pre = jnp.einsum("td,udf->utf", x_rows, w_gate, preferred_element_type=jnp.float32)
    up_pre = jnp.einsum("td,udf->utf", x_rows, w_up, preferred_element_type=jnp.float32)
    back_grad = jnp.einsum("td,ufd->utf", g_rows, w_down, preferred_element_type=jnp.float32)
    sig_gate = jax.nn.sigmoid(gate_pre)
    act_gate = gate_pre * sig_gate
    score_part = jnp.sum(act_gate * up_pre * back_grad, axis=2).T
    return score_part, gate_pre, up_pre, back_grad


def sparse_terms(gate_pre, up_pre, back_grad, column, w_gate, w_up, group_rows):
    picked = slot_rows(column, group_rows)
    groups = picked.shape[1]
    starts = (jnp.arange(groups, dtype=jnp.int32) * group_rows)[None, :, None]
    rows = (picked + starts).reshape(picked.shape[0], -1)
    take = lambda a: jnp.take_along_axis(a, rows[:, :, None], axis=1)
    gate_s, up_s, back_s = take(gate_pre), take(up_pre), take(back_grad)
    col_s = jnp.take_along_axis(column, rows, axis=1)
    sig_gate = jax.nn.sigmoid(gate_s)
    act_gate = gate_s * sig_gate
    weighted = col_s[:, :, None] * back_s
    grad_gate = (weighted * up_s * sig_gate * (1.0 + gate_s * (1.0 - sig_gate))).astype(jnp.bfloat16)
    grad_up = (weighted * act_gate).astype(jnp.bfloat16)
    part = jnp.einsum("usf,udf->usd", grad_gate, w_gate, preferred_element_type=jnp.float32)
    part = part + jnp.einsum("usf,udf->usd", grad_up, w_up, preferred_element_type=jnp.float32)
    return part.reshape(part.shape[0], groups, CAP, part.shape[-1])


def on_device(tokens, grad_out, router_logits, selected, router_w, w_gate, w_up, w_down):
    tok_local, model_width = tokens.shape
    unit_count = w_gate.shape[0]
    expert_count = router_logits.shape[1]
    spread_exp = lax.axis_size("exp")
    spread_hid = lax.axis_size("hid")
    group_rows = spread_hid * tok_local
    own_exp = lax.axis_index("exp")
    own_hid = lax.axis_index("hid")
    own_block = lax.axis_index(("exp", "hid"))
    unit_expert = (own_block * unit_count + jnp.arange(unit_count, dtype=jnp.int32)) // 2
    expert_ids = jnp.arange(expert_count, dtype=jnp.int32)
    unit_pick = (expert_ids[:, None] == unit_expert[None, :]).astype(jnp.bfloat16)
    combine = combine_table(router_logits, selected, expert_count)
    packed = jnp.concatenate([tokens, combine, grad_out], axis=1)
    near = hid_gather(packed)
    split_at = model_width + expert_count
    front = lax.all_gather(near[:, :split_at], "exp", axis=0, tiled=True)
    back = lax.all_gather(near[:, split_at:], "exp", axis=0, tiled=True)
    tokens_all = front[:, :model_width]
    combine_all = front[:, model_width:]
    score_part, gate_pre, up_pre, back_grad = dense_terms(tokens_all, back, w_gate, w_up, w_down)
    column = jnp.dot(combine_all, unit_pick, preferred_element_type=jnp.float32).T
    part = sparse_terms(gate_pre, up_pre, back_grad, column, w_gate, w_up, group_rows)
    lane = 128
    score_grp = jnp.swapaxes(score_part.T.reshape(unit_count, spread_exp, CAP, group_rows // CAP), 0, 1)
    score_grp = split3(score_grp)
    score_grp = jnp.pad(score_grp, ((0, 0), (0, 0), (0, 0), (0, lane - score_grp.shape[3])))
    sent = jnp.concatenate([jnp.swapaxes(part, 0, 1).astype(jnp.bfloat16), score_grp], axis=3)
    arrived_part = lax.all_to_all(sent, "exp", split_axis=0, concat_axis=0, tiled=True)
    sender_block = (jnp.arange(spread_exp, dtype=jnp.int32) * spread_hid + own_hid)[:, None]
    sender_expert = (sender_block * unit_count + jnp.arange(unit_count, dtype=jnp.int32)[None, :]) // 2
    own_combine = lax.dynamic_slice_in_dim(combine_all, own_exp * group_rows, group_rows, 0)
    sender_pick = (expert_ids[:, None] == sender_expert.reshape(1, -1)).astype(jnp.bfloat16)
    sender_column = jnp.dot(own_combine, sender_pick, preferred_element_type=jnp.float32).T
    sender_rows = slot_rows(sender_column, group_rows).reshape(-1)
    place = (sender_rows[:, None] == jnp.arange(group_rows, dtype=jnp.int32)[None, :]).astype(jnp.bfloat16)
    group_sum = jnp.einsum(
        "sj,sd->jd", place, arrived_part[..., :model_width].reshape(-1, model_width),
        preferred_element_type=jnp.float32,
    )
    got_scores = join3(arrived_part[..., model_width:], group_rows // CAP)
    got_scores = got_scores.reshape(spread_exp, unit_count, spread_hid, tok_local)
    score_cols = spread_exp * unit_count
    hid_scores = jnp.transpose(got_scores, (2, 3, 0, 1)).reshape(spread_hid, tok_local, score_cols)
    hid_scores = split3(hid_scores)
    score_width = -(-hid_scores.shape[2] // lane) * lane
    hid_scores = jnp.pad(hid_scores, ((0, 0), (0, 0), (0, score_width - hid_scores.shape[2])))
    hid_sent = jnp.concatenate(
        [group_sum.reshape(spread_hid, tok_local, model_width).astype(jnp.bfloat16), hid_scores], axis=2
    )
    spread_rows = lax.all_to_all(hid_sent, "hid", split_axis=0, concat_axis=0, tiled=True)
    input_sum = jnp.sum(spread_rows[..., :model_width].astype(jnp.float32), axis=0)
    own_scores = join3(spread_rows[..., model_width:], score_cols)
    own_scores = own_scores.reshape(spread_hid, tok_local, spread_exp, unit_count)
    unit_scores = jnp.transpose(own_scores, (1, 2, 0, 3)).reshape(tok_local, -1)
    expert_scores = jnp.sum(unit_scores.reshape(tok_local, expert_count, 2), axis=2)
    probs_all = softmax_rows(router_logits)
    mean_score = jnp.sum(probs_all * expert_scores, axis=1, keepdims=True)
    logit_grad = (probs_all * (expert_scores - mean_score)).astype(jnp.bfloat16)
    devices = spread_exp * spread_hid
    logit_all = lax.all_to_all(
        jnp.broadcast_to(logit_grad[None], (devices,) + logit_grad.shape), ("exp", "hid"), 0, 0, tiled=True
    ).reshape(-1, expert_count)
    grad_rows = model_width // devices
    token_cols = lax.dynamic_slice_in_dim(tokens_all, own_block * grad_rows, grad_rows, 1)
    router_grad = jnp.einsum("tc,te->ce", token_cols, logit_all, preferred_element_type=jnp.float32)
    router_part = jnp.einsum("te,de->td", logit_grad, router_w, preferred_element_type=jnp.float32)
    x_grad = (input_sum + router_part).astype(jnp.bfloat16)
    return (x_grad, router_grad)


def solution(mesh):
    placed = (
        P(("exp", "hid"), None),
        P(("exp", "hid"), None),
        P(("exp", "hid"), None),
        P(("exp", "hid"), None),
        P(),
        P(("exp", "hid"), None, None),
        P(("exp", "hid"), None, None),
        P(("exp", "hid"), None, None),
    )
    return jax.shard_map(
        on_device,
        mesh=mesh,
        in_specs=placed,
        out_specs=(P(("exp", "hid"), None), P(("exp", "hid"), None)),
        check_vma=False,
    )
```

```python
import functools
import jax
import jax.numpy as jnp
from jax import lax
from jax.sharding import PartitionSpec as P
from jax.experimental import pallas as pl
from jax.experimental.pallas import tpu as pltpu


def hid_gather_kernel(n, x_ref, out_ref, local_sem, send_sem, recv_sem):
    me = lax.axis_index("hid")
    row = lax.axis_index("exp")
    mesh_ids = pl.DeviceIdType.MESH
    barrier = pltpu.get_barrier_semaphore()
    for k in range(1, n):
        peer = lax.rem(me + k, n)
        pl.semaphore_signal(barrier, inc=1, device_id=(row, peer), device_id_type=mesh_ids)
    pl.semaphore_wait(barrier, n - 1)
    local = pltpu.make_async_copy(x_ref, out_ref.at[me], local_sem)
    local.start()
    copies = []
    for k in range(1, n):
        peer = lax.rem(me + k, n)
        copy = pltpu.make_async_remote_copy(
            src_ref=x_ref,
            dst_ref=out_ref.at[me],
            send_sem=send_sem.at[k],
            recv_sem=recv_sem.at[k],
            device_id=(row, peer),
            device_id_type=mesh_ids,
        )
        copy.start()
        copies.append(copy)
    local.wait()
    for copy in copies:
        copy.wait()


def exchange_kernel(axis, n, x_ref, out_ref, local_sem, send_sem, recv_sem):
    me = lax.axis_index(axis)
    own_exp = lax.axis_index("exp")
    own_hid = lax.axis_index("hid")
    mesh_ids = pl.DeviceIdType.MESH
    where = lambda peer: (peer, own_hid) if axis == "exp" else (own_exp, peer)
    barrier = pltpu.get_barrier_semaphore()
    for k in range(1, n):
        peer = lax.rem(me + k, n)
        pl.semaphore_signal(barrier, inc=1, device_id=where(peer), device_id_type=mesh_ids)
    pl.semaphore_wait(barrier, n - 1)
    local = pltpu.make_async_copy(x_ref.at[me], out_ref.at[me], local_sem)
    local.start()
    copies = []
    for k in range(1, n):
        peer = lax.rem(me + k, n)
        copy = pltpu.make_async_remote_copy(
            src_ref=x_ref.at[peer],
            dst_ref=out_ref.at[me],
            send_sem=send_sem.at[k],
            recv_sem=recv_sem.at[k],
            device_id=where(peer),
            device_id_type=mesh_ids,
        )
        copy.start()
        copies.append(copy)
    local.wait()
    for copy in copies:
        copy.wait()


def exchange(chunks, axis, kernel_id):
    n = chunks.shape[0]
    return pl.pallas_call(
        functools.partial(exchange_kernel, axis, n),
        out_shape=jax.ShapeDtypeStruct(chunks.shape, chunks.dtype),
        in_specs=[pl.BlockSpec(memory_space=pltpu.VMEM)],
        out_specs=pl.BlockSpec(memory_space=pltpu.VMEM),
        scratch_shapes=[
            pltpu.SemaphoreType.DMA,
            pltpu.SemaphoreType.DMA((n,)),
            pltpu.SemaphoreType.DMA((n,)),
        ],
        compiler_params=pltpu.CompilerParams(collective_id=kernel_id, has_side_effects=True),
    )(chunks)


def hid_gather(block):
    n = lax.axis_size("hid")
    return pl.pallas_call(
        functools.partial(hid_gather_kernel, n),
        out_shape=jax.ShapeDtypeStruct((n,) + block.shape, block.dtype),
        in_specs=[pl.BlockSpec(memory_space=pltpu.VMEM)],
        out_specs=pl.BlockSpec(memory_space=pltpu.VMEM),
        scratch_shapes=[
            pltpu.SemaphoreType.DMA,
            pltpu.SemaphoreType.DMA((n,)),
            pltpu.SemaphoreType.DMA((n,)),
        ],
        compiler_params=pltpu.CompilerParams(collective_id=0, has_side_effects=True),
    )(block).reshape((n * block.shape[0],) + block.shape[1:])


def softmax_rows(values):
    top_val = jnp.max(values, axis=-1, keepdims=True)
    raised = jnp.exp(values - top_val)
    return raised / jnp.sum(raised, axis=-1, keepdims=True)


def combine_table(logits, chosen, expert_count):
    picked = jnp.take_along_axis(logits, chosen, axis=1)
    weights = softmax_rows(picked)
    expert_ids = jnp.arange(expert_count, dtype=jnp.int32)
    matched = (chosen[:, :, None] == expert_ids[None, None, :]).astype(jnp.float32)
    return jnp.sum(weights[:, :, None] * matched, axis=1).astype(jnp.bfloat16)


CAP = 4


def slot_rows(column, group_rows):
    shaped = column.reshape(column.shape[:-1] + (-1, group_rows))
    place = jnp.arange(group_rows, dtype=jnp.int32)
    key = jnp.where(shaped != 0, 2 * group_rows - place, -place)
    return lax.top_k(key, CAP)[1]


def split3(value):
    hi = value.astype(jnp.bfloat16)
    rest = value - hi.astype(jnp.float32)
    mid = rest.astype(jnp.bfloat16)
    lo = (rest - mid.astype(jnp.float32)).astype(jnp.bfloat16)
    return jnp.concatenate([hi, mid, lo], axis=-1)


def join3(pieces, width):
    part = lambda i: pieces[..., i * width : (i + 1) * width].astype(jnp.float32)
    return (part(0) + part(1)) + part(2)


def dense_terms(x_rows, g_rows, w_gate, w_up, w_down):
    gate_pre = jnp.einsum("td,udf->utf", x_rows, w_gate, preferred_element_type=jnp.float32)
    up_pre = jnp.einsum("td,udf->utf", x_rows, w_up, preferred_element_type=jnp.float32)
    back_grad = jnp.einsum("td,ufd->utf", g_rows, w_down, preferred_element_type=jnp.float32)
    sig_gate = jax.nn.sigmoid(gate_pre)
    act_gate = gate_pre * sig_gate
    score_part = jnp.sum(act_gate * up_pre * back_grad, axis=2).T
    return score_part, gate_pre, up_pre, back_grad


def sparse_terms(gate_pre, up_pre, back_grad, column, w_gate, w_up, group_rows):
    picked = slot_rows(column, group_rows)
    groups = picked.shape[1]
    starts = (jnp.arange(groups, dtype=jnp.int32) * group_rows)[None, :, None]
    rows = (picked + starts).reshape(picked.shape[0], -1)
    take = lambda a: jnp.take_along_axis(a, rows[:, :, None], axis=1)
    gate_s, up_s, back_s = take(gate_pre), take(up_pre), take(back_grad)
    col_s = jnp.take_along_axis(column, rows, axis=1)
    sig_gate = jax.nn.sigmoid(gate_s)
    act_gate = gate_s * sig_gate
    weighted = col_s[:, :, None] * back_s
    grad_gate = (weighted * up_s * sig_gate * (1.0 + gate_s * (1.0 - sig_gate))).astype(jnp.bfloat16)
    grad_up = (weighted * act_gate).astype(jnp.bfloat16)
    part = jnp.einsum("usf,udf->usd", grad_gate, w_gate, preferred_element_type=jnp.float32)
    part = part + jnp.einsum("usf,udf->usd", grad_up, w_up, preferred_element_type=jnp.float32)
    return part.reshape(part.shape[0], groups, CAP, part.shape[-1])


def on_device(tokens, grad_out, router_logits, selected, router_w, w_gate, w_up, w_down):
    tok_local, model_width = tokens.shape
    unit_count = w_gate.shape[0]
    expert_count = router_logits.shape[1]
    spread_exp = lax.axis_size("exp")
    spread_hid = lax.axis_size("hid")
    group_rows = spread_hid * tok_local
    own_exp = lax.axis_index("exp")
    own_hid = lax.axis_index("hid")
    own_block = lax.axis_index(("exp", "hid"))
    unit_expert = (own_block * unit_count + jnp.arange(unit_count, dtype=jnp.int32)) // 2
    expert_ids = jnp.arange(expert_count, dtype=jnp.int32)
    unit_pick = (expert_ids[:, None] == unit_expert[None, :]).astype(jnp.bfloat16)
    combine = combine_table(router_logits, selected, expert_count)
    packed = jnp.concatenate([tokens, grad_out, combine], axis=1)
    gathered = lax.all_gather(hid_gather(packed), "exp", axis=0, tiled=True)
    combine_all = gathered[:, 2 * model_width :]
    score_part, gate_pre, up_pre, back_grad = dense_terms(
        gathered[:, :model_width], gathered[:, model_width : 2 * model_width], w_gate, w_up, w_down
    )
    column = jnp.dot(combine_all, unit_pick, preferred_element_type=jnp.float32).T
    part = sparse_terms(gate_pre, up_pre, back_grad, column, w_gate, w_up, group_rows)
    lane = 128
    score_grp = jnp.swapaxes(score_part.T.reshape(unit_count, spread_exp, CAP, group_rows // CAP), 0, 1)
    score_grp = split3(score_grp)
    score_grp = jnp.pad(score_grp, ((0, 0), (0, 0), (0, 0), (0, lane - score_grp.shape[3])))
    sent = jnp.concatenate([jnp.swapaxes(part, 0, 1).astype(jnp.bfloat16), score_grp], axis=3)
    arrived_part = exchange(sent, "exp", 1)
    sender_block = (jnp.arange(spread_exp, dtype=jnp.int32) * spread_hid + own_hid)[:, None]
    sender_expert = (sender_block * unit_count + jnp.arange(unit_count, dtype=jnp.int32)[None, :]) // 2
    own_combine = lax.dynamic_slice_in_dim(combine_all, own_exp * group_rows, group_rows, 0)
    sender_pick = (expert_ids[:, None] == sender_expert.reshape(1, -1)).astype(jnp.bfloat16)
    sender_column = jnp.dot(own_combine, sender_pick, preferred_element_type=jnp.float32).T
    sender_rows = slot_rows(sender_column, group_rows).reshape(-1)
    place = (sender_rows[:, None] == jnp.arange(group_rows, dtype=jnp.int32)[None, :]).astype(jnp.bfloat16)
    group_sum = jnp.einsum(
        "sj,sd->jd", place, arrived_part[..., :model_width].reshape(-1, model_width),
        preferred_element_type=jnp.float32,
    )
    got_scores = join3(arrived_part[..., model_width:], group_rows // CAP)
    got_scores = got_scores.reshape(spread_exp, unit_count, spread_hid, tok_local)
    score_cols = spread_exp * unit_count
    hid_scores = jnp.transpose(got_scores, (2, 3, 0, 1)).reshape(spread_hid, tok_local, score_cols)
    hid_scores = split3(hid_scores)
    score_width = -(-hid_scores.shape[2] // lane) * lane
    hid_scores = jnp.pad(hid_scores, ((0, 0), (0, 0), (0, score_width - hid_scores.shape[2])))
    hid_sent = jnp.concatenate(
        [group_sum.reshape(spread_hid, tok_local, model_width).astype(jnp.bfloat16), hid_scores], axis=2
    )
    spread_rows = exchange(hid_sent, "hid", 2)
    input_sum = jnp.sum(spread_rows[..., :model_width].astype(jnp.float32), axis=0)
    own_scores = join3(spread_rows[..., model_width:], score_cols)
    own_scores = own_scores.reshape(spread_hid, tok_local, spread_exp, unit_count)
    unit_scores = jnp.transpose(own_scores, (1, 2, 0, 3)).reshape(tok_local, -1)
    expert_scores = jnp.sum(unit_scores.reshape(tok_local, expert_count, 2), axis=2)
    probs_all = softmax_rows(router_logits)
    mean_score = jnp.sum(probs_all * expert_scores, axis=1, keepdims=True)
    logit_grad = (probs_all * (expert_scores - mean_score)).astype(jnp.bfloat16)
    devices = spread_exp * spread_hid
    logit_all = lax.all_to_all(
        jnp.broadcast_to(logit_grad[None], (devices,) + logit_grad.shape), ("exp", "hid"), 0, 0, tiled=True
    ).reshape(-1, expert_count)
    grad_rows = model_width // devices
    token_cols = lax.dynamic_slice_in_dim(gathered, own_block * grad_rows, grad_rows, 1)
    router_grad = jnp.einsum("tc,te->ce", token_cols, logit_all, preferred_element_type=jnp.float32)
    router_part = jnp.einsum("te,de->td", logit_grad, router_w, preferred_element_type=jnp.float32)
    x_grad = (input_sum + router_part).astype(jnp.bfloat16)
    return (x_grad, router_grad)


def solution(mesh):
    placed = (
        P(("exp", "hid"), None),
        P(("exp", "hid"), None),
        P(("exp", "hid"), None),
        P(("exp", "hid"), None),
        P(),
        P(("exp", "hid"), None, None),
        P(("exp", "hid"), None, None),
        P(("exp", "hid"), None, None),
    )
    return jax.shard_map(
        on_device,
        mesh=mesh,
        in_specs=placed,
        out_specs=(P(("exp", "hid"), None), P(("exp", "hid"), None)),
        check_vma=False,
    )
```

```python
import functools
import jax
import jax.numpy as jnp
from jax import lax
from jax.sharding import PartitionSpec as P
from jax.experimental import pallas as pl
from jax.experimental.pallas import tpu as pltpu


def hid_gather_kernel(n, x_ref, out_ref, local_sem, send_sem, recv_sem):
    me = lax.axis_index("hid")
    row = lax.axis_index("exp")
    mesh_ids = pl.DeviceIdType.MESH
    barrier = pltpu.get_barrier_semaphore()
    for k in range(1, n):
        peer = lax.rem(me + k, n)
        pl.semaphore_signal(barrier, inc=1, device_id=(row, peer), device_id_type=mesh_ids)
    pl.semaphore_wait(barrier, n - 1)
    local = pltpu.make_async_copy(x_ref, out_ref.at[me], local_sem)
    local.start()
    copies = []
    for k in range(1, n):
        peer = lax.rem(me + k, n)
        copy = pltpu.make_async_remote_copy(
            src_ref=x_ref,
            dst_ref=out_ref.at[me],
            send_sem=send_sem.at[k],
            recv_sem=recv_sem.at[k],
            device_id=(row, peer),
            device_id_type=mesh_ids,
        )
        copy.start()
        copies.append(copy)
    local.wait()
    for copy in copies:
        copy.wait()


def exchange_kernel(axis, n, x_ref, out_ref, local_sem, send_sem, recv_sem):
    me = lax.axis_index(axis)
    own_exp = lax.axis_index("exp")
    own_hid = lax.axis_index("hid")
    mesh_ids = pl.DeviceIdType.MESH
    where = lambda peer: (peer, own_hid) if axis == "exp" else (own_exp, peer)
    barrier = pltpu.get_barrier_semaphore()
    for k in range(1, n):
        peer = lax.rem(me + k, n)
        pl.semaphore_signal(barrier, inc=1, device_id=where(peer), device_id_type=mesh_ids)
    pl.semaphore_wait(barrier, n - 1)
    local = pltpu.make_async_copy(x_ref.at[me], out_ref.at[me], local_sem)
    local.start()
    copies = []
    for k in range(1, n):
        peer = lax.rem(me + k, n)
        copy = pltpu.make_async_remote_copy(
            src_ref=x_ref.at[peer],
            dst_ref=out_ref.at[me],
            send_sem=send_sem.at[k],
            recv_sem=recv_sem.at[k],
            device_id=where(peer),
            device_id_type=mesh_ids,
        )
        copy.start()
        copies.append(copy)
    local.wait()
    for copy in copies:
        copy.wait()


def exchange(chunks, axis, kernel_id):
    n = chunks.shape[0]
    return pl.pallas_call(
        functools.partial(exchange_kernel, axis, n),
        out_shape=jax.ShapeDtypeStruct(chunks.shape, chunks.dtype),
        in_specs=[pl.BlockSpec(memory_space=pltpu.VMEM)],
        out_specs=pl.BlockSpec(memory_space=pltpu.VMEM),
        scratch_shapes=[
            pltpu.SemaphoreType.DMA,
            pltpu.SemaphoreType.DMA((n,)),
            pltpu.SemaphoreType.DMA((n,)),
        ],
        compiler_params=pltpu.CompilerParams(collective_id=kernel_id, has_side_effects=True),
    )(chunks)


def hid_gather(block):
    n = lax.axis_size("hid")
    return pl.pallas_call(
        functools.partial(hid_gather_kernel, n),
        out_shape=jax.ShapeDtypeStruct((n,) + block.shape, block.dtype),
        in_specs=[pl.BlockSpec(memory_space=pltpu.VMEM)],
        out_specs=pl.BlockSpec(memory_space=pltpu.VMEM),
        scratch_shapes=[
            pltpu.SemaphoreType.DMA,
            pltpu.SemaphoreType.DMA((n,)),
            pltpu.SemaphoreType.DMA((n,)),
        ],
        compiler_params=pltpu.CompilerParams(collective_id=0, has_side_effects=True),
    )(block).reshape((n * block.shape[0],) + block.shape[1:])


def softmax_rows(values):
    top_val = jnp.max(values, axis=-1, keepdims=True)
    raised = jnp.exp(values - top_val)
    return raised / jnp.sum(raised, axis=-1, keepdims=True)


def combine_table(logits, chosen, expert_count):
    picked = jnp.take_along_axis(logits, chosen, axis=1)
    weights = softmax_rows(picked)
    expert_ids = jnp.arange(expert_count, dtype=jnp.int32)
    matched = (chosen[:, :, None] == expert_ids[None, None, :]).astype(jnp.float32)
    return jnp.sum(weights[:, :, None] * matched, axis=1).astype(jnp.bfloat16)


CAP = 4


def slot_rows(column, group_rows):
    shaped = column.reshape(column.shape[:-1] + (-1, group_rows))
    place = jnp.arange(group_rows, dtype=jnp.int32)
    key = jnp.where(shaped != 0, 2 * group_rows - place, -place)
    return lax.top_k(key, CAP)[1]


def split3(value):
    hi = value.astype(jnp.bfloat16)
    rest = value - hi.astype(jnp.float32)
    mid = rest.astype(jnp.bfloat16)
    lo = (rest - mid.astype(jnp.float32)).astype(jnp.bfloat16)
    return jnp.concatenate([hi, mid, lo], axis=-1)


def join3(pieces, width):
    part = lambda i: pieces[..., i * width : (i + 1) * width].astype(jnp.float32)
    return (part(0) + part(1)) + part(2)


def dense_kernel(x_ref, g_ref, wg_ref, wu_ref, wd_ref, gate_ref, up_ref, back_ref, score_ref):
    x = x_ref[...]
    gate_pre = jnp.dot(x, wg_ref[...], preferred_element_type=jnp.float32)
    up_pre = jnp.dot(x, wu_ref[...], preferred_element_type=jnp.float32)
    back_grad = lax.dot_general(
        g_ref[...], wd_ref[...], (((1,), (1,)), ((), ())), preferred_element_type=jnp.float32
    )
    sig_gate = 1.0 / (1.0 + jnp.exp(-gate_pre))
    gate_ref[...] = gate_pre
    up_ref[...] = up_pre
    back_ref[...] = back_grad
    score_ref[...] = jnp.sum(gate_pre * sig_gate * up_pre * back_grad, axis=1, keepdims=True)


def dense_unit(gathered, gate_w, up_w, down_w, tile=256):
    tokens_n = gathered.shape[0]
    width, hidden = gate_w.shape
    rows = lambda i: (i, 0)
    fixed = lambda i: (0, 0)
    f32 = jnp.float32
    return pl.pallas_call(
        dense_kernel,
        grid=(tokens_n // tile,),
        out_shape=[
            jax.ShapeDtypeStruct((tokens_n, hidden), f32),
            jax.ShapeDtypeStruct((tokens_n, hidden), f32),
            jax.ShapeDtypeStruct((tokens_n, hidden), f32),
            jax.ShapeDtypeStruct((tokens_n, 1), f32),
        ],
        in_specs=[
            pl.BlockSpec((tile, width), rows),
            pl.BlockSpec((tile, width), lambda i: (i, 1)),
            pl.BlockSpec((width, hidden), fixed),
            pl.BlockSpec((width, hidden), fixed),
            pl.BlockSpec((hidden, width), fixed),
        ],
        out_specs=[
            pl.BlockSpec((tile, hidden), rows),
            pl.BlockSpec((tile, hidden), rows),
            pl.BlockSpec((tile, hidden), rows),
            pl.BlockSpec((tile, 1), rows),
        ],
    )(gathered, gathered, gate_w, up_w, down_w)


def sparse_terms(gate_pre, up_pre, back_grad, column, w_gate, w_up, group_rows):
    picked = slot_rows(column, group_rows)
    groups = picked.shape[1]
    starts = (jnp.arange(groups, dtype=jnp.int32) * group_rows)[None, :, None]
    rows = (picked + starts).reshape(picked.shape[0], -1)
    take = lambda a: jnp.take_along_axis(a, rows[:, :, None], axis=1)
    gate_s, up_s, back_s = take(gate_pre), take(up_pre), take(back_grad)
    col_s = jnp.take_along_axis(column, rows, axis=1)
    sig_gate = jax.nn.sigmoid(gate_s)
    act_gate = gate_s * sig_gate
    weighted = col_s[:, :, None] * back_s
    grad_gate = (weighted * up_s * sig_gate * (1.0 + gate_s * (1.0 - sig_gate))).astype(jnp.bfloat16)
    grad_up = (weighted * act_gate).astype(jnp.bfloat16)
    part = jnp.einsum("usf,udf->usd", grad_gate, w_gate, preferred_element_type=jnp.float32)
    part = part + jnp.einsum("usf,udf->usd", grad_up, w_up, preferred_element_type=jnp.float32)
    return part.reshape(part.shape[0], groups, CAP, part.shape[-1])


def on_device(tokens, grad_out, router_logits, selected, router_w, w_gate, w_up, w_down):
    tok_local, model_width = tokens.shape
    unit_count = w_gate.shape[0]
    expert_count = router_logits.shape[1]
    spread_exp = lax.axis_size("exp")
    spread_hid = lax.axis_size("hid")
    group_rows = spread_hid * tok_local
    own_exp = lax.axis_index("exp")
    own_hid = lax.axis_index("hid")
    own_block = lax.axis_index(("exp", "hid"))
    unit_expert = (own_block * unit_count + jnp.arange(unit_count, dtype=jnp.int32)) // 2
    expert_ids = jnp.arange(expert_count, dtype=jnp.int32)
    unit_pick = (expert_ids[:, None] == unit_expert[None, :]).astype(jnp.bfloat16)
    combine = combine_table(router_logits, selected, expert_count)
    packed = jnp.concatenate([tokens, grad_out, combine], axis=1)
    gathered = lax.all_gather(hid_gather(packed), "exp", axis=0, tiled=True)
    combine_all = gathered[:, 2 * model_width :]
    dense = [dense_unit(gathered, w_gate[i], w_up[i], w_down[i]) for i in range(unit_count)]
    gate_pre, up_pre, back_grad = (jnp.stack([d[j] for d in dense]) for j in range(3))
    score_part = jnp.concatenate([d[3] for d in dense], axis=1)
    column = jnp.dot(combine_all, unit_pick, preferred_element_type=jnp.float32).T
    part = sparse_terms(gate_pre, up_pre, back_grad, column, w_gate, w_up, group_rows)
    lane = 128
    score_grp = jnp.swapaxes(score_part.T.reshape(unit_count, spread_exp, CAP, group_rows // CAP), 0, 1)
    score_grp = split3(score_grp)
    score_grp = jnp.pad(score_grp, ((0, 0), (0, 0), (0, 0), (0, lane - score_grp.shape[3])))
    sent = jnp.concatenate([jnp.swapaxes(part, 0, 1).astype(jnp.bfloat16), score_grp], axis=3)
    arrived_part = exchange(sent, "exp", 1)
    sender_block = (jnp.arange(spread_exp, dtype=jnp.int32) * spread_hid + own_hid)[:, None]
    sender_expert = (sender_block * unit_count + jnp.arange(unit_count, dtype=jnp.int32)[None, :]) // 2
    own_combine = lax.dynamic_slice_in_dim(combine_all, own_exp * group_rows, group_rows, 0)
    sender_pick = (expert_ids[:, None] == sender_expert.reshape(1, -1)).astype(jnp.bfloat16)
    sender_column = jnp.dot(own_combine, sender_pick, preferred_element_type=jnp.float32).T
    sender_rows = slot_rows(sender_column, group_rows).reshape(-1)
    place = (sender_rows[:, None] == jnp.arange(group_rows, dtype=jnp.int32)[None, :]).astype(jnp.bfloat16)
    group_sum = jnp.einsum(
        "sj,sd->jd", place, arrived_part[..., :model_width].reshape(-1, model_width),
        preferred_element_type=jnp.float32,
    )
    got_scores = join3(arrived_part[..., model_width:], group_rows // CAP)
    got_scores = got_scores.reshape(spread_exp, unit_count, spread_hid, tok_local)
    score_cols = spread_exp * unit_count
    hid_scores = jnp.transpose(got_scores, (2, 3, 0, 1)).reshape(spread_hid, tok_local, score_cols)
    hid_scores = split3(hid_scores)
    score_width = -(-hid_scores.shape[2] // lane) * lane
    hid_scores = jnp.pad(hid_scores, ((0, 0), (0, 0), (0, score_width - hid_scores.shape[2])))
    hid_sent = jnp.concatenate(
        [group_sum.reshape(spread_hid, tok_local, model_width).astype(jnp.bfloat16), hid_scores], axis=2
    )
    spread_rows = exchange(hid_sent, "hid", 2)
    input_sum = jnp.sum(spread_rows[..., :model_width].astype(jnp.float32), axis=0)
    own_scores = join3(spread_rows[..., model_width:], score_cols)
    own_scores = own_scores.reshape(spread_hid, tok_local, spread_exp, unit_count)
    unit_scores = jnp.transpose(own_scores, (1, 2, 0, 3)).reshape(tok_local, -1)
    expert_scores = jnp.sum(unit_scores.reshape(tok_local, expert_count, 2), axis=2)
    probs_all = softmax_rows(router_logits)
    mean_score = jnp.sum(probs_all * expert_scores, axis=1, keepdims=True)
    logit_grad = (probs_all * (expert_scores - mean_score)).astype(jnp.bfloat16)
    devices = spread_exp * spread_hid
    logit_all = lax.all_to_all(
        jnp.broadcast_to(logit_grad[None], (devices,) + logit_grad.shape), ("exp", "hid"), 0, 0, tiled=True
    ).reshape(-1, expert_count)
    grad_rows = model_width // devices
    token_cols = lax.dynamic_slice_in_dim(gathered, own_block * grad_rows, grad_rows, 1)
    router_grad = jnp.einsum("tc,te->ce", token_cols, logit_all, preferred_element_type=jnp.float32)
    router_part = jnp.einsum("te,de->td", logit_grad, router_w, preferred_element_type=jnp.float32)
    x_grad = (input_sum + router_part).astype(jnp.bfloat16)
    return (x_grad, router_grad)


def solution(mesh):
    placed = (
        P(("exp", "hid"), None),
        P(("exp", "hid"), None),
        P(("exp", "hid"), None),
        P(("exp", "hid"), None),
        P(),
        P(("exp", "hid"), None, None),
        P(("exp", "hid"), None, None),
        P(("exp", "hid"), None, None),
    )
    return jax.shard_map(
        on_device,
        mesh=mesh,
        in_specs=placed,
        out_specs=(P(("exp", "hid"), None), P(("exp", "hid"), None)),
        check_vma=False,
    )
```

```python
import functools
import jax
import jax.numpy as jnp
from jax import lax
from jax.sharding import PartitionSpec as P
from jax.experimental import pallas as pl
from jax.experimental.pallas import tpu as pltpu


def hid_gather_kernel(n, x_ref, out_ref, local_sem, send_sem, recv_sem):
    me = lax.axis_index("hid")
    row = lax.axis_index("exp")
    mesh_ids = pl.DeviceIdType.MESH
    barrier = pltpu.get_barrier_semaphore()
    for k in range(1, n):
        peer = lax.rem(me + k, n)
        pl.semaphore_signal(barrier, inc=1, device_id=(row, peer), device_id_type=mesh_ids)
    pl.semaphore_wait(barrier, n - 1)
    local = pltpu.make_async_copy(x_ref, out_ref.at[me], local_sem)
    local.start()
    copies = []
    for k in range(1, n):
        peer = lax.rem(me + k, n)
        copy = pltpu.make_async_remote_copy(
            src_ref=x_ref,
            dst_ref=out_ref.at[me],
            send_sem=send_sem.at[k],
            recv_sem=recv_sem.at[k],
            device_id=(row, peer),
            device_id_type=mesh_ids,
        )
        copy.start()
        copies.append(copy)
    local.wait()
    for copy in copies:
        copy.wait()


def exchange_kernel(axis, n, x_ref, out_ref, local_sem, send_sem, recv_sem):
    me = lax.axis_index(axis)
    own_exp = lax.axis_index("exp")
    own_hid = lax.axis_index("hid")
    mesh_ids = pl.DeviceIdType.MESH
    where = lambda peer: (peer, own_hid) if axis == "exp" else (own_exp, peer)
    barrier = pltpu.get_barrier_semaphore()
    for k in range(1, n):
        peer = lax.rem(me + k, n)
        pl.semaphore_signal(barrier, inc=1, device_id=where(peer), device_id_type=mesh_ids)
    pl.semaphore_wait(barrier, n - 1)
    local = pltpu.make_async_copy(x_ref.at[me], out_ref.at[me], local_sem)
    local.start()
    copies = []
    for k in range(1, n):
        peer = lax.rem(me + k, n)
        copy = pltpu.make_async_remote_copy(
            src_ref=x_ref.at[peer],
            dst_ref=out_ref.at[me],
            send_sem=send_sem.at[k],
            recv_sem=recv_sem.at[k],
            device_id=where(peer),
            device_id_type=mesh_ids,
        )
        copy.start()
        copies.append(copy)
    local.wait()
    for copy in copies:
        copy.wait()


def exchange(chunks, axis, kernel_id):
    n = chunks.shape[0]
    return pl.pallas_call(
        functools.partial(exchange_kernel, axis, n),
        out_shape=jax.ShapeDtypeStruct(chunks.shape, chunks.dtype),
        in_specs=[pl.BlockSpec(memory_space=pltpu.VMEM)],
        out_specs=pl.BlockSpec(memory_space=pltpu.VMEM),
        scratch_shapes=[
            pltpu.SemaphoreType.DMA,
            pltpu.SemaphoreType.DMA((n,)),
            pltpu.SemaphoreType.DMA((n,)),
        ],
        compiler_params=pltpu.CompilerParams(collective_id=kernel_id, has_side_effects=True),
    )(chunks)


def hid_gather(block):
    n = lax.axis_size("hid")
    return pl.pallas_call(
        functools.partial(hid_gather_kernel, n),
        out_shape=jax.ShapeDtypeStruct((n,) + block.shape, block.dtype),
        in_specs=[pl.BlockSpec(memory_space=pltpu.VMEM)],
        out_specs=pl.BlockSpec(memory_space=pltpu.VMEM),
        scratch_shapes=[
            pltpu.SemaphoreType.DMA,
            pltpu.SemaphoreType.DMA((n,)),
            pltpu.SemaphoreType.DMA((n,)),
        ],
        compiler_params=pltpu.CompilerParams(collective_id=0, has_side_effects=True),
    )(block).reshape((n * block.shape[0],) + block.shape[1:])


def softmax_rows(values):
    top_val = jnp.max(values, axis=-1, keepdims=True)
    raised = jnp.exp(values - top_val)
    return raised / jnp.sum(raised, axis=-1, keepdims=True)


def combine_table(logits, chosen, expert_count):
    picked = jnp.take_along_axis(logits, chosen, axis=1)
    weights = softmax_rows(picked)
    expert_ids = jnp.arange(expert_count, dtype=jnp.int32)
    matched = (chosen[:, :, None] == expert_ids[None, None, :]).astype(jnp.float32)
    return jnp.sum(weights[:, :, None] * matched, axis=1).astype(jnp.bfloat16)


CAP = 4


def slot_rows(column, group_rows):
    shaped = column.reshape(column.shape[:-1] + (-1, group_rows))
    place = jnp.arange(group_rows, dtype=jnp.int32)
    key = jnp.where(shaped != 0, 2 * group_rows - place, -place)
    return lax.top_k(key, CAP)[1]


def split3(value):
    hi = value.astype(jnp.bfloat16)
    rest = value - hi.astype(jnp.float32)
    mid = rest.astype(jnp.bfloat16)
    lo = (rest - mid.astype(jnp.float32)).astype(jnp.bfloat16)
    return jnp.concatenate([hi, mid, lo], axis=-1)


def join3(pieces, width):
    part = lambda i: pieces[..., i * width : (i + 1) * width].astype(jnp.float32)
    return (part(0) + part(1)) + part(2)


def dense_kernel(x_ref, g_ref, wg_ref, wu_ref, wd_ref, score_ref):
    x = x_ref[...]
    gate_pre = jnp.dot(x, wg_ref[...], preferred_element_type=jnp.float32)
    up_pre = jnp.dot(x, wu_ref[...], preferred_element_type=jnp.float32)
    back_grad = lax.dot_general(
        g_ref[...], wd_ref[...], (((1,), (1,)), ((), ())), preferred_element_type=jnp.float32
    )
    sig_gate = 1.0 / (1.0 + jnp.exp(-gate_pre))
    score_ref[...] = jnp.sum(gate_pre * sig_gate * up_pre * back_grad, axis=1, keepdims=True)


def dense_unit(gathered, gate_w, up_w, down_w, tile=256):
    tokens_n = gathered.shape[0]
    width, hidden = gate_w.shape
    rows = lambda i: (i, 0)
    fixed = lambda i: (0, 0)
    f32 = jnp.float32
    return pl.pallas_call(
        dense_kernel,
        grid=(tokens_n // tile,),
        out_shape=jax.ShapeDtypeStruct((tokens_n, 1), f32),
        in_specs=[
            pl.BlockSpec((tile, width), rows),
            pl.BlockSpec((tile, width), lambda i: (i, 1)),
            pl.BlockSpec((width, hidden), fixed),
            pl.BlockSpec((width, hidden), fixed),
            pl.BlockSpec((hidden, width), fixed),
        ],
        out_specs=pl.BlockSpec((tile, 1), rows),
    )(gathered, gathered, gate_w, up_w, down_w)


def sparse_terms(x_rows, g_rows, column, w_gate, w_up, w_down, group_rows):
    picked = slot_rows(column, group_rows)
    groups = picked.shape[1]
    starts = (jnp.arange(groups, dtype=jnp.int32) * group_rows)[None, :, None]
    rows = (picked + starts).reshape(picked.shape[0], -1)
    x_s, g_s = jnp.take(x_rows, rows, axis=0), jnp.take(g_rows, rows, axis=0)
    gate_s = jnp.einsum("usd,udf->usf", x_s, w_gate, preferred_element_type=jnp.float32)
    up_s = jnp.einsum("usd,udf->usf", x_s, w_up, preferred_element_type=jnp.float32)
    back_s = jnp.einsum("usd,ufd->usf", g_s, w_down, preferred_element_type=jnp.float32)
    col_s = jnp.take_along_axis(column, rows, axis=1)
    sig_gate = jax.nn.sigmoid(gate_s)
    act_gate = gate_s * sig_gate
    weighted = col_s[:, :, None] * back_s
    grad_gate = (weighted * up_s * sig_gate * (1.0 + gate_s * (1.0 - sig_gate))).astype(jnp.bfloat16)
    grad_up = (weighted * act_gate).astype(jnp.bfloat16)
    part = jnp.einsum("usf,udf->usd", grad_gate, w_gate, preferred_element_type=jnp.float32)
    part = part + jnp.einsum("usf,udf->usd", grad_up, w_up, preferred_element_type=jnp.float32)
    return part.reshape(part.shape[0], groups, CAP, part.shape[-1])


def on_device(tokens, grad_out, router_logits, selected, router_w, w_gate, w_up, w_down):
    tok_local, model_width = tokens.shape
    unit_count = w_gate.shape[0]
    expert_count = router_logits.shape[1]
    spread_exp = lax.axis_size("exp")
    spread_hid = lax.axis_size("hid")
    group_rows = spread_hid * tok_local
    own_exp = lax.axis_index("exp")
    own_hid = lax.axis_index("hid")
    own_block = lax.axis_index(("exp", "hid"))
    unit_expert = (own_block * unit_count + jnp.arange(unit_count, dtype=jnp.int32)) // 2
    expert_ids = jnp.arange(expert_count, dtype=jnp.int32)
    unit_pick = (expert_ids[:, None] == unit_expert[None, :]).astype(jnp.bfloat16)
    combine = combine_table(router_logits, selected, expert_count)
    packed = jnp.concatenate([tokens, grad_out, combine], axis=1)
    gathered = lax.all_gather(hid_gather(packed), "exp", axis=0, tiled=True)
    combine_all = gathered[:, 2 * model_width :]
    dense = [dense_unit(gathered, w_gate[i], w_up[i], w_down[i]) for i in range(unit_count)]
    score_part = jnp.concatenate(dense, axis=1)
    column = jnp.dot(combine_all, unit_pick, preferred_element_type=jnp.float32).T
    part = sparse_terms(
        gathered[:, :model_width], gathered[:, model_width : 2 * model_width], column, w_gate, w_up, w_down,
        group_rows,
    )
    lane = 128
    score_grp = jnp.swapaxes(score_part.T.reshape(unit_count, spread_exp, CAP, group_rows // CAP), 0, 1)
    score_grp = split3(score_grp)
    score_grp = jnp.pad(score_grp, ((0, 0), (0, 0), (0, 0), (0, lane - score_grp.shape[3])))
    sent = jnp.concatenate([jnp.swapaxes(part, 0, 1).astype(jnp.bfloat16), score_grp], axis=3)
    arrived_part = exchange(sent, "exp", 1)
    sender_block = (jnp.arange(spread_exp, dtype=jnp.int32) * spread_hid + own_hid)[:, None]
    sender_expert = (sender_block * unit_count + jnp.arange(unit_count, dtype=jnp.int32)[None, :]) // 2
    own_combine = lax.dynamic_slice_in_dim(combine_all, own_exp * group_rows, group_rows, 0)
    sender_pick = (expert_ids[:, None] == sender_expert.reshape(1, -1)).astype(jnp.bfloat16)
    sender_column = jnp.dot(own_combine, sender_pick, preferred_element_type=jnp.float32).T
    sender_rows = slot_rows(sender_column, group_rows).reshape(-1)
    place = (sender_rows[:, None] == jnp.arange(group_rows, dtype=jnp.int32)[None, :]).astype(jnp.bfloat16)
    group_sum = jnp.einsum(
        "sj,sd->jd", place, arrived_part[..., :model_width].reshape(-1, model_width),
        preferred_element_type=jnp.float32,
    )
    got_scores = join3(arrived_part[..., model_width:], group_rows // CAP)
    got_scores = got_scores.reshape(spread_exp, unit_count, spread_hid, tok_local)
    score_cols = spread_exp * unit_count
    hid_scores = jnp.transpose(got_scores, (2, 3, 0, 1)).reshape(spread_hid, tok_local, score_cols)
    hid_scores = split3(hid_scores)
    score_width = -(-hid_scores.shape[2] // lane) * lane
    hid_scores = jnp.pad(hid_scores, ((0, 0), (0, 0), (0, score_width - hid_scores.shape[2])))
    hid_sent = jnp.concatenate(
        [group_sum.reshape(spread_hid, tok_local, model_width).astype(jnp.bfloat16), hid_scores], axis=2
    )
    spread_rows = exchange(hid_sent, "hid", 2)
    input_sum = jnp.sum(spread_rows[..., :model_width].astype(jnp.float32), axis=0)
    own_scores = join3(spread_rows[..., model_width:], score_cols)
    own_scores = own_scores.reshape(spread_hid, tok_local, spread_exp, unit_count)
    unit_scores = jnp.transpose(own_scores, (1, 2, 0, 3)).reshape(tok_local, -1)
    expert_scores = jnp.sum(unit_scores.reshape(tok_local, expert_count, 2), axis=2)
    probs_all = softmax_rows(router_logits)
    mean_score = jnp.sum(probs_all * expert_scores, axis=1, keepdims=True)
    logit_grad = (probs_all * (expert_scores - mean_score)).astype(jnp.bfloat16)
    devices = spread_exp * spread_hid
    logit_all = lax.all_to_all(
        jnp.broadcast_to(logit_grad[None], (devices,) + logit_grad.shape), ("exp", "hid"), 0, 0, tiled=True
    ).reshape(-1, expert_count)
    grad_rows = model_width // devices
    token_cols = lax.dynamic_slice_in_dim(gathered, own_block * grad_rows, grad_rows, 1)
    router_grad = jnp.einsum("tc,te->ce", token_cols, logit_all, preferred_element_type=jnp.float32)
    router_part = jnp.einsum("te,de->td", logit_grad, router_w, preferred_element_type=jnp.float32)
    x_grad = (input_sum + router_part).astype(jnp.bfloat16)
    return (x_grad, router_grad)


def solution(mesh):
    placed = (
        P(("exp", "hid"), None),
        P(("exp", "hid"), None),
        P(("exp", "hid"), None),
        P(("exp", "hid"), None),
        P(),
        P(("exp", "hid"), None, None),
        P(("exp", "hid"), None, None),
        P(("exp", "hid"), None, None),
    )
    return jax.shard_map(
        on_device,
        mesh=mesh,
        in_specs=placed,
        out_specs=(P(("exp", "hid"), None), P(("exp", "hid"), None)),
        check_vma=False,
    )
```

```python
import functools
import jax
import jax.numpy as jnp
from jax import lax
from jax.sharding import PartitionSpec as P
from jax.experimental import pallas as pl
from jax.experimental.pallas import tpu as pltpu


def hid_gather_kernel(n, x_ref, out_ref, local_sem, send_sem, recv_sem):
    me = lax.axis_index("hid")
    row = lax.axis_index("exp")
    mesh_ids = pl.DeviceIdType.MESH
    barrier = pltpu.get_barrier_semaphore()
    for k in range(1, n):
        peer = lax.rem(me + k, n)
        pl.semaphore_signal(barrier, inc=1, device_id=(row, peer), device_id_type=mesh_ids)
    pl.semaphore_wait(barrier, n - 1)
    local = pltpu.make_async_copy(x_ref, out_ref.at[me], local_sem)
    local.start()
    copies = []
    for k in range(1, n):
        peer = lax.rem(me + k, n)
        copy = pltpu.make_async_remote_copy(
            src_ref=x_ref,
            dst_ref=out_ref.at[me],
            send_sem=send_sem.at[k],
            recv_sem=recv_sem.at[k],
            device_id=(row, peer),
            device_id_type=mesh_ids,
        )
        copy.start()
        copies.append(copy)
    local.wait()
    for copy in copies:
        copy.wait()


def exchange_kernel(n, spot, where, x_ref, out_ref, local_sem, send_sem, recv_sem):
    me = spot()
    mesh_ids = pl.DeviceIdType.MESH
    barrier = pltpu.get_barrier_semaphore()
    for k in range(1, n):
        peer = lax.rem(me + k, n)
        pl.semaphore_signal(barrier, inc=1, device_id=where(peer), device_id_type=mesh_ids)
    pl.semaphore_wait(barrier, n - 1)
    local = pltpu.make_async_copy(x_ref.at[me], out_ref.at[me], local_sem)
    local.start()
    copies = []
    for k in range(1, n):
        peer = lax.rem(me + k, n)
        copy = pltpu.make_async_remote_copy(
            src_ref=x_ref.at[peer],
            dst_ref=out_ref.at[me],
            send_sem=send_sem.at[k],
            recv_sem=recv_sem.at[k],
            device_id=where(peer),
            device_id_type=mesh_ids,
        )
        copy.start()
        copies.append(copy)
    local.wait()
    for copy in copies:
        copy.wait()


def exchange(chunks, spot, where, kernel_id):
    n = chunks.shape[0]
    return pl.pallas_call(
        functools.partial(exchange_kernel, n, spot, where),
        out_shape=jax.ShapeDtypeStruct(chunks.shape, chunks.dtype),
        in_specs=[pl.BlockSpec(memory_space=pltpu.VMEM)],
        out_specs=pl.BlockSpec(memory_space=pltpu.VMEM),
        scratch_shapes=[
            pltpu.SemaphoreType.DMA,
            pltpu.SemaphoreType.DMA((n,)),
            pltpu.SemaphoreType.DMA((n,)),
        ],
        compiler_params=pltpu.CompilerParams(collective_id=kernel_id, has_side_effects=True),
    )(chunks)


def exp_exchange(sent):
    exp_at = lambda: lax.axis_index("exp")
    hid_at = lambda: lax.axis_index("hid")
    chips = sent.shape[0] // 2
    across = exchange(
        sent.reshape((chips, 2) + sent.shape[1:]),
        lambda: exp_at() // 2,
        lambda p: (p * 2 + exp_at() % 2, hid_at()),
        1,
    )
    within = exchange(
        jnp.swapaxes(across, 0, 1),
        lambda: exp_at() % 2,
        lambda p: ((exp_at() // 2) * 2 + p, hid_at()),
        3,
    )
    return jnp.swapaxes(within, 0, 1).reshape(sent.shape)


def hid_exchange(sent):
    return exchange(
        sent, lambda: lax.axis_index("hid"), lambda p: (lax.axis_index("exp"), p), 2
    )


def hid_gather(block):
    n = lax.axis_size("hid")
    return pl.pallas_call(
        functools.partial(hid_gather_kernel, n),
        out_shape=jax.ShapeDtypeStruct((n,) + block.shape, block.dtype),
        in_specs=[pl.BlockSpec(memory_space=pltpu.VMEM)],
        out_specs=pl.BlockSpec(memory_space=pltpu.VMEM),
        scratch_shapes=[
            pltpu.SemaphoreType.DMA,
            pltpu.SemaphoreType.DMA((n,)),
            pltpu.SemaphoreType.DMA((n,)),
        ],
        compiler_params=pltpu.CompilerParams(collective_id=0, has_side_effects=True),
    )(block).reshape((n * block.shape[0],) + block.shape[1:])


def softmax_rows(values):
    top_val = jnp.max(values, axis=-1, keepdims=True)
    raised = jnp.exp(values - top_val)
    return raised / jnp.sum(raised, axis=-1, keepdims=True)


def combine_table(logits, chosen, expert_count):
    picked = jnp.take_along_axis(logits, chosen, axis=1)
    weights = softmax_rows(picked)
    expert_ids = jnp.arange(expert_count, dtype=jnp.int32)
    matched = (chosen[:, :, None] == expert_ids[None, None, :]).astype(jnp.float32)
    return jnp.sum(weights[:, :, None] * matched, axis=1).astype(jnp.bfloat16)


CAP = 4


def slot_rows(column, group_rows):
    shaped = column.reshape(column.shape[:-1] + (-1, group_rows))
    place = jnp.arange(group_rows, dtype=jnp.int32)
    key = jnp.where(shaped != 0, 2 * group_rows - place, -place)
    return lax.top_k(key, CAP)[1]


def split3(value):
    hi = value.astype(jnp.bfloat16)
    rest = value - hi.astype(jnp.float32)
    mid = rest.astype(jnp.bfloat16)
    lo = (rest - mid.astype(jnp.float32)).astype(jnp.bfloat16)
    return jnp.concatenate([hi, mid, lo], axis=-1)


def join3(pieces, width):
    part = lambda i: pieces[..., i * width : (i + 1) * width].astype(jnp.float32)
    return (part(0) + part(1)) + part(2)


def dense_kernel(x_ref, g_ref, wg_ref, wu_ref, wd_ref, gate_ref, up_ref, back_ref, score_ref):
    x = x_ref[...]
    gate_pre = jnp.dot(x, wg_ref[...], preferred_element_type=jnp.float32)
    up_pre = jnp.dot(x, wu_ref[...], preferred_element_type=jnp.float32)
    back_grad = lax.dot_general(
        g_ref[...], wd_ref[...], (((1,), (1,)), ((), ())), preferred_element_type=jnp.float32
    )
    sig_gate = 1.0 / (1.0 + jnp.exp(-gate_pre))
    gate_ref[...] = gate_pre
    up_ref[...] = up_pre
    back_ref[...] = back_grad
    score_ref[...] = jnp.sum(gate_pre * sig_gate * up_pre * back_grad, axis=1, keepdims=True)


def dense_unit(gathered, gate_w, up_w, down_w, tile=256):
    tokens_n = gathered.shape[0]
    width, hidden = gate_w.shape
    rows = lambda i: (i, 0)
    fixed = lambda i: (0, 0)
    f32 = jnp.float32
    return pl.pallas_call(
        dense_kernel,
        grid=(tokens_n // tile,),
        out_shape=[
            jax.ShapeDtypeStruct((tokens_n, hidden), f32),
            jax.ShapeDtypeStruct((tokens_n, hidden), f32),
            jax.ShapeDtypeStruct((tokens_n, hidden), f32),
            jax.ShapeDtypeStruct((tokens_n, 1), f32),
        ],
        in_specs=[
            pl.BlockSpec((tile, width), rows),
            pl.BlockSpec((tile, width), lambda i: (i, 1)),
            pl.BlockSpec((width, hidden), fixed),
            pl.BlockSpec((width, hidden), fixed),
            pl.BlockSpec((hidden, width), fixed),
        ],
        out_specs=[
            pl.BlockSpec((tile, hidden), rows),
            pl.BlockSpec((tile, hidden), rows),
            pl.BlockSpec((tile, hidden), rows),
            pl.BlockSpec((tile, 1), rows),
        ],
    )(gathered, gathered, gate_w, up_w, down_w)


def sparse_terms(gate_pre, up_pre, back_grad, column, w_gate, w_up, group_rows):
    picked = slot_rows(column, group_rows)
    groups = picked.shape[1]
    starts = (jnp.arange(groups, dtype=jnp.int32) * group_rows)[None, :, None]
    rows = (picked + starts).reshape(picked.shape[0], -1)
    take = lambda a: jnp.take_along_axis(a, rows[:, :, None], axis=1)
    gate_s, up_s, back_s = take(gate_pre), take(up_pre), take(back_grad)
    col_s = jnp.take_along_axis(column, rows, axis=1)
    sig_gate = jax.nn.sigmoid(gate_s)
    act_gate = gate_s * sig_gate
    weighted = col_s[:, :, None] * back_s
    grad_gate = (weighted * up_s * sig_gate * (1.0 + gate_s * (1.0 - sig_gate))).astype(jnp.bfloat16)
    grad_up = (weighted * act_gate).astype(jnp.bfloat16)
    part = jnp.einsum("usf,udf->usd", grad_gate, w_gate, preferred_element_type=jnp.float32)
    part = part + jnp.einsum("usf,udf->usd", grad_up, w_up, preferred_element_type=jnp.float32)
    return part.reshape(part.shape[0], groups, CAP, part.shape[-1])


def on_device(tokens, grad_out, router_logits, selected, router_w, w_gate, w_up, w_down):
    tok_local, model_width = tokens.shape
    unit_count = w_gate.shape[0]
    expert_count = router_logits.shape[1]
    spread_exp = lax.axis_size("exp")
    spread_hid = lax.axis_size("hid")
    group_rows = spread_hid * tok_local
    own_exp = lax.axis_index("exp")
    own_hid = lax.axis_index("hid")
    own_block = lax.axis_index(("exp", "hid"))
    unit_expert = (own_block * unit_count + jnp.arange(unit_count, dtype=jnp.int32)) // 2
    expert_ids = jnp.arange(expert_count, dtype=jnp.int32)
    unit_pick = (expert_ids[:, None] == unit_expert[None, :]).astype(jnp.bfloat16)
    combine = combine_table(router_logits, selected, expert_count)
    packed = jnp.concatenate([tokens, grad_out, combine], axis=1)
    gathered = lax.all_gather(hid_gather(packed), "exp", axis=0, tiled=True)
    combine_all = gathered[:, 2 * model_width :]
    dense = [dense_unit(gathered, w_gate[i], w_up[i], w_down[i]) for i in range(unit_count)]
    gate_pre, up_pre, back_grad = (jnp.stack([d[j] for d in dense]) for j in range(3))
    score_part = jnp.concatenate([d[3] for d in dense], axis=1)
    column = jnp.dot(combine_all, unit_pick, preferred_element_type=jnp.float32).T
    part = sparse_terms(gate_pre, up_pre, back_grad, column, w_gate, w_up, group_rows)
    lane = 128
    score_grp = jnp.swapaxes(score_part.T.reshape(unit_count, spread_exp, CAP, group_rows // CAP), 0, 1)
    score_grp = split3(score_grp)
    score_grp = jnp.pad(score_grp, ((0, 0), (0, 0), (0, 0), (0, lane - score_grp.shape[3])))
    sent = jnp.concatenate([jnp.swapaxes(part, 0, 1).astype(jnp.bfloat16), score_grp], axis=3)
    arrived_part = exp_exchange(sent)
    sender_block = (jnp.arange(spread_exp, dtype=jnp.int32) * spread_hid + own_hid)[:, None]
    sender_expert = (sender_block * unit_count + jnp.arange(unit_count, dtype=jnp.int32)[None, :]) // 2
    own_combine = lax.dynamic_slice_in_dim(combine_all, own_exp * group_rows, group_rows, 0)
    sender_pick = (expert_ids[:, None] == sender_expert.reshape(1, -1)).astype(jnp.bfloat16)
    sender_column = jnp.dot(own_combine, sender_pick, preferred_element_type=jnp.float32).T
    sender_rows = slot_rows(sender_column, group_rows).reshape(-1)
    place = (sender_rows[:, None] == jnp.arange(group_rows, dtype=jnp.int32)[None, :]).astype(jnp.bfloat16)
    group_sum = jnp.einsum(
        "sj,sd->jd", place, arrived_part[..., :model_width].reshape(-1, model_width),
        preferred_element_type=jnp.float32,
    )
    got_scores = join3(arrived_part[..., model_width:], group_rows // CAP)
    got_scores = got_scores.reshape(spread_exp, unit_count, spread_hid, tok_local)
    score_cols = spread_exp * unit_count
    hid_scores = jnp.transpose(got_scores, (2, 3, 0, 1)).reshape(spread_hid, tok_local, score_cols)
    hid_scores = split3(hid_scores)
    score_width = -(-hid_scores.shape[2] // lane) * lane
    hid_scores = jnp.pad(hid_scores, ((0, 0), (0, 0), (0, score_width - hid_scores.shape[2])))
    hid_sent = jnp.concatenate(
        [group_sum.reshape(spread_hid, tok_local, model_width).astype(jnp.bfloat16), hid_scores], axis=2
    )
    spread_rows = hid_exchange(hid_sent)
    input_sum = jnp.sum(spread_rows[..., :model_width].astype(jnp.float32), axis=0)
    own_scores = join3(spread_rows[..., model_width:], score_cols)
    own_scores = own_scores.reshape(spread_hid, tok_local, spread_exp, unit_count)
    unit_scores = jnp.transpose(own_scores, (1, 2, 0, 3)).reshape(tok_local, -1)
    expert_scores = jnp.sum(unit_scores.reshape(tok_local, expert_count, 2), axis=2)
    probs_all = softmax_rows(router_logits)
    mean_score = jnp.sum(probs_all * expert_scores, axis=1, keepdims=True)
    logit_grad = (probs_all * (expert_scores - mean_score)).astype(jnp.bfloat16)
    devices = spread_exp * spread_hid
    logit_all = lax.all_to_all(
        jnp.broadcast_to(logit_grad[None], (devices,) + logit_grad.shape), ("exp", "hid"), 0, 0, tiled=True
    ).reshape(-1, expert_count)
    grad_rows = model_width // devices
    token_cols = lax.dynamic_slice_in_dim(gathered, own_block * grad_rows, grad_rows, 1)
    router_grad = jnp.einsum("tc,te->ce", token_cols, logit_all, preferred_element_type=jnp.float32)
    router_part = jnp.einsum("te,de->td", logit_grad, router_w, preferred_element_type=jnp.float32)
    x_grad = (input_sum + router_part).astype(jnp.bfloat16)
    return (x_grad, router_grad)


def solution(mesh):
    placed = (
        P(("exp", "hid"), None),
        P(("exp", "hid"), None),
        P(("exp", "hid"), None),
        P(("exp", "hid"), None),
        P(),
        P(("exp", "hid"), None, None),
        P(("exp", "hid"), None, None),
        P(("exp", "hid"), None, None),
    )
    return jax.shard_map(
        on_device,
        mesh=mesh,
        in_specs=placed,
        out_specs=(P(("exp", "hid"), None), P(("exp", "hid"), None)),
        check_vma=False,
    )
```

```python
import functools
import jax
import jax.numpy as jnp
from jax import lax
from jax.sharding import PartitionSpec as P
from jax.experimental import pallas as pl
from jax.experimental.pallas import tpu as pltpu


def hid_gather_kernel(n, x_ref, out_ref, local_sem, send_sem, recv_sem):
    me = lax.axis_index("hid")
    row = lax.axis_index("exp")
    mesh_ids = pl.DeviceIdType.MESH
    barrier = pltpu.get_barrier_semaphore()
    for k in range(1, n):
        peer = lax.rem(me + k, n)
        pl.semaphore_signal(barrier, inc=1, device_id=(row, peer), device_id_type=mesh_ids)
    pl.semaphore_wait(barrier, n - 1)
    local = pltpu.make_async_copy(x_ref, out_ref.at[me], local_sem)
    local.start()
    copies = []
    for k in range(1, n):
        peer = lax.rem(me + k, n)
        copy = pltpu.make_async_remote_copy(
            src_ref=x_ref,
            dst_ref=out_ref.at[me],
            send_sem=send_sem.at[k],
            recv_sem=recv_sem.at[k],
            device_id=(row, peer),
            device_id_type=mesh_ids,
        )
        copy.start()
        copies.append(copy)
    local.wait()
    for copy in copies:
        copy.wait()


def exchange_kernel(axis, n, x_ref, out_ref, local_sem, send_sem, recv_sem):
    me = lax.axis_index(axis)
    own_exp = lax.axis_index("exp")
    own_hid = lax.axis_index("hid")
    mesh_ids = pl.DeviceIdType.MESH
    where = lambda peer: (peer, own_hid) if axis == "exp" else (own_exp, peer)
    barrier = pltpu.get_barrier_semaphore()
    for k in range(1, n):
        peer = lax.rem(me + k, n)
        pl.semaphore_signal(barrier, inc=1, device_id=where(peer), device_id_type=mesh_ids)
    pl.semaphore_wait(barrier, n - 1)
    local = pltpu.make_async_copy(x_ref.at[me], out_ref.at[me], local_sem)
    local.start()
    copies = []
    for k in range(1, n):
        peer = lax.rem(me + k, n)
        copy = pltpu.make_async_remote_copy(
            src_ref=x_ref.at[peer],
            dst_ref=out_ref.at[me],
            send_sem=send_sem.at[k],
            recv_sem=recv_sem.at[k],
            device_id=where(peer),
            device_id_type=mesh_ids,
        )
        copy.start()
        copies.append(copy)
    local.wait()
    for copy in copies:
        copy.wait()


def exchange(chunks, axis, kernel_id):
    n = chunks.shape[0]
    return pl.pallas_call(
        functools.partial(exchange_kernel, axis, n),
        out_shape=jax.ShapeDtypeStruct(chunks.shape, chunks.dtype),
        in_specs=[pl.BlockSpec(memory_space=pltpu.VMEM)],
        out_specs=pl.BlockSpec(memory_space=pltpu.VMEM),
        scratch_shapes=[
            pltpu.SemaphoreType.DMA,
            pltpu.SemaphoreType.DMA((n,)),
            pltpu.SemaphoreType.DMA((n,)),
        ],
        compiler_params=pltpu.CompilerParams(collective_id=kernel_id, has_side_effects=True),
    )(chunks)


def hid_gather(block):
    n = lax.axis_size("hid")
    return pl.pallas_call(
        functools.partial(hid_gather_kernel, n),
        out_shape=jax.ShapeDtypeStruct((n,) + block.shape, block.dtype),
        in_specs=[pl.BlockSpec(memory_space=pltpu.VMEM)],
        out_specs=pl.BlockSpec(memory_space=pltpu.VMEM),
        scratch_shapes=[
            pltpu.SemaphoreType.DMA,
            pltpu.SemaphoreType.DMA((n,)),
            pltpu.SemaphoreType.DMA((n,)),
        ],
        compiler_params=pltpu.CompilerParams(collective_id=0, has_side_effects=True),
    )(block).reshape((n * block.shape[0],) + block.shape[1:])


def softmax_rows(values):
    top_val = jnp.max(values, axis=-1, keepdims=True)
    raised = jnp.exp(values - top_val)
    return raised / jnp.sum(raised, axis=-1, keepdims=True)


def combine_table(logits, chosen, expert_count):
    picked = jnp.take_along_axis(logits, chosen, axis=1)
    weights = softmax_rows(picked)
    expert_ids = jnp.arange(expert_count, dtype=jnp.int32)
    matched = (chosen[:, :, None] == expert_ids[None, None, :]).astype(jnp.float32)
    return jnp.sum(weights[:, :, None] * matched, axis=1).astype(jnp.bfloat16)


CAP = 4


def slot_rows(column, group_rows):
    shaped = column.reshape(column.shape[:-1] + (-1, group_rows))
    place = jnp.arange(group_rows, dtype=jnp.int32)
    key = jnp.where(shaped != 0, 2 * group_rows - place, -place)
    return lax.top_k(key, CAP)[1]


def split3(value):
    hi = value.astype(jnp.bfloat16)
    rest = value - hi.astype(jnp.float32)
    mid = rest.astype(jnp.bfloat16)
    lo = (rest - mid.astype(jnp.float32)).astype(jnp.bfloat16)
    return jnp.concatenate([hi, mid, lo], axis=-1)


def join3(pieces, width):
    part = lambda i: pieces[..., i * width : (i + 1) * width].astype(jnp.float32)
    return (part(0) + part(1)) + part(2)


def pick_rows(choice, value):
    hi = value.astype(jnp.bfloat16)
    rest = value - hi.astype(jnp.float32)
    mid = rest.astype(jnp.bfloat16)
    lo = (rest - mid.astype(jnp.float32)).astype(jnp.bfloat16)
    dot = lambda piece: jnp.dot(choice, piece, preferred_element_type=jnp.float32)
    return (dot(hi) + dot(mid)) + dot(lo)


def dense_kernel(rows_ref, x_ref, g_ref, wg_ref, wu_ref, wd_ref, score_ref, gate_ref, up_ref, back_ref):
    step = pl.program_id(0)
    x = x_ref[...]
    gate_pre = jnp.dot(x, wg_ref[...], preferred_element_type=jnp.float32)
    up_pre = jnp.dot(x, wu_ref[...], preferred_element_type=jnp.float32)
    back_grad = lax.dot_general(
        g_ref[...], wd_ref[...], (((1,), (1,)), ((), ())), preferred_element_type=jnp.float32
    )
    sig_gate = 1.0 / (1.0 + jnp.exp(-gate_pre))
    score_ref[...] = jnp.sum(gate_pre * sig_gate * up_pre * back_grad, axis=1, keepdims=True)
    tile = x.shape[0]
    place = step * tile + lax.broadcasted_iota(jnp.int32, (1, tile), 1)
    choice = (rows_ref[...] == place).astype(jnp.bfloat16)

    @pl.when(step == 0)
    def _():
        gate_ref[...] = jnp.zeros_like(gate_ref)
        up_ref[...] = jnp.zeros_like(up_ref)
        back_ref[...] = jnp.zeros_like(back_ref)

    gate_ref[...] += pick_rows(choice, gate_pre)
    up_ref[...] += pick_rows(choice, up_pre)
    back_ref[...] += pick_rows(choice, back_grad)


def dense_unit(gathered, rows, gate_w, up_w, down_w, tile=256):
    tokens_n = gathered.shape[0]
    width, hidden = gate_w.shape
    slots = rows.shape[0]
    tiles = lambda i: (i, 0)
    fixed = lambda i: (0, 0)
    f32 = jnp.float32
    return pl.pallas_call(
        dense_kernel,
        grid=(tokens_n // tile,),
        out_shape=[
            jax.ShapeDtypeStruct((tokens_n, 1), f32),
            jax.ShapeDtypeStruct((slots, hidden), f32),
            jax.ShapeDtypeStruct((slots, hidden), f32),
            jax.ShapeDtypeStruct((slots, hidden), f32),
        ],
        in_specs=[
            pl.BlockSpec((slots, 1), fixed),
            pl.BlockSpec((tile, width), tiles),
            pl.BlockSpec((tile, width), lambda i: (i, 1)),
            pl.BlockSpec((width, hidden), fixed),
            pl.BlockSpec((width, hidden), fixed),
            pl.BlockSpec((hidden, width), fixed),
        ],
        out_specs=[
            pl.BlockSpec((tile, 1), tiles),
            pl.BlockSpec((slots, hidden), fixed),
            pl.BlockSpec((slots, hidden), fixed),
            pl.BlockSpec((slots, hidden), fixed),
        ],
    )(rows.reshape(slots, 1), gathered, gathered, gate_w, up_w, down_w)


def chosen_rows(column, group_rows):
    picked = slot_rows(column, group_rows)
    starts = (jnp.arange(picked.shape[1], dtype=jnp.int32) * group_rows)[None, :, None]
    return (picked + starts).reshape(picked.shape[0], -1)


def sparse_terms(gate_s, up_s, back_s, rows, column, w_gate, w_up):
    col_s = jnp.take_along_axis(column, rows, axis=1)
    sig_gate = jax.nn.sigmoid(gate_s)
    act_gate = gate_s * sig_gate
    weighted = col_s[:, :, None] * back_s
    grad_gate = (weighted * up_s * sig_gate * (1.0 + gate_s * (1.0 - sig_gate))).astype(jnp.bfloat16)
    grad_up = (weighted * act_gate).astype(jnp.bfloat16)
    part = jnp.einsum("usf,udf->usd", grad_gate, w_gate, preferred_element_type=jnp.float32)
    part = part + jnp.einsum("usf,udf->usd", grad_up, w_up, preferred_element_type=jnp.float32)
    return part.reshape(part.shape[0], -1, CAP, part.shape[-1])


def on_device(tokens, grad_out, router_logits, selected, router_w, w_gate, w_up, w_down):
    tok_local, model_width = tokens.shape
    unit_count = w_gate.shape[0]
    expert_count = router_logits.shape[1]
    spread_exp = lax.axis_size("exp")
    spread_hid = lax.axis_size("hid")
    group_rows = spread_hid * tok_local
    own_exp = lax.axis_index("exp")
    own_hid = lax.axis_index("hid")
    own_block = lax.axis_index(("exp", "hid"))
    unit_expert = (own_block * unit_count + jnp.arange(unit_count, dtype=jnp.int32)) // 2
    expert_ids = jnp.arange(expert_count, dtype=jnp.int32)
    unit_pick = (expert_ids[:, None] == unit_expert[None, :]).astype(jnp.bfloat16)
    combine = combine_table(router_logits, selected, expert_count)
    packed = jnp.concatenate([tokens, grad_out, combine], axis=1)
    gathered = lax.all_gather(hid_gather(packed), "exp", axis=0, tiled=True)
    combine_all = gathered[:, 2 * model_width :]
    column = jnp.dot(combine_all, unit_pick, preferred_element_type=jnp.float32).T
    rows = chosen_rows(column, group_rows)
    dense = [dense_unit(gathered, rows[i], w_gate[i], w_up[i], w_down[i]) for i in range(unit_count)]
    score_part = jnp.concatenate([d[0] for d in dense], axis=1)
    gate_s, up_s, back_s = (jnp.stack([d[j] for d in dense]) for j in (1, 2, 3))
    part = sparse_terms(gate_s, up_s, back_s, rows, column, w_gate, w_up)
    lane = 128
    score_grp = jnp.swapaxes(score_part.T.reshape(unit_count, spread_exp, CAP, group_rows // CAP), 0, 1)
    score_grp = split3(score_grp)
    score_grp = jnp.pad(score_grp, ((0, 0), (0, 0), (0, 0), (0, lane - score_grp.shape[3])))
    sent = jnp.concatenate([jnp.swapaxes(part, 0, 1).astype(jnp.bfloat16), score_grp], axis=3)
    arrived_part = exchange(sent, "exp", 1)
    sender_block = (jnp.arange(spread_exp, dtype=jnp.int32) * spread_hid + own_hid)[:, None]
    sender_expert = (sender_block * unit_count + jnp.arange(unit_count, dtype=jnp.int32)[None, :]) // 2
    own_combine = lax.dynamic_slice_in_dim(combine_all, own_exp * group_rows, group_rows, 0)
    sender_pick = (expert_ids[:, None] == sender_expert.reshape(1, -1)).astype(jnp.bfloat16)
    sender_column = jnp.dot(own_combine, sender_pick, preferred_element_type=jnp.float32).T
    sender_rows = slot_rows(sender_column, group_rows).reshape(-1)
    place = (sender_rows[:, None] == jnp.arange(group_rows, dtype=jnp.int32)[None, :]).astype(jnp.bfloat16)
    group_sum = jnp.einsum(
        "sj,sd->jd", place, arrived_part[..., :model_width].reshape(-1, model_width),
        preferred_element_type=jnp.float32,
    )
    got_scores = join3(arrived_part[..., model_width:], group_rows // CAP)
    got_scores = got_scores.reshape(spread_exp, unit_count, spread_hid, tok_local)
    score_cols = spread_exp * unit_count
    hid_scores = jnp.transpose(got_scores, (2, 3, 0, 1)).reshape(spread_hid, tok_local, score_cols)
    hid_scores = split3(hid_scores)
    score_width = -(-hid_scores.shape[2] // lane) * lane
    hid_scores = jnp.pad(hid_scores, ((0, 0), (0, 0), (0, score_width - hid_scores.shape[2])))
    hid_sent = jnp.concatenate(
        [group_sum.reshape(spread_hid, tok_local, model_width).astype(jnp.bfloat16), hid_scores], axis=2
    )
    spread_rows = exchange(hid_sent, "hid", 2)
    input_sum = jnp.sum(spread_rows[..., :model_width].astype(jnp.float32), axis=0)
    own_scores = join3(spread_rows[..., model_width:], score_cols)
    own_scores = own_scores.reshape(spread_hid, tok_local, spread_exp, unit_count)
    unit_scores = jnp.transpose(own_scores, (1, 2, 0, 3)).reshape(tok_local, -1)
    expert_scores = jnp.sum(unit_scores.reshape(tok_local, expert_count, 2), axis=2)
    probs_all = softmax_rows(router_logits)
    mean_score = jnp.sum(probs_all * expert_scores, axis=1, keepdims=True)
    logit_grad = (probs_all * (expert_scores - mean_score)).astype(jnp.bfloat16)
    devices = spread_exp * spread_hid
    logit_all = lax.all_to_all(
        jnp.broadcast_to(logit_grad[None], (devices,) + logit_grad.shape), ("exp", "hid"), 0, 0, tiled=True
    ).reshape(-1, expert_count)
    grad_rows = model_width // devices
    token_cols = lax.dynamic_slice_in_dim(gathered, own_block * grad_rows, grad_rows, 1)
    router_grad = jnp.einsum("tc,te->ce", token_cols, logit_all, preferred_element_type=jnp.float32)
    router_part = jnp.einsum("te,de->td", logit_grad, router_w, preferred_element_type=jnp.float32)
    x_grad = (input_sum + router_part).astype(jnp.bfloat16)
    return (x_grad, router_grad)


def solution(mesh):
    placed = (
        P(("exp", "hid"), None),
        P(("exp", "hid"), None),
        P(("exp", "hid"), None),
        P(("exp", "hid"), None),
        P(),
        P(("exp", "hid"), None, None),
        P(("exp", "hid"), None, None),
        P(("exp", "hid"), None, None),
    )
    return jax.shard_map(
        on_device,
        mesh=mesh,
        in_specs=placed,
        out_specs=(P(("exp", "hid"), None), P(("exp", "hid"), None)),
        check_vma=False,
    )
```

```python
import functools
import jax
import jax.numpy as jnp
from jax import lax
from jax.sharding import PartitionSpec as P
from jax.experimental import pallas as pl
from jax.experimental.pallas import tpu as pltpu


def hid_gather_kernel(n, x_ref, out_ref, local_sem, send_sem, recv_sem):
    me = lax.axis_index("hid")
    rows = x_ref.shape[0]
    slot = out_ref.at[pl.ds(pl.multiple_of(me * rows, rows), rows)]
    row = lax.axis_index("exp")
    mesh_ids = pl.DeviceIdType.MESH
    barrier = pltpu.get_barrier_semaphore()
    for k in range(1, n):
        peer = lax.rem(me + k, n)
        pl.semaphore_signal(barrier, inc=1, device_id=(row, peer), device_id_type=mesh_ids)
    pl.semaphore_wait(barrier, n - 1)
    local = pltpu.make_async_copy(x_ref, slot, local_sem)
    local.start()
    copies = []
    for k in range(1, n):
        peer = lax.rem(me + k, n)
        copy = pltpu.make_async_remote_copy(
            src_ref=x_ref,
            dst_ref=slot,
            send_sem=send_sem.at[k],
            recv_sem=recv_sem.at[k],
            device_id=(row, peer),
            device_id_type=mesh_ids,
        )
        copy.start()
        copies.append(copy)
    local.wait()
    for copy in copies:
        copy.wait()


def exchange_kernel(axis, n, x_ref, out_ref, local_sem, send_sem, recv_sem):
    me = lax.axis_index(axis)
    own_exp = lax.axis_index("exp")
    own_hid = lax.axis_index("hid")
    mesh_ids = pl.DeviceIdType.MESH
    where = lambda peer: (peer, own_hid) if axis == "exp" else (own_exp, peer)
    barrier = pltpu.get_barrier_semaphore()
    for k in range(1, n):
        peer = lax.rem(me + k, n)
        pl.semaphore_signal(barrier, inc=1, device_id=where(peer), device_id_type=mesh_ids)
    pl.semaphore_wait(barrier, n - 1)
    local = pltpu.make_async_copy(x_ref.at[me], out_ref.at[me], local_sem)
    local.start()
    copies = []
    for k in range(1, n):
        peer = lax.rem(me + k, n)
        copy = pltpu.make_async_remote_copy(
            src_ref=x_ref.at[peer],
            dst_ref=out_ref.at[me],
            send_sem=send_sem.at[k],
            recv_sem=recv_sem.at[k],
            device_id=where(peer),
            device_id_type=mesh_ids,
        )
        copy.start()
        copies.append(copy)
    local.wait()
    for copy in copies:
        copy.wait()


def exchange(chunks, axis, kernel_id):
    n = chunks.shape[0]
    return pl.pallas_call(
        functools.partial(exchange_kernel, axis, n),
        out_shape=jax.ShapeDtypeStruct(chunks.shape, chunks.dtype),
        in_specs=[pl.BlockSpec(memory_space=pltpu.VMEM)],
        out_specs=pl.BlockSpec(memory_space=pltpu.VMEM),
        scratch_shapes=[
            pltpu.SemaphoreType.DMA,
            pltpu.SemaphoreType.DMA((n,)),
            pltpu.SemaphoreType.DMA((n,)),
        ],
        compiler_params=pltpu.CompilerParams(collective_id=kernel_id, has_side_effects=True),
    )(chunks)


def hid_gather(block):
    n = lax.axis_size("hid")
    return pl.pallas_call(
        functools.partial(hid_gather_kernel, n),
        out_shape=jax.ShapeDtypeStruct((n * block.shape[0],) + block.shape[1:], block.dtype),
        in_specs=[pl.BlockSpec(memory_space=pltpu.VMEM)],
        out_specs=pl.BlockSpec(memory_space=pltpu.VMEM),
        scratch_shapes=[
            pltpu.SemaphoreType.DMA,
            pltpu.SemaphoreType.DMA((n,)),
            pltpu.SemaphoreType.DMA((n,)),
        ],
        compiler_params=pltpu.CompilerParams(collective_id=0, has_side_effects=True),
    )(block)


def softmax_rows(values):
    top_val = jnp.max(values, axis=-1, keepdims=True)
    raised = jnp.exp(values - top_val)
    return raised / jnp.sum(raised, axis=-1, keepdims=True)


def combine_table(logits, chosen, expert_count):
    picked = jnp.take_along_axis(logits, chosen, axis=1)
    weights = softmax_rows(picked)
    expert_ids = jnp.arange(expert_count, dtype=jnp.int32)
    matched = (chosen[:, :, None] == expert_ids[None, None, :]).astype(jnp.float32)
    return jnp.sum(weights[:, :, None] * matched, axis=1).astype(jnp.bfloat16)


CAP = 4


def slot_rows(column, group_rows):
    shaped = column.reshape(column.shape[:-1] + (-1, group_rows))
    place = jnp.arange(group_rows, dtype=jnp.int32)
    key = jnp.where(shaped != 0, 2 * group_rows - place, -place)
    return lax.top_k(key, CAP)[1]


def split3(value):
    hi = value.astype(jnp.bfloat16)
    rest = value - hi.astype(jnp.float32)
    mid = rest.astype(jnp.bfloat16)
    lo = (rest - mid.astype(jnp.float32)).astype(jnp.bfloat16)
    return jnp.concatenate([hi, mid, lo], axis=-1)


def join3(pieces, width):
    part = lambda i: pieces[..., i * width : (i + 1) * width].astype(jnp.float32)
    return (part(0) + part(1)) + part(2)


def pick_rows(choice, value):
    hi = value.astype(jnp.bfloat16)
    rest = value - hi.astype(jnp.float32)
    mid = rest.astype(jnp.bfloat16)
    lo = (rest - mid.astype(jnp.float32)).astype(jnp.bfloat16)
    dot = lambda piece: jnp.dot(choice, piece, preferred_element_type=jnp.float32)
    return (dot(hi) + dot(mid)) + dot(lo)


def dense_kernel(rows_ref, x_ref, g_ref, wg_ref, wu_ref, wd_ref, score_ref, gate_ref, up_ref, back_ref):
    step = pl.program_id(0)
    x = x_ref[...]
    gate_pre = jnp.dot(x, wg_ref[...], preferred_element_type=jnp.float32)
    up_pre = jnp.dot(x, wu_ref[...], preferred_element_type=jnp.float32)
    back_grad = lax.dot_general(
        g_ref[...], wd_ref[...], (((1,), (1,)), ((), ())), preferred_element_type=jnp.float32
    )
    sig_gate = 1.0 / (1.0 + jnp.exp(-gate_pre))
    score_ref[...] = jnp.sum(gate_pre * sig_gate * up_pre * back_grad, axis=1, keepdims=True)
    tile = x.shape[0]
    place = step * tile + lax.broadcasted_iota(jnp.int32, (1, tile), 1)
    choice = (rows_ref[...] == place).astype(jnp.bfloat16)

    @pl.when(step == 0)
    def _():
        gate_ref[...] = jnp.zeros_like(gate_ref)
        up_ref[...] = jnp.zeros_like(up_ref)
        back_ref[...] = jnp.zeros_like(back_ref)

    gate_ref[...] += pick_rows(choice, gate_pre)
    up_ref[...] += pick_rows(choice, up_pre)
    back_ref[...] += pick_rows(choice, back_grad)


def dense_unit(gathered, rows, gate_w, up_w, down_w, tile=256):
    tokens_n = gathered.shape[0]
    width, hidden = gate_w.shape
    slots = rows.shape[0]
    tiles = lambda i: (i, 0)
    fixed = lambda i: (0, 0)
    f32 = jnp.float32
    return pl.pallas_call(
        dense_kernel,
        grid=(tokens_n // tile,),
        out_shape=[
            jax.ShapeDtypeStruct((tokens_n, 1), f32),
            jax.ShapeDtypeStruct((slots, hidden), f32),
            jax.ShapeDtypeStruct((slots, hidden), f32),
            jax.ShapeDtypeStruct((slots, hidden), f32),
        ],
        in_specs=[
            pl.BlockSpec((slots, 1), fixed),
            pl.BlockSpec((tile, width), tiles),
            pl.BlockSpec((tile, width), lambda i: (i, 1)),
            pl.BlockSpec((width, hidden), fixed),
            pl.BlockSpec((width, hidden), fixed),
            pl.BlockSpec((hidden, width), fixed),
        ],
        out_specs=[
            pl.BlockSpec((tile, 1), tiles),
            pl.BlockSpec((slots, hidden), fixed),
            pl.BlockSpec((slots, hidden), fixed),
            pl.BlockSpec((slots, hidden), fixed),
        ],
    )(rows.reshape(slots, 1), gathered, gathered, gate_w, up_w, down_w)


def chosen_rows(column, group_rows):
    picked = slot_rows(column, group_rows)
    starts = (jnp.arange(picked.shape[1], dtype=jnp.int32) * group_rows)[None, :, None]
    return (picked + starts).reshape(picked.shape[0], -1)


def sparse_terms(gate_s, up_s, back_s, rows, column, w_gate, w_up):
    col_s = jnp.take_along_axis(column, rows, axis=1)
    sig_gate = jax.nn.sigmoid(gate_s)
    act_gate = gate_s * sig_gate
    weighted = col_s[:, :, None] * back_s
    grad_gate = (weighted * up_s * sig_gate * (1.0 + gate_s * (1.0 - sig_gate))).astype(jnp.bfloat16)
    grad_up = (weighted * act_gate).astype(jnp.bfloat16)
    part = jnp.einsum("usf,udf->usd", grad_gate, w_gate, preferred_element_type=jnp.float32)
    part = part + jnp.einsum("usf,udf->usd", grad_up, w_up, preferred_element_type=jnp.float32)
    return part.reshape(part.shape[0], -1, CAP, part.shape[-1])


def on_device(tokens, grad_out, router_logits, selected, router_w, w_gate, w_up, w_down):
    tok_local, model_width = tokens.shape
    unit_count = w_gate.shape[0]
    expert_count = router_logits.shape[1]
    spread_exp = lax.axis_size("exp")
    spread_hid = lax.axis_size("hid")
    group_rows = spread_hid * tok_local
    own_exp = lax.axis_index("exp")
    own_hid = lax.axis_index("hid")
    own_block = lax.axis_index(("exp", "hid"))
    unit_expert = (own_block * unit_count + jnp.arange(unit_count, dtype=jnp.int32)) // 2
    expert_ids = jnp.arange(expert_count, dtype=jnp.int32)
    unit_pick = (expert_ids[:, None] == unit_expert[None, :]).astype(jnp.bfloat16)
    combine = combine_table(router_logits, selected, expert_count)
    packed = jnp.concatenate([tokens, grad_out, combine], axis=1)
    gathered = lax.all_gather(hid_gather(packed), "exp", axis=0, tiled=True)
    combine_all = gathered[:, 2 * model_width :]
    column = jnp.dot(combine_all, unit_pick, preferred_element_type=jnp.float32).T
    rows = chosen_rows(column, group_rows)
    dense = [dense_unit(gathered, rows[i], w_gate[i], w_up[i], w_down[i]) for i in range(unit_count)]
    score_part = jnp.concatenate([d[0] for d in dense], axis=1)
    gate_s, up_s, back_s = (jnp.stack([d[j] for d in dense]) for j in (1, 2, 3))
    part = sparse_terms(gate_s, up_s, back_s, rows, column, w_gate, w_up)
    lane = 128
    score_grp = jnp.swapaxes(score_part.T.reshape(unit_count, spread_exp, CAP, group_rows // CAP), 0, 1)
    score_grp = split3(score_grp)
    score_grp = jnp.pad(score_grp, ((0, 0), (0, 0), (0, 0), (0, lane - score_grp.shape[3])))
    sent = jnp.concatenate([jnp.swapaxes(part, 0, 1).astype(jnp.bfloat16), score_grp], axis=3)
    arrived_part = exchange(sent, "exp", 1)
    sender_block = (jnp.arange(spread_exp, dtype=jnp.int32) * spread_hid + own_hid)[:, None]
    sender_expert = (sender_block * unit_count + jnp.arange(unit_count, dtype=jnp.int32)[None, :]) // 2
    own_combine = lax.dynamic_slice_in_dim(combine_all, own_exp * group_rows, group_rows, 0)
    sender_pick = (expert_ids[:, None] == sender_expert.reshape(1, -1)).astype(jnp.bfloat16)
    sender_column = jnp.dot(own_combine, sender_pick, preferred_element_type=jnp.float32).T
    sender_rows = slot_rows(sender_column, group_rows).reshape(-1)
    place = (sender_rows[:, None] == jnp.arange(group_rows, dtype=jnp.int32)[None, :]).astype(jnp.bfloat16)
    group_sum = jnp.einsum(
        "sj,sd->jd", place, arrived_part[..., :model_width].reshape(-1, model_width),
        preferred_element_type=jnp.float32,
    )
    got_scores = join3(arrived_part[..., model_width:], group_rows // CAP)
    got_scores = got_scores.reshape(spread_exp, unit_count, spread_hid, tok_local)
    score_cols = spread_exp * unit_count
    hid_scores = jnp.transpose(got_scores, (2, 3, 0, 1)).reshape(spread_hid, tok_local, score_cols)
    hid_scores = split3(hid_scores)
    score_width = -(-hid_scores.shape[2] // lane) * lane
    hid_scores = jnp.pad(hid_scores, ((0, 0), (0, 0), (0, score_width - hid_scores.shape[2])))
    hid_sent = jnp.concatenate(
        [group_sum.reshape(spread_hid, tok_local, model_width).astype(jnp.bfloat16), hid_scores], axis=2
    )
    spread_rows = exchange(hid_sent, "hid", 2)
    input_sum = jnp.sum(spread_rows[..., :model_width].astype(jnp.float32), axis=0)
    own_scores = join3(spread_rows[..., model_width:], score_cols)
    own_scores = own_scores.reshape(spread_hid, tok_local, spread_exp, unit_count)
    unit_scores = jnp.transpose(own_scores, (1, 2, 0, 3)).reshape(tok_local, -1)
    expert_scores = jnp.sum(unit_scores.reshape(tok_local, expert_count, 2), axis=2)
    probs_all = softmax_rows(router_logits)
    mean_score = jnp.sum(probs_all * expert_scores, axis=1, keepdims=True)
    logit_grad = (probs_all * (expert_scores - mean_score)).astype(jnp.bfloat16)
    devices = spread_exp * spread_hid
    logit_all = lax.all_to_all(
        jnp.broadcast_to(logit_grad[None], (devices,) + logit_grad.shape), ("exp", "hid"), 0, 0, tiled=True
    ).reshape(-1, expert_count)
    grad_rows = model_width // devices
    token_cols = lax.dynamic_slice_in_dim(gathered, own_block * grad_rows, grad_rows, 1)
    router_grad = jnp.einsum("tc,te->ce", token_cols, logit_all, preferred_element_type=jnp.float32)
    router_part = jnp.einsum("te,de->td", logit_grad, router_w, preferred_element_type=jnp.float32)
    x_grad = (input_sum + router_part).astype(jnp.bfloat16)
    return (x_grad, router_grad)


def solution(mesh):
    placed = (
        P(("exp", "hid"), None),
        P(("exp", "hid"), None),
        P(("exp", "hid"), None),
        P(("exp", "hid"), None),
        P(),
        P(("exp", "hid"), None, None),
        P(("exp", "hid"), None, None),
        P(("exp", "hid"), None, None),
    )
    return jax.shard_map(
        on_device,
        mesh=mesh,
        in_specs=placed,
        out_specs=(P(("exp", "hid"), None), P(("exp", "hid"), None)),
        check_vma=False,
    )
```

```python
import functools
import jax
import jax.numpy as jnp
from jax import lax
from jax.sharding import PartitionSpec as P
from jax.experimental import pallas as pl
from jax.experimental.pallas import tpu as pltpu


def hid_gather_kernel(n, x_ref, out_ref, local_sem, send_sem, recv_sem):
    me = lax.axis_index("hid")
    rows = x_ref.shape[0]
    slot = out_ref.at[pl.ds(pl.multiple_of(me * rows, rows), rows)]
    row = lax.axis_index("exp")
    mesh_ids = pl.DeviceIdType.MESH
    barrier = pltpu.get_barrier_semaphore()
    for k in range(1, n):
        peer = lax.rem(me + k, n)
        pl.semaphore_signal(barrier, inc=1, device_id=(row, peer), device_id_type=mesh_ids)
    pl.semaphore_wait(barrier, n - 1)
    local = pltpu.make_async_copy(x_ref, slot, local_sem)
    local.start()
    copies = []
    for k in range(1, n):
        peer = lax.rem(me + k, n)
        copy = pltpu.make_async_remote_copy(
            src_ref=x_ref,
            dst_ref=slot,
            send_sem=send_sem.at[k],
            recv_sem=recv_sem.at[k],
            device_id=(row, peer),
            device_id_type=mesh_ids,
        )
        copy.start()
        copies.append(copy)
    local.wait()
    for copy in copies:
        copy.wait()


def exchange_kernel(axis, n, x_ref, out_ref, local_sem, send_sem, recv_sem):
    me = lax.axis_index(axis)
    own_exp = lax.axis_index("exp")
    own_hid = lax.axis_index("hid")
    mesh_ids = pl.DeviceIdType.MESH
    where = lambda peer: (peer, own_hid) if axis == "exp" else (own_exp, peer)
    barrier = pltpu.get_barrier_semaphore()
    for k in range(1, n):
        peer = lax.rem(me + k, n)
        pl.semaphore_signal(barrier, inc=1, device_id=where(peer), device_id_type=mesh_ids)
    pl.semaphore_wait(barrier, n - 1)
    local = pltpu.make_async_copy(x_ref.at[me], out_ref.at[me], local_sem)
    local.start()
    copies = []
    for k in range(1, n):
        peer = lax.rem(me + k, n)
        copy = pltpu.make_async_remote_copy(
            src_ref=x_ref.at[peer],
            dst_ref=out_ref.at[me],
            send_sem=send_sem.at[k],
            recv_sem=recv_sem.at[k],
            device_id=where(peer),
            device_id_type=mesh_ids,
        )
        copy.start()
        copies.append(copy)
    local.wait()
    for copy in copies:
        copy.wait()


def exchange(chunks, axis, kernel_id):
    n = chunks.shape[0]
    return pl.pallas_call(
        functools.partial(exchange_kernel, axis, n),
        out_shape=jax.ShapeDtypeStruct(chunks.shape, chunks.dtype),
        in_specs=[pl.BlockSpec(memory_space=pltpu.VMEM)],
        out_specs=pl.BlockSpec(memory_space=pltpu.VMEM),
        scratch_shapes=[
            pltpu.SemaphoreType.DMA,
            pltpu.SemaphoreType.DMA((n,)),
            pltpu.SemaphoreType.DMA((n,)),
        ],
        compiler_params=pltpu.CompilerParams(collective_id=kernel_id, has_side_effects=True),
    )(chunks)


def hid_gather(block):
    n = lax.axis_size("hid")
    return pl.pallas_call(
        functools.partial(hid_gather_kernel, n),
        out_shape=jax.ShapeDtypeStruct((n * block.shape[0],) + block.shape[1:], block.dtype),
        in_specs=[pl.BlockSpec(memory_space=pltpu.VMEM)],
        out_specs=pl.BlockSpec(memory_space=pltpu.VMEM),
        scratch_shapes=[
            pltpu.SemaphoreType.DMA,
            pltpu.SemaphoreType.DMA((n,)),
            pltpu.SemaphoreType.DMA((n,)),
        ],
        compiler_params=pltpu.CompilerParams(collective_id=0, has_side_effects=True),
    )(block)


def softmax_rows(values):
    top_val = jnp.max(values, axis=-1, keepdims=True)
    raised = jnp.exp(values - top_val)
    return raised / jnp.sum(raised, axis=-1, keepdims=True)


def combine_table(logits, chosen, expert_count):
    picked = jnp.take_along_axis(logits, chosen, axis=1)
    weights = softmax_rows(picked)
    expert_ids = jnp.arange(expert_count, dtype=jnp.int32)
    matched = (chosen[:, :, None] == expert_ids[None, None, :]).astype(jnp.float32)
    return jnp.sum(weights[:, :, None] * matched, axis=1).astype(jnp.bfloat16)


CAP = 4


def slot_rows(column, group_rows):
    shaped = column.reshape(column.shape[:-1] + (-1, group_rows))
    place = jnp.arange(group_rows, dtype=jnp.int32)
    key = jnp.where(shaped != 0, 2 * group_rows - place, -place)
    return lax.top_k(key, CAP)[1]


def split3(value):
    hi = value.astype(jnp.bfloat16)
    rest = value - hi.astype(jnp.float32)
    mid = rest.astype(jnp.bfloat16)
    lo = (rest - mid.astype(jnp.float32)).astype(jnp.bfloat16)
    return jnp.concatenate([hi, mid, lo], axis=-1)


def join3(pieces, width):
    part = lambda i: pieces[..., i * width : (i + 1) * width].astype(jnp.float32)
    return (part(0) + part(1)) + part(2)


def pick_rows(choice, value):
    hi = value.astype(jnp.bfloat16)
    rest = value - hi.astype(jnp.float32)
    mid = rest.astype(jnp.bfloat16)
    lo = (rest - mid.astype(jnp.float32)).astype(jnp.bfloat16)
    dot = lambda piece: jnp.dot(choice, piece, preferred_element_type=jnp.float32)
    return (dot(hi) + dot(mid)) + dot(lo)


def dense_kernel(rows_ref, x_ref, g_ref, wg_ref, wu_ref, wd_ref, score_ref, gate_ref, up_ref, back_ref):
    step = pl.program_id(0)
    x = x_ref[...]
    gate_pre = jnp.dot(x, wg_ref[...], preferred_element_type=jnp.float32)
    up_pre = jnp.dot(x, wu_ref[...], preferred_element_type=jnp.float32)
    back_grad = lax.dot_general(
        g_ref[...], wd_ref[...], (((1,), (1,)), ((), ())), preferred_element_type=jnp.float32
    )
    sig_gate = 1.0 / (1.0 + jnp.exp(-gate_pre))
    score_ref[...] = jnp.sum(gate_pre * sig_gate * up_pre * back_grad, axis=1, keepdims=True)
    tile = x.shape[0]
    place = step * tile + lax.broadcasted_iota(jnp.int32, (1, tile), 1)
    choice = (rows_ref[...] == place).astype(jnp.bfloat16)

    @pl.when(step == 0)
    def _():
        gate_ref[...] = jnp.zeros_like(gate_ref)
        up_ref[...] = jnp.zeros_like(up_ref)
        back_ref[...] = jnp.zeros_like(back_ref)

    gate_ref[...] += pick_rows(choice, gate_pre)
    up_ref[...] += pick_rows(choice, up_pre)
    back_ref[...] += pick_rows(choice, back_grad)


def dense_unit(gathered, rows, gate_w, up_w, down_w, tile=512):
    tokens_n = gathered.shape[0]
    width, hidden = gate_w.shape
    slots = rows.shape[0]
    tiles = lambda i: (i, 0)
    fixed = lambda i: (0, 0)
    f32 = jnp.float32
    return pl.pallas_call(
        dense_kernel,
        grid=(tokens_n // tile,),
        out_shape=[
            jax.ShapeDtypeStruct((tokens_n, 1), f32),
            jax.ShapeDtypeStruct((slots, hidden), f32),
            jax.ShapeDtypeStruct((slots, hidden), f32),
            jax.ShapeDtypeStruct((slots, hidden), f32),
        ],
        in_specs=[
            pl.BlockSpec((slots, 1), fixed),
            pl.BlockSpec((tile, width), tiles),
            pl.BlockSpec((tile, width), lambda i: (i, 1)),
            pl.BlockSpec((width, hidden), fixed),
            pl.BlockSpec((width, hidden), fixed),
            pl.BlockSpec((hidden, width), fixed),
        ],
        out_specs=[
            pl.BlockSpec((tile, 1), tiles),
            pl.BlockSpec((slots, hidden), fixed),
            pl.BlockSpec((slots, hidden), fixed),
            pl.BlockSpec((slots, hidden), fixed),
        ],
    )(rows.reshape(slots, 1), gathered, gathered, gate_w, up_w, down_w)


def chosen_rows(column, group_rows):
    picked = slot_rows(column, group_rows)
    starts = (jnp.arange(picked.shape[1], dtype=jnp.int32) * group_rows)[None, :, None]
    return (picked + starts).reshape(picked.shape[0], -1)


def sparse_terms(gate_s, up_s, back_s, rows, column, w_gate, w_up):
    col_s = jnp.take_along_axis(column, rows, axis=1)
    sig_gate = jax.nn.sigmoid(gate_s)
    act_gate = gate_s * sig_gate
    weighted = col_s[:, :, None] * back_s
    grad_gate = (weighted * up_s * sig_gate * (1.0 + gate_s * (1.0 - sig_gate))).astype(jnp.bfloat16)
    grad_up = (weighted * act_gate).astype(jnp.bfloat16)
    part = jnp.einsum("usf,udf->usd", grad_gate, w_gate, preferred_element_type=jnp.float32)
    part = part + jnp.einsum("usf,udf->usd", grad_up, w_up, preferred_element_type=jnp.float32)
    return part.reshape(part.shape[0], -1, CAP, part.shape[-1])


def on_device(tokens, grad_out, router_logits, selected, router_w, w_gate, w_up, w_down):
    tok_local, model_width = tokens.shape
    unit_count = w_gate.shape[0]
    expert_count = router_logits.shape[1]
    spread_exp = lax.axis_size("exp")
    spread_hid = lax.axis_size("hid")
    group_rows = spread_hid * tok_local
    own_exp = lax.axis_index("exp")
    own_hid = lax.axis_index("hid")
    own_block = lax.axis_index(("exp", "hid"))
    unit_expert = (own_block * unit_count + jnp.arange(unit_count, dtype=jnp.int32)) // 2
    expert_ids = jnp.arange(expert_count, dtype=jnp.int32)
    unit_pick = (expert_ids[:, None] == unit_expert[None, :]).astype(jnp.bfloat16)
    combine = combine_table(router_logits, selected, expert_count)
    packed = jnp.concatenate([tokens, grad_out, combine], axis=1)
    gathered = lax.all_gather(hid_gather(packed), "exp", axis=0, tiled=True)
    combine_all = gathered[:, 2 * model_width :]
    column = jnp.dot(combine_all, unit_pick, preferred_element_type=jnp.float32).T
    rows = chosen_rows(column, group_rows)
    dense = [dense_unit(gathered, rows[i], w_gate[i], w_up[i], w_down[i]) for i in range(unit_count)]
    score_part = jnp.concatenate([d[0] for d in dense], axis=1)
    gate_s, up_s, back_s = (jnp.stack([d[j] for d in dense]) for j in (1, 2, 3))
    part = sparse_terms(gate_s, up_s, back_s, rows, column, w_gate, w_up)
    lane = 128
    score_grp = jnp.swapaxes(score_part.T.reshape(unit_count, spread_exp, CAP, group_rows // CAP), 0, 1)
    score_grp = split3(score_grp)
    score_grp = jnp.pad(score_grp, ((0, 0), (0, 0), (0, 0), (0, lane - score_grp.shape[3])))
    sent = jnp.concatenate([jnp.swapaxes(part, 0, 1).astype(jnp.bfloat16), score_grp], axis=3)
    arrived_part = exchange(sent, "exp", 1)
    sender_block = (jnp.arange(spread_exp, dtype=jnp.int32) * spread_hid + own_hid)[:, None]
    sender_expert = (sender_block * unit_count + jnp.arange(unit_count, dtype=jnp.int32)[None, :]) // 2
    own_combine = lax.dynamic_slice_in_dim(combine_all, own_exp * group_rows, group_rows, 0)
    sender_pick = (expert_ids[:, None] == sender_expert.reshape(1, -1)).astype(jnp.bfloat16)
    sender_column = jnp.dot(own_combine, sender_pick, preferred_element_type=jnp.float32).T
    sender_rows = slot_rows(sender_column, group_rows).reshape(-1)
    place = (sender_rows[:, None] == jnp.arange(group_rows, dtype=jnp.int32)[None, :]).astype(jnp.bfloat16)
    group_sum = jnp.einsum(
        "sj,sd->jd", place, arrived_part[..., :model_width].reshape(-1, model_width),
        preferred_element_type=jnp.float32,
    )
    got_scores = join3(arrived_part[..., model_width:], group_rows // CAP)
    got_scores = got_scores.reshape(spread_exp, unit_count, spread_hid, tok_local)
    score_cols = spread_exp * unit_count
    hid_scores = jnp.transpose(got_scores, (2, 3, 0, 1)).reshape(spread_hid, tok_local, score_cols)
    hid_scores = split3(hid_scores)
    score_width = -(-hid_scores.shape[2] // lane) * lane
    hid_scores = jnp.pad(hid_scores, ((0, 0), (0, 0), (0, score_width - hid_scores.shape[2])))
    hid_sent = jnp.concatenate(
        [group_sum.reshape(spread_hid, tok_local, model_width).astype(jnp.bfloat16), hid_scores], axis=2
    )
    spread_rows = exchange(hid_sent, "hid", 2)
    input_sum = jnp.sum(spread_rows[..., :model_width].astype(jnp.float32), axis=0)
    own_scores = join3(spread_rows[..., model_width:], score_cols)
    own_scores = own_scores.reshape(spread_hid, tok_local, spread_exp, unit_count)
    unit_scores = jnp.transpose(own_scores, (1, 2, 0, 3)).reshape(tok_local, -1)
    expert_scores = jnp.sum(unit_scores.reshape(tok_local, expert_count, 2), axis=2)
    probs_all = softmax_rows(router_logits)
    mean_score = jnp.sum(probs_all * expert_scores, axis=1, keepdims=True)
    logit_grad = (probs_all * (expert_scores - mean_score)).astype(jnp.bfloat16)
    devices = spread_exp * spread_hid
    logit_all = lax.all_to_all(
        jnp.broadcast_to(logit_grad[None], (devices,) + logit_grad.shape), ("exp", "hid"), 0, 0, tiled=True
    ).reshape(-1, expert_count)
    grad_rows = model_width // devices
    token_cols = lax.dynamic_slice_in_dim(gathered, own_block * grad_rows, grad_rows, 1)
    router_grad = jnp.einsum("tc,te->ce", token_cols, logit_all, preferred_element_type=jnp.float32)
    router_part = jnp.einsum("te,de->td", logit_grad, router_w, preferred_element_type=jnp.float32)
    x_grad = (input_sum + router_part).astype(jnp.bfloat16)
    return (x_grad, router_grad)


def solution(mesh):
    placed = (
        P(("exp", "hid"), None),
        P(("exp", "hid"), None),
        P(("exp", "hid"), None),
        P(("exp", "hid"), None),
        P(),
        P(("exp", "hid"), None, None),
        P(("exp", "hid"), None, None),
        P(("exp", "hid"), None, None),
    )
    return jax.shard_map(
        on_device,
        mesh=mesh,
        in_specs=placed,
        out_specs=(P(("exp", "hid"), None), P(("exp", "hid"), None)),
        check_vma=False,
    )
```

```python
import functools
import jax
import jax.numpy as jnp
from jax import lax
from jax.sharding import PartitionSpec as P
from jax.experimental import pallas as pl
from jax.experimental.pallas import tpu as pltpu


def hid_gather_kernel(n, x_ref, out_ref, local_sem, send_sem, recv_sem):
    me = lax.axis_index("hid")
    rows = x_ref.shape[0]
    slot = out_ref.at[pl.ds(pl.multiple_of(me * rows, rows), rows)]
    row = lax.axis_index("exp")
    mesh_ids = pl.DeviceIdType.MESH
    barrier = pltpu.get_barrier_semaphore()
    for k in range(1, n):
        peer = lax.rem(me + k, n)
        pl.semaphore_signal(barrier, inc=1, device_id=(row, peer), device_id_type=mesh_ids)
    pl.semaphore_wait(barrier, n - 1)
    local = pltpu.make_async_copy(x_ref, slot, local_sem)
    local.start()
    copies = []
    for k in range(1, n):
        peer = lax.rem(me + k, n)
        copy = pltpu.make_async_remote_copy(
            src_ref=x_ref,
            dst_ref=slot,
            send_sem=send_sem.at[k],
            recv_sem=recv_sem.at[k],
            device_id=(row, peer),
            device_id_type=mesh_ids,
        )
        copy.start()
        copies.append(copy)
    local.wait()
    for copy in copies:
        copy.wait()


def exchange_kernel(axis, n, x_ref, out_ref, local_sem, send_sem, recv_sem):
    me = lax.axis_index(axis)
    own_exp = lax.axis_index("exp")
    own_hid = lax.axis_index("hid")
    mesh_ids = pl.DeviceIdType.MESH
    where = lambda peer: (peer, own_hid) if axis == "exp" else (own_exp, peer)
    barrier = pltpu.get_barrier_semaphore()
    for k in range(1, n):
        peer = lax.rem(me + k, n)
        pl.semaphore_signal(barrier, inc=1, device_id=where(peer), device_id_type=mesh_ids)
    pl.semaphore_wait(barrier, n - 1)
    local = pltpu.make_async_copy(x_ref.at[me], out_ref.at[me], local_sem)
    local.start()
    copies = []
    for k in range(1, n):
        peer = lax.rem(me + k, n)
        copy = pltpu.make_async_remote_copy(
            src_ref=x_ref.at[peer],
            dst_ref=out_ref.at[me],
            send_sem=send_sem.at[k],
            recv_sem=recv_sem.at[k],
            device_id=where(peer),
            device_id_type=mesh_ids,
        )
        copy.start()
        copies.append(copy)
    local.wait()
    for copy in copies:
        copy.wait()


def exchange(chunks, axis, kernel_id):
    n = chunks.shape[0]
    return pl.pallas_call(
        functools.partial(exchange_kernel, axis, n),
        out_shape=jax.ShapeDtypeStruct(chunks.shape, chunks.dtype),
        in_specs=[pl.BlockSpec(memory_space=pltpu.VMEM)],
        out_specs=pl.BlockSpec(memory_space=pltpu.VMEM),
        scratch_shapes=[
            pltpu.SemaphoreType.DMA,
            pltpu.SemaphoreType.DMA((n,)),
            pltpu.SemaphoreType.DMA((n,)),
        ],
        compiler_params=pltpu.CompilerParams(collective_id=kernel_id, has_side_effects=True),
    )(chunks)


def hid_gather(block, kernel_id=0):
    n = lax.axis_size("hid")
    return pl.pallas_call(
        functools.partial(hid_gather_kernel, n),
        out_shape=jax.ShapeDtypeStruct((n * block.shape[0],) + block.shape[1:], block.dtype),
        in_specs=[pl.BlockSpec(memory_space=pltpu.VMEM)],
        out_specs=pl.BlockSpec(memory_space=pltpu.VMEM),
        scratch_shapes=[
            pltpu.SemaphoreType.DMA,
            pltpu.SemaphoreType.DMA((n,)),
            pltpu.SemaphoreType.DMA((n,)),
        ],
        compiler_params=pltpu.CompilerParams(collective_id=kernel_id, has_side_effects=True),
    )(block)


def softmax_rows(values):
    top_val = jnp.max(values, axis=-1, keepdims=True)
    raised = jnp.exp(values - top_val)
    return raised / jnp.sum(raised, axis=-1, keepdims=True)


def combine_table(logits, chosen, expert_count):
    picked = jnp.take_along_axis(logits, chosen, axis=1)
    weights = softmax_rows(picked)
    expert_ids = jnp.arange(expert_count, dtype=jnp.int32)
    matched = (chosen[:, :, None] == expert_ids[None, None, :]).astype(jnp.float32)
    return jnp.sum(weights[:, :, None] * matched, axis=1).astype(jnp.bfloat16)


CAP = 4


def slot_rows(column, group_rows):
    shaped = column.reshape(column.shape[:-1] + (-1, group_rows))
    place = jnp.arange(group_rows, dtype=jnp.int32)
    key = jnp.where(shaped != 0, 2 * group_rows - place, -place)
    return lax.top_k(key, CAP)[1]


def split3(value):
    hi = value.astype(jnp.bfloat16)
    rest = value - hi.astype(jnp.float32)
    mid = rest.astype(jnp.bfloat16)
    lo = (rest - mid.astype(jnp.float32)).astype(jnp.bfloat16)
    return jnp.concatenate([hi, mid, lo], axis=-1)


def join3(pieces, width):
    part = lambda i: pieces[..., i * width : (i + 1) * width].astype(jnp.float32)
    return (part(0) + part(1)) + part(2)


def pick_rows(choice, value):
    hi = value.astype(jnp.bfloat16)
    rest = value - hi.astype(jnp.float32)
    mid = rest.astype(jnp.bfloat16)
    lo = (rest - mid.astype(jnp.float32)).astype(jnp.bfloat16)
    dot = lambda piece: jnp.dot(choice, piece, preferred_element_type=jnp.float32)
    return (dot(hi) + dot(mid)) + dot(lo)


def dense_kernel(rows_ref, x_ref, g_ref, wg_ref, wu_ref, wd_ref, score_ref, gate_ref, up_ref, back_ref):
    step = pl.program_id(0)
    x = x_ref[...]
    gate_pre = jnp.dot(x, wg_ref[...], preferred_element_type=jnp.float32)
    up_pre = jnp.dot(x, wu_ref[...], preferred_element_type=jnp.float32)
    back_grad = lax.dot_general(
        g_ref[...], wd_ref[...], (((1,), (1,)), ((), ())), preferred_element_type=jnp.float32
    )
    sig_gate = 1.0 / (1.0 + jnp.exp(-gate_pre))
    score_ref[...] = jnp.sum(gate_pre * sig_gate * up_pre * back_grad, axis=1, keepdims=True)
    tile = x.shape[0]
    place = step * tile + lax.broadcasted_iota(jnp.int32, (1, tile), 1)
    choice = (rows_ref[...] == place).astype(jnp.bfloat16)

    @pl.when(step == 0)
    def _():
        gate_ref[...] = jnp.zeros_like(gate_ref)
        up_ref[...] = jnp.zeros_like(up_ref)
        back_ref[...] = jnp.zeros_like(back_ref)

    gate_ref[...] += pick_rows(choice, gate_pre)
    up_ref[...] += pick_rows(choice, up_pre)
    back_ref[...] += pick_rows(choice, back_grad)


def dense_unit(gathered, rows, gate_w, up_w, down_w, tile=256):
    tokens_n = gathered.shape[0]
    width, hidden = gate_w.shape
    slots = rows.shape[0]
    tiles = lambda i: (i, 0)
    fixed = lambda i: (0, 0)
    f32 = jnp.float32
    return pl.pallas_call(
        dense_kernel,
        grid=(tokens_n // tile,),
        out_shape=[
            jax.ShapeDtypeStruct((tokens_n, 1), f32),
            jax.ShapeDtypeStruct((slots, hidden), f32),
            jax.ShapeDtypeStruct((slots, hidden), f32),
            jax.ShapeDtypeStruct((slots, hidden), f32),
        ],
        in_specs=[
            pl.BlockSpec((slots, 1), fixed),
            pl.BlockSpec((tile, width), tiles),
            pl.BlockSpec((tile, width), lambda i: (i, 1)),
            pl.BlockSpec((width, hidden), fixed),
            pl.BlockSpec((width, hidden), fixed),
            pl.BlockSpec((hidden, width), fixed),
        ],
        out_specs=[
            pl.BlockSpec((tile, 1), tiles),
            pl.BlockSpec((slots, hidden), fixed),
            pl.BlockSpec((slots, hidden), fixed),
            pl.BlockSpec((slots, hidden), fixed),
        ],
    )(rows.reshape(slots, 1), gathered, gathered, gate_w, up_w, down_w)


def chosen_rows(column, group_rows):
    picked = slot_rows(column, group_rows)
    starts = (jnp.arange(picked.shape[1], dtype=jnp.int32) * group_rows)[None, :, None]
    return (picked + starts).reshape(picked.shape[0], -1)


def sparse_terms(gate_s, up_s, back_s, rows, column, w_gate, w_up):
    col_s = jnp.take_along_axis(column, rows, axis=1)
    sig_gate = jax.nn.sigmoid(gate_s)
    act_gate = gate_s * sig_gate
    weighted = col_s[:, :, None] * back_s
    grad_gate = (weighted * up_s * sig_gate * (1.0 + gate_s * (1.0 - sig_gate))).astype(jnp.bfloat16)
    grad_up = (weighted * act_gate).astype(jnp.bfloat16)
    part = jnp.einsum("usf,udf->usd", grad_gate, w_gate, preferred_element_type=jnp.float32)
    part = part + jnp.einsum("usf,udf->usd", grad_up, w_up, preferred_element_type=jnp.float32)
    return part.reshape(part.shape[0], -1, CAP, part.shape[-1])


def on_device(tokens, grad_out, router_logits, selected, router_w, w_gate, w_up, w_down):
    tok_local, model_width = tokens.shape
    unit_count = w_gate.shape[0]
    expert_count = router_logits.shape[1]
    spread_exp = lax.axis_size("exp")
    spread_hid = lax.axis_size("hid")
    group_rows = spread_hid * tok_local
    own_exp = lax.axis_index("exp")
    own_hid = lax.axis_index("hid")
    own_block = lax.axis_index(("exp", "hid"))
    unit_expert = (own_block * unit_count + jnp.arange(unit_count, dtype=jnp.int32)) // 2
    expert_ids = jnp.arange(expert_count, dtype=jnp.int32)
    unit_pick = (expert_ids[:, None] == unit_expert[None, :]).astype(jnp.bfloat16)
    combine = combine_table(router_logits, selected, expert_count)
    packed = jnp.concatenate([tokens, grad_out, combine], axis=1)
    gathered = lax.all_gather(hid_gather(packed), "exp", axis=0, tiled=True)
    combine_all = gathered[:, 2 * model_width :]
    column = jnp.dot(combine_all, unit_pick, preferred_element_type=jnp.float32).T
    rows = chosen_rows(column, group_rows)
    dense = [dense_unit(gathered, rows[i], w_gate[i], w_up[i], w_down[i]) for i in range(unit_count)]
    score_part = jnp.concatenate([d[0] for d in dense], axis=1)
    gate_s, up_s, back_s = (jnp.stack([d[j] for d in dense]) for j in (1, 2, 3))
    part = sparse_terms(gate_s, up_s, back_s, rows, column, w_gate, w_up)
    lane = 128
    score_grp = jnp.swapaxes(score_part.T.reshape(unit_count, spread_exp, CAP, group_rows // CAP), 0, 1)
    score_grp = split3(score_grp)
    score_grp = jnp.pad(score_grp, ((0, 0), (0, 0), (0, 0), (0, lane - score_grp.shape[3])))
    sent = jnp.concatenate([jnp.swapaxes(part, 0, 1).astype(jnp.bfloat16), score_grp], axis=3)
    arrived_part = exchange(sent, "exp", 1)
    sender_block = (jnp.arange(spread_exp, dtype=jnp.int32) * spread_hid + own_hid)[:, None]
    sender_expert = (sender_block * unit_count + jnp.arange(unit_count, dtype=jnp.int32)[None, :]) // 2
    own_combine = lax.dynamic_slice_in_dim(combine_all, own_exp * group_rows, group_rows, 0)
    sender_pick = (expert_ids[:, None] == sender_expert.reshape(1, -1)).astype(jnp.bfloat16)
    sender_column = jnp.dot(own_combine, sender_pick, preferred_element_type=jnp.float32).T
    sender_rows = slot_rows(sender_column, group_rows).reshape(-1)
    place = (sender_rows[:, None] == jnp.arange(group_rows, dtype=jnp.int32)[None, :]).astype(jnp.bfloat16)
    group_sum = jnp.einsum(
        "sj,sd->jd", place, arrived_part[..., :model_width].reshape(-1, model_width),
        preferred_element_type=jnp.float32,
    )
    got_scores = join3(arrived_part[..., model_width:], group_rows // CAP)
    got_scores = got_scores.reshape(spread_exp, unit_count, spread_hid, tok_local)
    score_cols = spread_exp * unit_count
    hid_scores = jnp.transpose(got_scores, (2, 3, 0, 1)).reshape(spread_hid, tok_local, score_cols)
    hid_scores = split3(hid_scores)
    score_width = -(-hid_scores.shape[2] // lane) * lane
    hid_scores = jnp.pad(hid_scores, ((0, 0), (0, 0), (0, score_width - hid_scores.shape[2])))
    hid_sent = jnp.concatenate(
        [group_sum.reshape(spread_hid, tok_local, model_width).astype(jnp.bfloat16), hid_scores], axis=2
    )
    spread_rows = exchange(hid_sent, "hid", 2)
    input_sum = jnp.sum(spread_rows[..., :model_width].astype(jnp.float32), axis=0)
    own_scores = join3(spread_rows[..., model_width:], score_cols)
    own_scores = own_scores.reshape(spread_hid, tok_local, spread_exp, unit_count)
    unit_scores = jnp.transpose(own_scores, (1, 2, 0, 3)).reshape(tok_local, -1)
    expert_scores = jnp.sum(unit_scores.reshape(tok_local, expert_count, 2), axis=2)
    probs_all = softmax_rows(router_logits)
    mean_score = jnp.sum(probs_all * expert_scores, axis=1, keepdims=True)
    logit_grad = (probs_all * (expert_scores - mean_score)).astype(jnp.bfloat16)
    devices = spread_exp * spread_hid
    near_logit = hid_gather(logit_grad, 3)
    logit_all = exchange(
        jnp.broadcast_to(near_logit[None], (spread_exp,) + near_logit.shape), "exp", 4
    ).reshape(-1, expert_count)
    grad_rows = model_width // devices
    token_cols = lax.dynamic_slice_in_dim(gathered, own_block * grad_rows, grad_rows, 1)
    router_grad = jnp.einsum("tc,te->ce", token_cols, logit_all, preferred_element_type=jnp.float32)
    router_part = jnp.einsum("te,de->td", logit_grad, router_w, preferred_element_type=jnp.float32)
    x_grad = (input_sum + router_part).astype(jnp.bfloat16)
    return (x_grad, router_grad)


def solution(mesh):
    placed = (
        P(("exp", "hid"), None),
        P(("exp", "hid"), None),
        P(("exp", "hid"), None),
        P(("exp", "hid"), None),
        P(),
        P(("exp", "hid"), None, None),
        P(("exp", "hid"), None, None),
        P(("exp", "hid"), None, None),
    )
    return jax.shard_map(
        on_device,
        mesh=mesh,
        in_specs=placed,
        out_specs=(P(("exp", "hid"), None), P(("exp", "hid"), None)),
        check_vma=False,
    )
```

```python
import functools
import jax
import jax.numpy as jnp
from jax import lax
from jax.sharding import PartitionSpec as P
from jax.experimental import pallas as pl
from jax.experimental.pallas import tpu as pltpu


def hid_gather_kernel(n, x_ref, out_ref, local_sem, send_sem, recv_sem):
    me = lax.axis_index("hid")
    rows = x_ref.shape[0]
    slot = out_ref.at[pl.ds(pl.multiple_of(me * rows, rows), rows)]
    row = lax.axis_index("exp")
    mesh_ids = pl.DeviceIdType.MESH
    barrier = pltpu.get_barrier_semaphore()
    for k in range(1, n):
        peer = lax.rem(me + k, n)
        pl.semaphore_signal(barrier, inc=1, device_id=(row, peer), device_id_type=mesh_ids)
    pl.semaphore_wait(barrier, n - 1)
    local = pltpu.make_async_copy(x_ref, slot, local_sem)
    local.start()
    copies = []
    for k in range(1, n):
        peer = lax.rem(me + k, n)
        copy = pltpu.make_async_remote_copy(
            src_ref=x_ref,
            dst_ref=slot,
            send_sem=send_sem.at[k],
            recv_sem=recv_sem.at[k],
            device_id=(row, peer),
            device_id_type=mesh_ids,
        )
        copy.start()
        copies.append(copy)
    local.wait()
    for copy in copies:
        copy.wait()


def exchange_kernel(axis, n, x_ref, out_ref, local_sem, send_sem, recv_sem):
    me = lax.axis_index(axis)
    own_exp = lax.axis_index("exp")
    own_hid = lax.axis_index("hid")
    mesh_ids = pl.DeviceIdType.MESH
    where = lambda peer: (peer, own_hid) if axis == "exp" else (own_exp, peer)
    barrier = pltpu.get_barrier_semaphore()
    for k in range(1, n):
        peer = lax.rem(me + k, n)
        pl.semaphore_signal(barrier, inc=1, device_id=where(peer), device_id_type=mesh_ids)
    pl.semaphore_wait(barrier, n - 1)
    local = pltpu.make_async_copy(x_ref.at[me], out_ref.at[me], local_sem)
    local.start()
    copies = []
    for k in range(1, n):
        peer = lax.rem(me + k, n)
        copy = pltpu.make_async_remote_copy(
            src_ref=x_ref.at[peer],
            dst_ref=out_ref.at[me],
            send_sem=send_sem.at[k],
            recv_sem=recv_sem.at[k],
            device_id=where(peer),
            device_id_type=mesh_ids,
        )
        copy.start()
        copies.append(copy)
    local.wait()
    for copy in copies:
        copy.wait()


def exchange(chunks, axis, kernel_id):
    n = chunks.shape[0]
    return pl.pallas_call(
        functools.partial(exchange_kernel, axis, n),
        out_shape=jax.ShapeDtypeStruct(chunks.shape, chunks.dtype),
        in_specs=[pl.BlockSpec(memory_space=pltpu.VMEM)],
        out_specs=pl.BlockSpec(memory_space=pltpu.VMEM),
        scratch_shapes=[
            pltpu.SemaphoreType.DMA,
            pltpu.SemaphoreType.DMA((n,)),
            pltpu.SemaphoreType.DMA((n,)),
        ],
        compiler_params=pltpu.CompilerParams(collective_id=kernel_id, has_side_effects=True),
    )(chunks)


def hid_gather(block):
    n = lax.axis_size("hid")
    return pl.pallas_call(
        functools.partial(hid_gather_kernel, n),
        out_shape=jax.ShapeDtypeStruct((n * block.shape[0],) + block.shape[1:], block.dtype),
        in_specs=[pl.BlockSpec(memory_space=pltpu.VMEM)],
        out_specs=pl.BlockSpec(memory_space=pltpu.VMEM),
        scratch_shapes=[
            pltpu.SemaphoreType.DMA,
            pltpu.SemaphoreType.DMA((n,)),
            pltpu.SemaphoreType.DMA((n,)),
        ],
        compiler_params=pltpu.CompilerParams(collective_id=0, has_side_effects=True),
    )(block)


def softmax_rows(values):
    top_val = jnp.max(values, axis=-1, keepdims=True)
    raised = jnp.exp(values - top_val)
    return raised / jnp.sum(raised, axis=-1, keepdims=True)


def combine_table(logits, chosen, expert_count):
    picked = jnp.take_along_axis(logits, chosen, axis=1)
    weights = softmax_rows(picked)
    expert_ids = jnp.arange(expert_count, dtype=jnp.int32)
    matched = (chosen[:, :, None] == expert_ids[None, None, :]).astype(jnp.float32)
    return jnp.sum(weights[:, :, None] * matched, axis=1).astype(jnp.bfloat16)


CAP = 4


def slot_rows(column, group_rows):
    shaped = column.reshape(column.shape[:-1] + (-1, group_rows))
    place = jnp.arange(group_rows, dtype=jnp.int32)
    key = jnp.where(shaped != 0, 2 * group_rows - place, -place)
    return lax.top_k(key, CAP)[1]


def split3(value):
    hi = value.astype(jnp.bfloat16)
    rest = value - hi.astype(jnp.float32)
    mid = rest.astype(jnp.bfloat16)
    lo = (rest - mid.astype(jnp.float32)).astype(jnp.bfloat16)
    return jnp.concatenate([hi, mid, lo], axis=-1)


def join3(pieces, width):
    part = lambda i: pieces[..., i * width : (i + 1) * width].astype(jnp.float32)
    return (part(0) + part(1)) + part(2)


def pick_rows(choice, value):
    hi = value.astype(jnp.bfloat16)
    rest = value - hi.astype(jnp.float32)
    mid = rest.astype(jnp.bfloat16)
    lo = (rest - mid.astype(jnp.float32)).astype(jnp.bfloat16)
    dot = lambda piece: jnp.dot(choice, piece, preferred_element_type=jnp.float32)
    return (dot(hi) + dot(mid)) + dot(lo)


def dense_kernel(rows_ref, x_ref, g_ref, wg_ref, wu_ref, wd_ref, score_ref, gate_ref, up_ref, back_ref):
    step = pl.program_id(0)
    x = x_ref[...]
    gate_pre = jnp.dot(x, wg_ref[...], preferred_element_type=jnp.float32)
    up_pre = jnp.dot(x, wu_ref[...], preferred_element_type=jnp.float32)
    back_grad = lax.dot_general(
        g_ref[...], wd_ref[...], (((1,), (1,)), ((), ())), preferred_element_type=jnp.float32
    )
    sig_gate = 1.0 / (1.0 + jnp.exp(-gate_pre))
    score_ref[...] = jnp.sum(gate_pre * sig_gate * up_pre * back_grad, axis=1, keepdims=True)
    tile = x.shape[0]
    place = step * tile + lax.broadcasted_iota(jnp.int32, (1, tile), 1)
    choice = (rows_ref[...] == place).astype(jnp.bfloat16)

    @pl.when(step == 0)
    def _():
        gate_ref[...] = jnp.zeros_like(gate_ref)
        up_ref[...] = jnp.zeros_like(up_ref)
        back_ref[...] = jnp.zeros_like(back_ref)

    gate_ref[...] += pick_rows(choice, gate_pre)
    up_ref[...] += pick_rows(choice, up_pre)
    back_ref[...] += pick_rows(choice, back_grad)


def dense_unit(gathered, rows, gate_w, up_w, down_w, tile=256):
    tokens_n = gathered.shape[0]
    width, hidden = gate_w.shape
    slots = rows.shape[0]
    tiles = lambda i: (i, 0)
    fixed = lambda i: (0, 0)
    f32 = jnp.float32
    return pl.pallas_call(
        dense_kernel,
        grid=(tokens_n // tile,),
        out_shape=[
            jax.ShapeDtypeStruct((tokens_n, 1), f32),
            jax.ShapeDtypeStruct((slots, hidden), f32),
            jax.ShapeDtypeStruct((slots, hidden), f32),
            jax.ShapeDtypeStruct((slots, hidden), f32),
        ],
        in_specs=[
            pl.BlockSpec((slots, 1), fixed),
            pl.BlockSpec((tile, width), tiles),
            pl.BlockSpec((tile, width), lambda i: (i, 1)),
            pl.BlockSpec((width, hidden), fixed),
            pl.BlockSpec((width, hidden), fixed),
            pl.BlockSpec((hidden, width), fixed),
        ],
        out_specs=[
            pl.BlockSpec((tile, 1), tiles),
            pl.BlockSpec((slots, hidden), fixed),
            pl.BlockSpec((slots, hidden), fixed),
            pl.BlockSpec((slots, hidden), fixed),
        ],
    )(rows.reshape(slots, 1), gathered, gathered, gate_w, up_w, down_w)


def chosen_rows(column, group_rows):
    picked = slot_rows(column, group_rows)
    starts = (jnp.arange(picked.shape[1], dtype=jnp.int32) * group_rows)[None, :, None]
    return (picked + starts).reshape(picked.shape[0], -1)


def sparse_terms(gate_s, up_s, back_s, rows, column, w_gate, w_up):
    col_s = jnp.take_along_axis(column, rows, axis=1)
    sig_gate = jax.nn.sigmoid(gate_s)
    act_gate = gate_s * sig_gate
    weighted = col_s[:, :, None] * back_s
    grad_gate = (weighted * up_s * sig_gate * (1.0 + gate_s * (1.0 - sig_gate))).astype(jnp.bfloat16)
    grad_up = (weighted * act_gate).astype(jnp.bfloat16)
    part = jnp.einsum("usf,udf->usd", grad_gate, w_gate, preferred_element_type=jnp.float32)
    part = part + jnp.einsum("usf,udf->usd", grad_up, w_up, preferred_element_type=jnp.float32)
    return part.reshape(part.shape[0], -1, CAP, part.shape[-1])


def on_device(tokens, grad_out, router_logits, selected, router_w, w_gate, w_up, w_down):
    tok_local, model_width = tokens.shape
    unit_count = w_gate.shape[0]
    expert_count = router_logits.shape[1]
    spread_exp = lax.axis_size("exp")
    spread_hid = lax.axis_size("hid")
    group_rows = spread_hid * tok_local
    own_exp = lax.axis_index("exp")
    own_hid = lax.axis_index("hid")
    own_block = lax.axis_index(("exp", "hid"))
    unit_expert = (own_block * unit_count + jnp.arange(unit_count, dtype=jnp.int32)) // 2
    expert_ids = jnp.arange(expert_count, dtype=jnp.int32)
    unit_pick = (expert_ids[:, None] == unit_expert[None, :]).astype(jnp.bfloat16)
    combine = combine_table(router_logits, selected, expert_count)
    packed = jnp.concatenate([tokens, grad_out, combine], axis=1)
    near = hid_gather(packed)
    gathered = lax.all_gather(near, "exp", axis=0, tiled=True)
    combine_all = gathered[:, 2 * model_width :]
    column = jnp.dot(combine_all, unit_pick, preferred_element_type=jnp.float32).T
    rows = chosen_rows(column, group_rows)
    dense = [dense_unit(gathered, rows[i], w_gate[i], w_up[i], w_down[i]) for i in range(unit_count)]
    score_part = jnp.concatenate([d[0] for d in dense], axis=1)
    gate_s, up_s, back_s = (jnp.stack([d[j] for d in dense]) for j in (1, 2, 3))
    part = sparse_terms(gate_s, up_s, back_s, rows, column, w_gate, w_up)
    lane = 128
    score_grp = jnp.swapaxes(score_part.T.reshape(unit_count, spread_exp, CAP, group_rows // CAP), 0, 1)
    score_grp = split3(score_grp)
    score_grp = jnp.pad(score_grp, ((0, 0), (0, 0), (0, 0), (0, lane - score_grp.shape[3])))
    sent = jnp.concatenate([jnp.swapaxes(part, 0, 1).astype(jnp.bfloat16), score_grp], axis=3)
    arrived_part = exchange(sent, "exp", 1)
    sender_block = (jnp.arange(spread_exp, dtype=jnp.int32) * spread_hid + own_hid)[:, None]
    sender_expert = (sender_block * unit_count + jnp.arange(unit_count, dtype=jnp.int32)[None, :]) // 2
    own_combine = near[:, 2 * model_width :]
    sender_pick = (expert_ids[:, None] == sender_expert.reshape(1, -1)).astype(jnp.bfloat16)
    sender_column = jnp.dot(own_combine, sender_pick, preferred_element_type=jnp.float32).T
    sender_rows = slot_rows(sender_column, group_rows).reshape(-1)
    place = (sender_rows[:, None] == jnp.arange(group_rows, dtype=jnp.int32)[None, :]).astype(jnp.bfloat16)
    group_sum = jnp.einsum(
        "sj,sd->jd", place, arrived_part[..., :model_width].reshape(-1, model_width),
        preferred_element_type=jnp.float32,
    )
    got_scores = join3(arrived_part[..., model_width:], group_rows // CAP)
    got_scores = got_scores.reshape(spread_exp, unit_count, spread_hid, tok_local)
    score_cols = spread_exp * unit_count
    hid_scores = jnp.transpose(got_scores, (2, 3, 0, 1)).reshape(spread_hid, tok_local, score_cols)
    hid_scores = split3(hid_scores)
    score_width = -(-hid_scores.shape[2] // lane) * lane
    hid_scores = jnp.pad(hid_scores, ((0, 0), (0, 0), (0, score_width - hid_scores.shape[2])))
    hid_sent = jnp.concatenate(
        [group_sum.reshape(spread_hid, tok_local, model_width).astype(jnp.bfloat16), hid_scores], axis=2
    )
    spread_rows = exchange(hid_sent, "hid", 2)
    input_sum = jnp.sum(spread_rows[..., :model_width].astype(jnp.float32), axis=0)
    own_scores = join3(spread_rows[..., model_width:], score_cols)
    own_scores = own_scores.reshape(spread_hid, tok_local, spread_exp, unit_count)
    unit_scores = jnp.transpose(own_scores, (1, 2, 0, 3)).reshape(tok_local, -1)
    expert_scores = jnp.sum(unit_scores.reshape(tok_local, expert_count, 2), axis=2)
    probs_all = softmax_rows(router_logits)
    mean_score = jnp.sum(probs_all * expert_scores, axis=1, keepdims=True)
    logit_grad = (probs_all * (expert_scores - mean_score)).astype(jnp.bfloat16)
    devices = spread_exp * spread_hid
    logit_all = lax.all_to_all(
        jnp.broadcast_to(logit_grad[None], (devices,) + logit_grad.shape), ("exp", "hid"), 0, 0, tiled=True
    ).reshape(-1, expert_count)
    grad_rows = model_width // devices
    token_cols = lax.dynamic_slice_in_dim(gathered, own_block * grad_rows, grad_rows, 1)
    router_grad = jnp.einsum("tc,te->ce", token_cols, logit_all, preferred_element_type=jnp.float32)
    router_part = jnp.einsum("te,de->td", logit_grad, router_w, preferred_element_type=jnp.float32)
    x_grad = (input_sum + router_part).astype(jnp.bfloat16)
    return (x_grad, router_grad)


def solution(mesh):
    placed = (
        P(("exp", "hid"), None),
        P(("exp", "hid"), None),
        P(("exp", "hid"), None),
        P(("exp", "hid"), None),
        P(),
        P(("exp", "hid"), None, None),
        P(("exp", "hid"), None, None),
        P(("exp", "hid"), None, None),
    )
    return jax.shard_map(
        on_device,
        mesh=mesh,
        in_specs=placed,
        out_specs=(P(("exp", "hid"), None), P(("exp", "hid"), None)),
        check_vma=False,
    )
```

```python
import functools
import jax
import jax.numpy as jnp
from jax import lax
from jax.sharding import PartitionSpec as P
from jax.experimental import pallas as pl
from jax.experimental.pallas import tpu as pltpu


def hid_gather_kernel(n, x_ref, out_ref, local_sem, send_sem, recv_sem):
    me = lax.axis_index("hid")
    rows = x_ref.shape[0]
    slot = out_ref.at[pl.ds(pl.multiple_of(me * rows, rows), rows)]
    row = lax.axis_index("exp")
    mesh_ids = pl.DeviceIdType.MESH
    barrier = pltpu.get_barrier_semaphore()
    for k in range(1, n):
        peer = lax.rem(me + k, n)
        pl.semaphore_signal(barrier, inc=1, device_id=(row, peer), device_id_type=mesh_ids)
    pl.semaphore_wait(barrier, n - 1)
    local = pltpu.make_async_copy(x_ref, slot, local_sem)
    local.start()
    copies = []
    for k in range(1, n):
        peer = lax.rem(me + k, n)
        copy = pltpu.make_async_remote_copy(
            src_ref=x_ref,
            dst_ref=slot,
            send_sem=send_sem.at[k],
            recv_sem=recv_sem.at[k],
            device_id=(row, peer),
            device_id_type=mesh_ids,
        )
        copy.start()
        copies.append(copy)
    local.wait()
    for copy in copies:
        copy.wait()


def exchange_kernel(axis, n, x_ref, out_ref, local_sem, send_sem, recv_sem):
    me = lax.axis_index(axis)
    own_exp = lax.axis_index("exp")
    own_hid = lax.axis_index("hid")
    mesh_ids = pl.DeviceIdType.MESH
    where = lambda peer: (peer, own_hid) if axis == "exp" else (own_exp, peer)
    barrier = pltpu.get_barrier_semaphore()
    for k in range(1, n):
        peer = lax.rem(me + k, n)
        pl.semaphore_signal(barrier, inc=1, device_id=where(peer), device_id_type=mesh_ids)
    pl.semaphore_wait(barrier, n - 1)
    local = pltpu.make_async_copy(x_ref.at[me], out_ref.at[me], local_sem)
    local.start()
    copies = []
    for k in range(1, n):
        peer = lax.rem(me + k, n)
        copy = pltpu.make_async_remote_copy(
            src_ref=x_ref.at[peer],
            dst_ref=out_ref.at[me],
            send_sem=send_sem.at[k],
            recv_sem=recv_sem.at[k],
            device_id=where(peer),
            device_id_type=mesh_ids,
        )
        copy.start()
        copies.append(copy)
    local.wait()
    for copy in copies:
        copy.wait()


def exchange(chunks, axis, kernel_id):
    n = chunks.shape[0]
    return pl.pallas_call(
        functools.partial(exchange_kernel, axis, n),
        out_shape=jax.ShapeDtypeStruct(chunks.shape, chunks.dtype),
        in_specs=[pl.BlockSpec(memory_space=pltpu.VMEM)],
        out_specs=pl.BlockSpec(memory_space=pltpu.VMEM),
        scratch_shapes=[
            pltpu.SemaphoreType.DMA,
            pltpu.SemaphoreType.DMA((n,)),
            pltpu.SemaphoreType.DMA((n,)),
        ],
        compiler_params=pltpu.CompilerParams(collective_id=kernel_id, has_side_effects=True),
    )(chunks)


def hid_gather(block):
    n = lax.axis_size("hid")
    return pl.pallas_call(
        functools.partial(hid_gather_kernel, n),
        out_shape=jax.ShapeDtypeStruct((n * block.shape[0],) + block.shape[1:], block.dtype),
        in_specs=[pl.BlockSpec(memory_space=pltpu.VMEM)],
        out_specs=pl.BlockSpec(memory_space=pltpu.VMEM),
        scratch_shapes=[
            pltpu.SemaphoreType.DMA,
            pltpu.SemaphoreType.DMA((n,)),
            pltpu.SemaphoreType.DMA((n,)),
        ],
        compiler_params=pltpu.CompilerParams(collective_id=0, has_side_effects=True),
    )(block)


def softmax_rows(values):
    top_val = jnp.max(values, axis=-1, keepdims=True)
    raised = jnp.exp(values - top_val)
    return raised / jnp.sum(raised, axis=-1, keepdims=True)


def combine_table(logits, chosen, expert_count):
    expert_ids = jnp.arange(expert_count, dtype=jnp.int32)
    matched = chosen[:, :, None] == expert_ids[None, None, :]
    picked = jnp.sum(jnp.where(matched, logits[:, None, :], 0.0), axis=2)
    weights = softmax_rows(picked)
    return jnp.sum(weights[:, :, None] * matched.astype(jnp.float32), axis=1).astype(jnp.bfloat16)


CAP = 4


def slot_rows(column, group_rows):
    shaped = column.reshape(column.shape[:-1] + (-1, group_rows))
    place = jnp.arange(group_rows, dtype=jnp.int32)
    key = jnp.where(shaped != 0, 2 * group_rows - place, -place)
    return lax.top_k(key, CAP)[1]


def split3(value):
    hi = value.astype(jnp.bfloat16)
    rest = value - hi.astype(jnp.float32)
    mid = rest.astype(jnp.bfloat16)
    lo = (rest - mid.astype(jnp.float32)).astype(jnp.bfloat16)
    return jnp.concatenate([hi, mid, lo], axis=-1)


def join3(pieces, width):
    part = lambda i: pieces[..., i * width : (i + 1) * width].astype(jnp.float32)
    return (part(0) + part(1)) + part(2)


def pick_rows(choice, value):
    hi = value.astype(jnp.bfloat16)
    rest = value - hi.astype(jnp.float32)
    mid = rest.astype(jnp.bfloat16)
    lo = (rest - mid.astype(jnp.float32)).astype(jnp.bfloat16)
    dot = lambda piece: jnp.dot(choice, piece, preferred_element_type=jnp.float32)
    return (dot(hi) + dot(mid)) + dot(lo)


def dense_kernel(rows_ref, x_ref, g_ref, wg_ref, wu_ref, wd_ref, score_ref, gate_ref, up_ref, back_ref):
    step = pl.program_id(0)
    x = x_ref[...]
    gate_pre = jnp.dot(x, wg_ref[...], preferred_element_type=jnp.float32)
    up_pre = jnp.dot(x, wu_ref[...], preferred_element_type=jnp.float32)
    back_grad = lax.dot_general(
        g_ref[...], wd_ref[...], (((1,), (1,)), ((), ())), preferred_element_type=jnp.float32
    )
    sig_gate = 1.0 / (1.0 + jnp.exp(-gate_pre))
    score_ref[...] = jnp.sum(gate_pre * sig_gate * up_pre * back_grad, axis=1, keepdims=True)
    tile = x.shape[0]
    place = step * tile + lax.broadcasted_iota(jnp.int32, (1, tile), 1)
    choice = (rows_ref[...] == place).astype(jnp.bfloat16)

    @pl.when(step == 0)
    def _():
        gate_ref[...] = jnp.zeros_like(gate_ref)
        up_ref[...] = jnp.zeros_like(up_ref)
        back_ref[...] = jnp.zeros_like(back_ref)

    gate_ref[...] += pick_rows(choice, gate_pre)
    up_ref[...] += pick_rows(choice, up_pre)
    back_ref[...] += pick_rows(choice, back_grad)


def dense_unit(gathered, rows, gate_w, up_w, down_w, tile=256):
    tokens_n = gathered.shape[0]
    width, hidden = gate_w.shape
    slots = rows.shape[0]
    tiles = lambda i: (i, 0)
    fixed = lambda i: (0, 0)
    f32 = jnp.float32
    return pl.pallas_call(
        dense_kernel,
        grid=(tokens_n // tile,),
        out_shape=[
            jax.ShapeDtypeStruct((tokens_n, 1), f32),
            jax.ShapeDtypeStruct((slots, hidden), f32),
            jax.ShapeDtypeStruct((slots, hidden), f32),
            jax.ShapeDtypeStruct((slots, hidden), f32),
        ],
        in_specs=[
            pl.BlockSpec((slots, 1), fixed),
            pl.BlockSpec((tile, width), tiles),
            pl.BlockSpec((tile, width), lambda i: (i, 1)),
            pl.BlockSpec((width, hidden), fixed),
            pl.BlockSpec((width, hidden), fixed),
            pl.BlockSpec((hidden, width), fixed),
        ],
        out_specs=[
            pl.BlockSpec((tile, 1), tiles),
            pl.BlockSpec((slots, hidden), fixed),
            pl.BlockSpec((slots, hidden), fixed),
            pl.BlockSpec((slots, hidden), fixed),
        ],
    )(rows.reshape(slots, 1), gathered, gathered, gate_w, up_w, down_w)


def chosen_rows(column, group_rows):
    picked = slot_rows(column, group_rows)
    starts = (jnp.arange(picked.shape[1], dtype=jnp.int32) * group_rows)[None, :, None]
    return (picked + starts).reshape(picked.shape[0], -1)


def sparse_terms(gate_s, up_s, back_s, rows, column, w_gate, w_up):
    col_s = jnp.take_along_axis(column, rows, axis=1)
    sig_gate = jax.nn.sigmoid(gate_s)
    act_gate = gate_s * sig_gate
    weighted = col_s[:, :, None] * back_s
    grad_gate = (weighted * up_s * sig_gate * (1.0 + gate_s * (1.0 - sig_gate))).astype(jnp.bfloat16)
    grad_up = (weighted * act_gate).astype(jnp.bfloat16)
    part = jnp.einsum("usf,udf->usd", grad_gate, w_gate, preferred_element_type=jnp.float32)
    part = part + jnp.einsum("usf,udf->usd", grad_up, w_up, preferred_element_type=jnp.float32)
    return part.reshape(part.shape[0], -1, CAP, part.shape[-1])


def on_device(tokens, grad_out, router_logits, selected, router_w, w_gate, w_up, w_down):
    tok_local, model_width = tokens.shape
    unit_count = w_gate.shape[0]
    expert_count = router_logits.shape[1]
    spread_exp = lax.axis_size("exp")
    spread_hid = lax.axis_size("hid")
    group_rows = spread_hid * tok_local
    own_exp = lax.axis_index("exp")
    own_hid = lax.axis_index("hid")
    own_block = lax.axis_index(("exp", "hid"))
    unit_expert = (own_block * unit_count + jnp.arange(unit_count, dtype=jnp.int32)) // 2
    expert_ids = jnp.arange(expert_count, dtype=jnp.int32)
    unit_pick = (expert_ids[:, None] == unit_expert[None, :]).astype(jnp.bfloat16)
    combine = combine_table(router_logits, selected, expert_count)
    packed = jnp.concatenate([tokens, grad_out, combine], axis=1)
    near = hid_gather(packed)
    gathered = lax.all_gather(near, "exp", axis=0, tiled=True)
    combine_all = gathered[:, 2 * model_width :]
    column = jnp.dot(combine_all, unit_pick, preferred_element_type=jnp.float32).T
    rows = chosen_rows(column, group_rows)
    dense = [dense_unit(gathered, rows[i], w_gate[i], w_up[i], w_down[i]) for i in range(unit_count)]
    score_part = jnp.concatenate([d[0] for d in dense], axis=1)
    gate_s, up_s, back_s = (jnp.stack([d[j] for d in dense]) for j in (1, 2, 3))
    part = sparse_terms(gate_s, up_s, back_s, rows, column, w_gate, w_up)
    lane = 128
    score_grp = jnp.swapaxes(score_part.T.reshape(unit_count, spread_exp, CAP, group_rows // CAP), 0, 1)
    score_grp = split3(score_grp)
    score_grp = jnp.pad(score_grp, ((0, 0), (0, 0), (0, 0), (0, lane - score_grp.shape[3])))
    sent = jnp.concatenate([jnp.swapaxes(part, 0, 1).astype(jnp.bfloat16), score_grp], axis=3)
    arrived_part = exchange(sent, "exp", 1)
    sender_block = (jnp.arange(spread_exp, dtype=jnp.int32) * spread_hid + own_hid)[:, None]
    sender_expert = (sender_block * unit_count + jnp.arange(unit_count, dtype=jnp.int32)[None, :]) // 2
    own_combine = near[:, 2 * model_width :]
    sender_pick = (expert_ids[:, None] == sender_expert.reshape(1, -1)).astype(jnp.bfloat16)
    sender_column = jnp.dot(own_combine, sender_pick, preferred_element_type=jnp.float32).T
    sender_rows = slot_rows(sender_column, group_rows).reshape(-1)
    place = (sender_rows[:, None] == jnp.arange(group_rows, dtype=jnp.int32)[None, :]).astype(jnp.bfloat16)
    group_sum = jnp.einsum(
        "sj,sd->jd", place, arrived_part[..., :model_width].reshape(-1, model_width),
        preferred_element_type=jnp.float32,
    )
    got_scores = join3(arrived_part[..., model_width:], group_rows // CAP)
    got_scores = got_scores.reshape(spread_exp, unit_count, spread_hid, tok_local)
    score_cols = spread_exp * unit_count
    hid_scores = jnp.transpose(got_scores, (2, 3, 0, 1)).reshape(spread_hid, tok_local, score_cols)
    hid_scores = split3(hid_scores)
    score_width = -(-hid_scores.shape[2] // lane) * lane
    hid_scores = jnp.pad(hid_scores, ((0, 0), (0, 0), (0, score_width - hid_scores.shape[2])))
    hid_sent = jnp.concatenate(
        [group_sum.reshape(spread_hid, tok_local, model_width).astype(jnp.bfloat16), hid_scores], axis=2
    )
    spread_rows = exchange(hid_sent, "hid", 2)
    input_sum = jnp.sum(spread_rows[..., :model_width].astype(jnp.float32), axis=0)
    own_scores = join3(spread_rows[..., model_width:], score_cols)
    own_scores = own_scores.reshape(spread_hid, tok_local, spread_exp, unit_count)
    unit_scores = jnp.transpose(own_scores, (1, 2, 0, 3)).reshape(tok_local, -1)
    expert_scores = jnp.sum(unit_scores.reshape(tok_local, expert_count, 2), axis=2)
    probs_all = softmax_rows(router_logits)
    mean_score = jnp.sum(probs_all * expert_scores, axis=1, keepdims=True)
    logit_grad = (probs_all * (expert_scores - mean_score)).astype(jnp.bfloat16)
    devices = spread_exp * spread_hid
    logit_all = lax.all_to_all(
        jnp.broadcast_to(logit_grad[None], (devices,) + logit_grad.shape), ("exp", "hid"), 0, 0, tiled=True
    ).reshape(-1, expert_count)
    grad_rows = model_width // devices
    token_cols = lax.dynamic_slice_in_dim(gathered, own_block * grad_rows, grad_rows, 1)
    router_grad = jnp.einsum("tc,te->ce", token_cols, logit_all, preferred_element_type=jnp.float32)
    router_part = jnp.einsum("te,de->td", logit_grad, router_w, preferred_element_type=jnp.float32)
    x_grad = (input_sum + router_part).astype(jnp.bfloat16)
    return (x_grad, router_grad)


def solution(mesh):
    placed = (
        P(("exp", "hid"), None),
        P(("exp", "hid"), None),
        P(("exp", "hid"), None),
        P(("exp", "hid"), None),
        P(),
        P(("exp", "hid"), None, None),
        P(("exp", "hid"), None, None),
        P(("exp", "hid"), None, None),
    )
    return jax.shard_map(
        on_device,
        mesh=mesh,
        in_specs=placed,
        out_specs=(P(("exp", "hid"), None), P(("exp", "hid"), None)),
        check_vma=False,
    )
```

```python
import functools
import jax
import jax.numpy as jnp
from jax import lax
from jax.sharding import PartitionSpec as P
from jax.experimental import pallas as pl
from jax.experimental.pallas import tpu as pltpu


def hid_gather_kernel(n, x_ref, out_ref, local_sem, send_sem, recv_sem):
    me = lax.axis_index("hid")
    rows = x_ref.shape[0]
    slot = out_ref.at[pl.ds(pl.multiple_of(me * rows, rows), rows)]
    row = lax.axis_index("exp")
    mesh_ids = pl.DeviceIdType.MESH
    barrier = pltpu.get_barrier_semaphore()
    for k in range(1, n):
        peer = lax.rem(me + k, n)
        pl.semaphore_signal(barrier, inc=1, device_id=(row, peer), device_id_type=mesh_ids)
    pl.semaphore_wait(barrier, n - 1)
    local = pltpu.make_async_copy(x_ref, slot, local_sem)
    local.start()
    copies = []
    for k in range(1, n):
        peer = lax.rem(me + k, n)
        copy = pltpu.make_async_remote_copy(
            src_ref=x_ref,
            dst_ref=slot,
            send_sem=send_sem.at[k],
            recv_sem=recv_sem.at[k],
            device_id=(row, peer),
            device_id_type=mesh_ids,
        )
        copy.start()
        copies.append(copy)
    local.wait()
    for copy in copies:
        copy.wait()


def exchange_kernel(axis, n, x_ref, out_ref, local_sem, send_sem, recv_sem):
    me = lax.axis_index(axis)
    own_exp = lax.axis_index("exp")
    own_hid = lax.axis_index("hid")
    mesh_ids = pl.DeviceIdType.MESH
    where = lambda peer: (peer, own_hid) if axis == "exp" else (own_exp, peer)
    barrier = pltpu.get_barrier_semaphore()
    for k in range(1, n):
        peer = lax.rem(me + k, n)
        pl.semaphore_signal(barrier, inc=1, device_id=where(peer), device_id_type=mesh_ids)
    pl.semaphore_wait(barrier, n - 1)
    local = pltpu.make_async_copy(x_ref.at[me], out_ref.at[me], local_sem)
    local.start()
    copies = []
    for k in range(1, n):
        peer = lax.rem(me + k, n)
        copy = pltpu.make_async_remote_copy(
            src_ref=x_ref.at[peer],
            dst_ref=out_ref.at[me],
            send_sem=send_sem.at[k],
            recv_sem=recv_sem.at[k],
            device_id=where(peer),
            device_id_type=mesh_ids,
        )
        copy.start()
        copies.append(copy)
    local.wait()
    for copy in copies:
        copy.wait()


def exchange(chunks, axis, kernel_id):
    n = chunks.shape[0]
    return pl.pallas_call(
        functools.partial(exchange_kernel, axis, n),
        out_shape=jax.ShapeDtypeStruct(chunks.shape, chunks.dtype),
        in_specs=[pl.BlockSpec(memory_space=pltpu.VMEM)],
        out_specs=pl.BlockSpec(memory_space=pltpu.VMEM),
        scratch_shapes=[
            pltpu.SemaphoreType.DMA,
            pltpu.SemaphoreType.DMA((n,)),
            pltpu.SemaphoreType.DMA((n,)),
        ],
        compiler_params=pltpu.CompilerParams(collective_id=kernel_id, has_side_effects=True),
    )(chunks)


def hid_gather(block):
    n = lax.axis_size("hid")
    return pl.pallas_call(
        functools.partial(hid_gather_kernel, n),
        out_shape=jax.ShapeDtypeStruct((n * block.shape[0],) + block.shape[1:], block.dtype),
        in_specs=[pl.BlockSpec(memory_space=pltpu.VMEM)],
        out_specs=pl.BlockSpec(memory_space=pltpu.VMEM),
        scratch_shapes=[
            pltpu.SemaphoreType.DMA,
            pltpu.SemaphoreType.DMA((n,)),
            pltpu.SemaphoreType.DMA((n,)),
        ],
        compiler_params=pltpu.CompilerParams(collective_id=0, has_side_effects=True),
    )(block)


def softmax_rows(values):
    top_val = jnp.max(values, axis=-1, keepdims=True)
    raised = jnp.exp(values - top_val)
    return raised / jnp.sum(raised, axis=-1, keepdims=True)


def combine_table(logits, chosen, expert_count):
    expert_ids = jnp.arange(expert_count, dtype=jnp.int32)
    matched = chosen[:, :, None] == expert_ids[None, None, :]
    picked = jnp.sum(jnp.where(matched, logits[:, None, :], 0.0), axis=2)
    weights = softmax_rows(picked)
    return jnp.sum(weights[:, :, None] * matched.astype(jnp.float32), axis=1).astype(jnp.bfloat16)


CAP = 4


def slot_rows(column, group_rows):
    shaped = column.reshape(column.shape[:-1] + (-1, group_rows))
    place = jnp.arange(group_rows, dtype=jnp.int32)
    key = jnp.where(shaped != 0, 2 * group_rows - place, -place)
    return lax.top_k(key, CAP)[1]


def split3(value):
    hi = value.astype(jnp.bfloat16)
    rest = value - hi.astype(jnp.float32)
    mid = rest.astype(jnp.bfloat16)
    lo = (rest - mid.astype(jnp.float32)).astype(jnp.bfloat16)
    return jnp.concatenate([hi, mid, lo], axis=-1)


def join3(pieces, width):
    part = lambda i: pieces[..., i * width : (i + 1) * width].astype(jnp.float32)
    return (part(0) + part(1)) + part(2)


def pick_rows(choice, value):
    hi = value.astype(jnp.bfloat16)
    rest = value - hi.astype(jnp.float32)
    mid = rest.astype(jnp.bfloat16)
    lo = (rest - mid.astype(jnp.float32)).astype(jnp.bfloat16)
    dot = lambda piece: jnp.dot(choice, piece, preferred_element_type=jnp.float32)
    return (dot(hi) + dot(mid)) + dot(lo)


def dense_kernel(rows_ref, x_ref, g_ref, wg_ref, wu_ref, wd_ref, score_ref, gate_ref, up_ref, back_ref):
    step = pl.program_id(0)
    x = x_ref[...]
    gate_pre = jnp.dot(x, wg_ref[...], preferred_element_type=jnp.float32)
    up_pre = jnp.dot(x, wu_ref[...], preferred_element_type=jnp.float32)
    back_grad = lax.dot_general(
        g_ref[...], wd_ref[...], (((1,), (1,)), ((), ())), preferred_element_type=jnp.float32
    )
    sig_gate = 1.0 / (1.0 + jnp.exp(-gate_pre))
    score_ref[...] = jnp.sum((gate_pre * sig_gate * up_pre * back_grad).T, axis=0, keepdims=True)
    tile = x.shape[0]
    place = step * tile + lax.broadcasted_iota(jnp.int32, (1, tile), 1)
    choice = (rows_ref[...] == place).astype(jnp.bfloat16)

    @pl.when(step == 0)
    def _():
        gate_ref[...] = jnp.zeros_like(gate_ref)
        up_ref[...] = jnp.zeros_like(up_ref)
        back_ref[...] = jnp.zeros_like(back_ref)

    gate_ref[...] += pick_rows(choice, gate_pre)
    up_ref[...] += pick_rows(choice, up_pre)
    back_ref[...] += pick_rows(choice, back_grad)


def dense_unit(gathered, rows, gate_w, up_w, down_w, tile=256):
    tokens_n = gathered.shape[0]
    width, hidden = gate_w.shape
    slots = rows.shape[0]
    tiles = lambda i: (i, 0)
    fixed = lambda i: (0, 0)
    f32 = jnp.float32
    return pl.pallas_call(
        dense_kernel,
        grid=(tokens_n // tile,),
        out_shape=[
            jax.ShapeDtypeStruct((1, tokens_n), f32),
            jax.ShapeDtypeStruct((slots, hidden), f32),
            jax.ShapeDtypeStruct((slots, hidden), f32),
            jax.ShapeDtypeStruct((slots, hidden), f32),
        ],
        in_specs=[
            pl.BlockSpec((slots, 1), fixed),
            pl.BlockSpec((tile, width), tiles),
            pl.BlockSpec((tile, width), lambda i: (i, 1)),
            pl.BlockSpec((width, hidden), fixed),
            pl.BlockSpec((width, hidden), fixed),
            pl.BlockSpec((hidden, width), fixed),
        ],
        out_specs=[
            pl.BlockSpec((1, tile), lambda i: (0, i)),
            pl.BlockSpec((slots, hidden), fixed),
            pl.BlockSpec((slots, hidden), fixed),
            pl.BlockSpec((slots, hidden), fixed),
        ],
    )(rows.reshape(slots, 1), gathered, gathered, gate_w, up_w, down_w)


def chosen_rows(column, group_rows):
    picked = slot_rows(column, group_rows)
    starts = (jnp.arange(picked.shape[1], dtype=jnp.int32) * group_rows)[None, :, None]
    return (picked + starts).reshape(picked.shape[0], -1)


def sparse_terms(gate_s, up_s, back_s, rows, column, w_gate, w_up):
    col_s = jnp.take_along_axis(column, rows, axis=1)
    sig_gate = jax.nn.sigmoid(gate_s)
    act_gate = gate_s * sig_gate
    weighted = col_s[:, :, None] * back_s
    grad_gate = (weighted * up_s * sig_gate * (1.0 + gate_s * (1.0 - sig_gate))).astype(jnp.bfloat16)
    grad_up = (weighted * act_gate).astype(jnp.bfloat16)
    part = jnp.einsum("usf,udf->usd", grad_gate, w_gate, preferred_element_type=jnp.float32)
    part = part + jnp.einsum("usf,udf->usd", grad_up, w_up, preferred_element_type=jnp.float32)
    return part.reshape(part.shape[0], -1, CAP, part.shape[-1])


def on_device(tokens, grad_out, router_logits, selected, router_w, w_gate, w_up, w_down):
    tok_local, model_width = tokens.shape
    unit_count = w_gate.shape[0]
    expert_count = router_logits.shape[1]
    spread_exp = lax.axis_size("exp")
    spread_hid = lax.axis_size("hid")
    group_rows = spread_hid * tok_local
    own_exp = lax.axis_index("exp")
    own_hid = lax.axis_index("hid")
    own_block = lax.axis_index(("exp", "hid"))
    unit_expert = (own_block * unit_count + jnp.arange(unit_count, dtype=jnp.int32)) // 2
    expert_ids = jnp.arange(expert_count, dtype=jnp.int32)
    unit_pick = (expert_ids[:, None] == unit_expert[None, :]).astype(jnp.bfloat16)
    combine = combine_table(router_logits, selected, expert_count)
    packed = jnp.concatenate([tokens, grad_out, combine], axis=1)
    near = hid_gather(packed)
    gathered = lax.all_gather(near, "exp", axis=0, tiled=True)
    combine_all = gathered[:, 2 * model_width :]
    column = jnp.dot(combine_all, unit_pick, preferred_element_type=jnp.float32).T
    rows = chosen_rows(column, group_rows)
    dense = [dense_unit(gathered, rows[i], w_gate[i], w_up[i], w_down[i]) for i in range(unit_count)]
    score_part = jnp.concatenate([d[0] for d in dense], axis=0).T
    gate_s, up_s, back_s = (jnp.stack([d[j] for d in dense]) for j in (1, 2, 3))
    part = sparse_terms(gate_s, up_s, back_s, rows, column, w_gate, w_up)
    lane = 128
    score_grp = jnp.swapaxes(score_part.T.reshape(unit_count, spread_exp, CAP, group_rows // CAP), 0, 1)
    score_grp = split3(score_grp)
    score_grp = jnp.pad(score_grp, ((0, 0), (0, 0), (0, 0), (0, lane - score_grp.shape[3])))
    sent = jnp.concatenate([jnp.swapaxes(part, 0, 1).astype(jnp.bfloat16), score_grp], axis=3)
    arrived_part = exchange(sent, "exp", 1)
    sender_block = (jnp.arange(spread_exp, dtype=jnp.int32) * spread_hid + own_hid)[:, None]
    sender_expert = (sender_block * unit_count + jnp.arange(unit_count, dtype=jnp.int32)[None, :]) // 2
    own_combine = near[:, 2 * model_width :]
    sender_pick = (expert_ids[:, None] == sender_expert.reshape(1, -1)).astype(jnp.bfloat16)
    sender_column = jnp.dot(own_combine, sender_pick, preferred_element_type=jnp.float32).T
    sender_rows = slot_rows(sender_column, group_rows).reshape(-1)
    place = (sender_rows[:, None] == jnp.arange(group_rows, dtype=jnp.int32)[None, :]).astype(jnp.bfloat16)
    group_sum = jnp.einsum(
        "sj,sd->jd", place, arrived_part[..., :model_width].reshape(-1, model_width),
        preferred_element_type=jnp.float32,
    )
    got_scores = join3(arrived_part[..., model_width:], group_rows // CAP)
    got_scores = got_scores.reshape(spread_exp, unit_count, spread_hid, tok_local)
    score_cols = spread_exp * unit_count
    hid_scores = jnp.transpose(got_scores, (2, 3, 0, 1)).reshape(spread_hid, tok_local, score_cols)
    hid_scores = split3(hid_scores)
    score_width = -(-hid_scores.shape[2] // lane) * lane
    hid_scores = jnp.pad(hid_scores, ((0, 0), (0, 0), (0, score_width - hid_scores.shape[2])))
    hid_sent = jnp.concatenate(
        [group_sum.reshape(spread_hid, tok_local, model_width).astype(jnp.bfloat16), hid_scores], axis=2
    )
    spread_rows = exchange(hid_sent, "hid", 2)
    input_sum = jnp.sum(spread_rows[..., :model_width].astype(jnp.float32), axis=0)
    own_scores = join3(spread_rows[..., model_width:], score_cols)
    own_scores = own_scores.reshape(spread_hid, tok_local, spread_exp, unit_count)
    unit_scores = jnp.transpose(own_scores, (1, 2, 0, 3)).reshape(tok_local, -1)
    expert_scores = jnp.sum(unit_scores.reshape(tok_local, expert_count, 2), axis=2)
    probs_all = softmax_rows(router_logits)
    mean_score = jnp.sum(probs_all * expert_scores, axis=1, keepdims=True)
    logit_grad = (probs_all * (expert_scores - mean_score)).astype(jnp.bfloat16)
    devices = spread_exp * spread_hid
    logit_all = lax.all_to_all(
        jnp.broadcast_to(logit_grad[None], (devices,) + logit_grad.shape), ("exp", "hid"), 0, 0, tiled=True
    ).reshape(-1, expert_count)
    grad_rows = model_width // devices
    token_cols = lax.dynamic_slice_in_dim(gathered, own_block * grad_rows, grad_rows, 1)
    router_grad = jnp.einsum("tc,te->ce", token_cols, logit_all, preferred_element_type=jnp.float32)
    router_part = jnp.einsum("te,de->td", logit_grad, router_w, preferred_element_type=jnp.float32)
    x_grad = (input_sum + router_part).astype(jnp.bfloat16)
    return (x_grad, router_grad)


def solution(mesh):
    placed = (
        P(("exp", "hid"), None),
        P(("exp", "hid"), None),
        P(("exp", "hid"), None),
        P(("exp", "hid"), None),
        P(),
        P(("exp", "hid"), None, None),
        P(("exp", "hid"), None, None),
        P(("exp", "hid"), None, None),
    )
    return jax.shard_map(
        on_device,
        mesh=mesh,
        in_specs=placed,
        out_specs=(P(("exp", "hid"), None), P(("exp", "hid"), None)),
        check_vma=False,
    )
```

```python
import functools
import jax
import jax.numpy as jnp
from jax import lax
from jax.sharding import PartitionSpec as P
from jax.experimental import pallas as pl
from jax.experimental.pallas import tpu as pltpu


def hid_gather_kernel(n, x_ref, out_ref, local_sem, send_sem, recv_sem):
    me = lax.axis_index("hid")
    rows = x_ref.shape[0]
    slot = out_ref.at[pl.ds(pl.multiple_of(me * rows, rows), rows)]
    row = lax.axis_index("exp")
    mesh_ids = pl.DeviceIdType.MESH
    barrier = pltpu.get_barrier_semaphore()
    for k in range(1, n):
        peer = lax.rem(me + k, n)
        pl.semaphore_signal(barrier, inc=1, device_id=(row, peer), device_id_type=mesh_ids)
    pl.semaphore_wait(barrier, n - 1)
    local = pltpu.make_async_copy(x_ref, slot, local_sem)
    local.start()
    copies = []
    for k in range(1, n):
        peer = lax.rem(me + k, n)
        copy = pltpu.make_async_remote_copy(
            src_ref=x_ref,
            dst_ref=slot,
            send_sem=send_sem.at[k],
            recv_sem=recv_sem.at[k],
            device_id=(row, peer),
            device_id_type=mesh_ids,
        )
        copy.start()
        copies.append(copy)
    local.wait()
    for copy in copies:
        copy.wait()


def exchange_kernel(axis, n, x_ref, out_ref, local_sem, send_sem, recv_sem):
    me = lax.axis_index(axis)
    own_exp = lax.axis_index("exp")
    own_hid = lax.axis_index("hid")
    mesh_ids = pl.DeviceIdType.MESH
    where = lambda peer: (peer, own_hid) if axis == "exp" else (own_exp, peer)
    barrier = pltpu.get_barrier_semaphore()
    for k in range(1, n):
        peer = lax.rem(me + k, n)
        pl.semaphore_signal(barrier, inc=1, device_id=where(peer), device_id_type=mesh_ids)
    pl.semaphore_wait(barrier, n - 1)
    local = pltpu.make_async_copy(x_ref.at[me], out_ref.at[me], local_sem)
    local.start()
    copies = []
    for k in range(1, n):
        peer = lax.rem(me + k, n)
        copy = pltpu.make_async_remote_copy(
            src_ref=x_ref.at[peer],
            dst_ref=out_ref.at[me],
            send_sem=send_sem.at[k],
            recv_sem=recv_sem.at[k],
            device_id=where(peer),
            device_id_type=mesh_ids,
        )
        copy.start()
        copies.append(copy)
    local.wait()
    for copy in copies:
        copy.wait()


def exchange(chunks, axis, kernel_id):
    n = chunks.shape[0]
    return pl.pallas_call(
        functools.partial(exchange_kernel, axis, n),
        out_shape=jax.ShapeDtypeStruct(chunks.shape, chunks.dtype),
        in_specs=[pl.BlockSpec(memory_space=pltpu.VMEM)],
        out_specs=pl.BlockSpec(memory_space=pltpu.VMEM),
        scratch_shapes=[
            pltpu.SemaphoreType.DMA,
            pltpu.SemaphoreType.DMA((n,)),
            pltpu.SemaphoreType.DMA((n,)),
        ],
        compiler_params=pltpu.CompilerParams(collective_id=kernel_id, has_side_effects=True),
    )(chunks)


def hid_gather(block):
    n = lax.axis_size("hid")
    return pl.pallas_call(
        functools.partial(hid_gather_kernel, n),
        out_shape=jax.ShapeDtypeStruct((n * block.shape[0],) + block.shape[1:], block.dtype),
        in_specs=[pl.BlockSpec(memory_space=pltpu.VMEM)],
        out_specs=pl.BlockSpec(memory_space=pltpu.VMEM),
        scratch_shapes=[
            pltpu.SemaphoreType.DMA,
            pltpu.SemaphoreType.DMA((n,)),
            pltpu.SemaphoreType.DMA((n,)),
        ],
        compiler_params=pltpu.CompilerParams(collective_id=0, has_side_effects=True),
    )(block)


def softmax_rows(values):
    top_val = jnp.max(values, axis=-1, keepdims=True)
    raised = jnp.exp(values - top_val)
    return raised / jnp.sum(raised, axis=-1, keepdims=True)


def combine_table(logits, chosen, expert_count):
    expert_ids = jnp.arange(expert_count, dtype=jnp.int32)
    matched = chosen[:, :, None] == expert_ids[None, None, :]
    picked = jnp.sum(jnp.where(matched, logits[:, None, :], 0.0), axis=2)
    weights = softmax_rows(picked)
    return jnp.sum(weights[:, :, None] * matched.astype(jnp.float32), axis=1).astype(jnp.bfloat16)


CAP = 4


def slot_rows(column, group_rows):
    shaped = column.reshape(column.shape[:-1] + (-1, group_rows))
    place = jnp.arange(group_rows, dtype=jnp.int32)
    key = jnp.where(shaped != 0, 2 * group_rows - place, -place)
    return lax.top_k(key, CAP)[1]


def split3(value):
    hi = value.astype(jnp.bfloat16)
    rest = value - hi.astype(jnp.float32)
    mid = rest.astype(jnp.bfloat16)
    lo = (rest - mid.astype(jnp.float32)).astype(jnp.bfloat16)
    return jnp.concatenate([hi, mid, lo], axis=-1)


def join3(pieces, width):
    part = lambda i: pieces[..., i * width : (i + 1) * width].astype(jnp.float32)
    return (part(0) + part(1)) + part(2)


def pick_rows(choice, value):
    hi = value.astype(jnp.bfloat16)
    rest = value - hi.astype(jnp.float32)
    mid = rest.astype(jnp.bfloat16)
    lo = (rest - mid.astype(jnp.float32)).astype(jnp.bfloat16)
    dot = lambda piece: jnp.dot(choice, piece, preferred_element_type=jnp.float32)
    return (dot(hi) + dot(mid)) + dot(lo)


def dense_kernel(rows_ref, x_ref, g_ref, wg_ref, wu_ref, wd_ref, score_ref, gate_ref, up_ref, back_ref):
    step = pl.program_id(0)
    x = x_ref[...]
    gate_pre = jnp.dot(x, wg_ref[...], preferred_element_type=jnp.float32)
    up_pre = jnp.dot(x, wu_ref[...], preferred_element_type=jnp.float32)
    back_grad = lax.dot_general(
        g_ref[...], wd_ref[...], (((1,), (1,)), ((), ())), preferred_element_type=jnp.float32
    )
    sig_gate = 1.0 / (1.0 + jnp.exp(-gate_pre))
    score_ref[...] = jnp.sum(gate_pre * sig_gate * up_pre * back_grad, axis=1, keepdims=True)
    tile = x.shape[0]
    place = step * tile + lax.broadcasted_iota(jnp.int32, (1, tile), 1)
    choice = (rows_ref[...] == place).astype(jnp.bfloat16)

    @pl.when(step == 0)
    def _():
        gate_ref[...] = jnp.zeros_like(gate_ref)
        up_ref[...] = jnp.zeros_like(up_ref)
        back_ref[...] = jnp.zeros_like(back_ref)

    hidden = gate_pre.shape[1]
    picked = pick_rows(choice, jnp.concatenate([gate_pre, up_pre, back_grad], axis=1))
    gate_ref[...] += picked[:, :hidden]
    up_ref[...] += picked[:, hidden : 2 * hidden]
    back_ref[...] += picked[:, 2 * hidden :]


def dense_unit(gathered, rows, gate_w, up_w, down_w, tile=256):
    tokens_n = gathered.shape[0]
    width, hidden = gate_w.shape
    slots = rows.shape[0]
    tiles = lambda i: (i, 0)
    fixed = lambda i: (0, 0)
    f32 = jnp.float32
    return pl.pallas_call(
        dense_kernel,
        grid=(tokens_n // tile,),
        out_shape=[
            jax.ShapeDtypeStruct((tokens_n, 1), f32),
            jax.ShapeDtypeStruct((slots, hidden), f32),
            jax.ShapeDtypeStruct((slots, hidden), f32),
            jax.ShapeDtypeStruct((slots, hidden), f32),
        ],
        in_specs=[
            pl.BlockSpec((slots, 1), fixed),
            pl.BlockSpec((tile, width), tiles),
            pl.BlockSpec((tile, width), lambda i: (i, 1)),
            pl.BlockSpec((width, hidden), fixed),
            pl.BlockSpec((width, hidden), fixed),
            pl.BlockSpec((hidden, width), fixed),
        ],
        out_specs=[
            pl.BlockSpec((tile, 1), tiles),
            pl.BlockSpec((slots, hidden), fixed),
            pl.BlockSpec((slots, hidden), fixed),
            pl.BlockSpec((slots, hidden), fixed),
        ],
    )(rows.reshape(slots, 1), gathered, gathered, gate_w, up_w, down_w)


def chosen_rows(column, group_rows):
    picked = slot_rows(column, group_rows)
    starts = (jnp.arange(picked.shape[1], dtype=jnp.int32) * group_rows)[None, :, None]
    return (picked + starts).reshape(picked.shape[0], -1)


def sparse_terms(gate_s, up_s, back_s, rows, column, w_gate, w_up):
    col_s = jnp.take_along_axis(column, rows, axis=1)
    sig_gate = jax.nn.sigmoid(gate_s)
    act_gate = gate_s * sig_gate
    weighted = col_s[:, :, None] * back_s
    grad_gate = (weighted * up_s * sig_gate * (1.0 + gate_s * (1.0 - sig_gate))).astype(jnp.bfloat16)
    grad_up = (weighted * act_gate).astype(jnp.bfloat16)
    part = jnp.einsum("usf,udf->usd", grad_gate, w_gate, preferred_element_type=jnp.float32)
    part = part + jnp.einsum("usf,udf->usd", grad_up, w_up, preferred_element_type=jnp.float32)
    return part.reshape(part.shape[0], -1, CAP, part.shape[-1])


def on_device(tokens, grad_out, router_logits, selected, router_w, w_gate, w_up, w_down):
    tok_local, model_width = tokens.shape
    unit_count = w_gate.shape[0]
    expert_count = router_logits.shape[1]
    spread_exp = lax.axis_size("exp")
    spread_hid = lax.axis_size("hid")
    group_rows = spread_hid * tok_local
    own_exp = lax.axis_index("exp")
    own_hid = lax.axis_index("hid")
    own_block = lax.axis_index(("exp", "hid"))
    unit_expert = (own_block * unit_count + jnp.arange(unit_count, dtype=jnp.int32)) // 2
    expert_ids = jnp.arange(expert_count, dtype=jnp.int32)
    unit_pick = (expert_ids[:, None] == unit_expert[None, :]).astype(jnp.bfloat16)
    combine = combine_table(router_logits, selected, expert_count)
    packed = jnp.concatenate([tokens, grad_out, combine], axis=1)
    near = hid_gather(packed)
    gathered = lax.all_gather(near, "exp", axis=0, tiled=True)
    combine_all = gathered[:, 2 * model_width :]
    column = jnp.dot(combine_all, unit_pick, preferred_element_type=jnp.float32).T
    rows = chosen_rows(column, group_rows)
    dense = [dense_unit(gathered, rows[i], w_gate[i], w_up[i], w_down[i]) for i in range(unit_count)]
    score_part = jnp.concatenate([d[0] for d in dense], axis=1)
    gate_s, up_s, back_s = (jnp.stack([d[j] for d in dense]) for j in (1, 2, 3))
    part = sparse_terms(gate_s, up_s, back_s, rows, column, w_gate, w_up)
    lane = 128
    score_grp = jnp.swapaxes(score_part.T.reshape(unit_count, spread_exp, CAP, group_rows // CAP), 0, 1)
    score_grp = split3(score_grp)
    score_grp = jnp.pad(score_grp, ((0, 0), (0, 0), (0, 0), (0, lane - score_grp.shape[3])))
    sent = jnp.concatenate([jnp.swapaxes(part, 0, 1).astype(jnp.bfloat16), score_grp], axis=3)
    arrived_part = exchange(sent, "exp", 1)
    sender_block = (jnp.arange(spread_exp, dtype=jnp.int32) * spread_hid + own_hid)[:, None]
    sender_expert = (sender_block * unit_count + jnp.arange(unit_count, dtype=jnp.int32)[None, :]) // 2
    own_combine = near[:, 2 * model_width :]
    sender_pick = (expert_ids[:, None] == sender_expert.reshape(1, -1)).astype(jnp.bfloat16)
    sender_column = jnp.dot(own_combine, sender_pick, preferred_element_type=jnp.float32).T
    sender_rows = slot_rows(sender_column, group_rows).reshape(-1)
    place = (sender_rows[:, None] == jnp.arange(group_rows, dtype=jnp.int32)[None, :]).astype(jnp.bfloat16)
    group_sum = jnp.einsum(
        "sj,sd->jd", place, arrived_part[..., :model_width].reshape(-1, model_width),
        preferred_element_type=jnp.float32,
    )
    got_scores = join3(arrived_part[..., model_width:], group_rows // CAP)
    got_scores = got_scores.reshape(spread_exp, unit_count, spread_hid, tok_local)
    score_cols = spread_exp * unit_count
    hid_scores = jnp.transpose(got_scores, (2, 3, 0, 1)).reshape(spread_hid, tok_local, score_cols)
    hid_scores = split3(hid_scores)
    score_width = -(-hid_scores.shape[2] // lane) * lane
    hid_scores = jnp.pad(hid_scores, ((0, 0), (0, 0), (0, score_width - hid_scores.shape[2])))
    hid_sent = jnp.concatenate(
        [group_sum.reshape(spread_hid, tok_local, model_width).astype(jnp.bfloat16), hid_scores], axis=2
    )
    spread_rows = exchange(hid_sent, "hid", 2)
    input_sum = jnp.sum(spread_rows[..., :model_width].astype(jnp.float32), axis=0)
    own_scores = join3(spread_rows[..., model_width:], score_cols)
    own_scores = own_scores.reshape(spread_hid, tok_local, spread_exp, unit_count)
    unit_scores = jnp.transpose(own_scores, (1, 2, 0, 3)).reshape(tok_local, -1)
    expert_scores = jnp.sum(unit_scores.reshape(tok_local, expert_count, 2), axis=2)
    probs_all = softmax_rows(router_logits)
    mean_score = jnp.sum(probs_all * expert_scores, axis=1, keepdims=True)
    logit_grad = (probs_all * (expert_scores - mean_score)).astype(jnp.bfloat16)
    devices = spread_exp * spread_hid
    logit_all = lax.all_to_all(
        jnp.broadcast_to(logit_grad[None], (devices,) + logit_grad.shape), ("exp", "hid"), 0, 0, tiled=True
    ).reshape(-1, expert_count)
    grad_rows = model_width // devices
    token_cols = lax.dynamic_slice_in_dim(gathered, own_block * grad_rows, grad_rows, 1)
    router_grad = jnp.einsum("tc,te->ce", token_cols, logit_all, preferred_element_type=jnp.float32)
    router_part = jnp.einsum("te,de->td", logit_grad, router_w, preferred_element_type=jnp.float32)
    x_grad = (input_sum + router_part).astype(jnp.bfloat16)
    return (x_grad, router_grad)


def solution(mesh):
    placed = (
        P(("exp", "hid"), None),
        P(("exp", "hid"), None),
        P(("exp", "hid"), None),
        P(("exp", "hid"), None),
        P(),
        P(("exp", "hid"), None, None),
        P(("exp", "hid"), None, None),
        P(("exp", "hid"), None, None),
    )
    return jax.shard_map(
        on_device,
        mesh=mesh,
        in_specs=placed,
        out_specs=(P(("exp", "hid"), None), P(("exp", "hid"), None)),
        check_vma=False,
    )
```
